256 devices in a mesh: gx: 8 (over z), gy: 32 (over x, y, core).
Axes of the slice: x: 4, y: 4, z: 8, core: 2. Of those that a mesh axis runs over, the one named last changes fastest.
Arguments:
- initial_basis: float32 [8, 128, 512, 128], P(None, 'gx', 'gy'), may hold values from 0.1 to 0.5
- labels: int32 [128, 512, 128], P('gx', 'gy'), may hold values from 0 to 15
- class_perm: float32 [16], replicated, may hold values from 0.01 to 100
- support: int32 [128, 512, 128], P('gx', 'gy'), may hold values from 0 to 255
Outputs:
- basis: float32 [8, 128, 512, 128], P(None, 'gx', 'gy')
- coarse: float32 [27, 8, 32, 8], P(None, 'gx', 'gy')
The draws below stay inside these ranges and needn't reach their ends.
Inputs may be any that keep to these rules, and one draw needn't show every extreme that they name: `support`: bit s of a cell's entry says whether the basis function of its block's corner slot s may be nonzero in that cell.
All inputs are finite; a program needn't handle non-finite values.
Results may differ from the reference program's by a relative error of at most 0.0003.
Values sent between devices are 32-bit elements; how exact they have to be, the bound alone decides.
A program may use at most 64 MiB of HBM per device.

```python
import math
import jax
import jax.numpy as jnp
import numpy as np
from jax import lax

CB = 16
ITERS = 3
NCLASS = 16
LZ = 128
NX = 128
NY = 512


def set_ends(entries, rng, smallest, largest):
    dims = entries.shape
    place = [jax.random.randint(jax.random.fold_in(rng, axis), (), 0, dims[axis]) for axis in range(len(dims))]
    entries = entries.at[tuple(place)].set(smallest)
    longest = dims.index(max(dims))
    place[longest] = (place[longest] + 1) % dims[longest]
    return entries.at[tuple(place)].set(largest)


def shard_levels(own_key, shape, split, low, largest):
    def one(position, shards_of):
        steps = jax.random.uniform(jax.random.fold_in(jax.random.fold_in(own_key, 6), position), (shards_of,), jnp.float32, low / len(split), largest / len(split))
        return jnp.repeat(jnp.exp(steps), shape[position] // shards_of).reshape((-1,) + (1,) * (len(shape) - position - 1))

    loudness = one(*split[0])
    for cut in split[1:]:
        loudness = loudness * one(*cut)
    return loudness


def rank_table(count, lean):
    weights = [(1 << 20) // math.isqrt(standing ** lean) + 1 for standing in range(1, count + 1)]
    spread = 1 + sum(weights) // (1 << 30)
    return np.cumsum(np.array([max(1, weight // spread) for weight in weights]))


def skewed_ids(own_key, extent, amount, slope):
    listing = rank_table(amount, slope)
    pick = jax.random.randint(jax.random.fold_in(own_key, 1), extent, 0, int(listing[amount - 1]))
    standing = jnp.searchsorted(jnp.asarray(listing, jnp.int32), pick, side="right")
    return jax.random.permutation(jax.random.fold_in(own_key, 2), amount)[standing].astype(jnp.int32)


def setup_inputs(seed: int = 0) -> dict:
    key_of = jax.random.split(jax.random.key(seed), 5)
    return {
        "initial_basis": jnp.clip(0.1 + 0.4 * jax.random.uniform(key_of[0], (8, NX, NY, LZ), jnp.float32) ** shard_levels(key_of[0], (8, NX, NY, LZ), ((1, 8), (2, 32)), -0.2, 0.2), 0.1, 0.5),
        "labels": set_ends(skewed_ids(key_of[1], (NX, NY, LZ), NCLASS, 2), jax.random.fold_in(key_of[1], 3), 0, NCLASS - 1).astype(jnp.int32),
        "class_perm": jnp.clip(jnp.exp(jax.random.uniform(key_of[2], (NCLASS,), jnp.float32, math.log(0.01), math.log(100.0))), 0.01, 100.0),
        "support": set_ends(jax.random.randint(key_of[3], (NX, NY, LZ), 0, 256), jax.random.fold_in(key_of[3], 1), 0, 255).astype(jnp.int32),
    }


omega_jacobi = 2.0 / 3.0
renorm_floor = 0.5


def corner_of(slot_index):
    return ((slot_index >> 2) & 1, (slot_index >> 1) & 1, slot_index & 1)


def slot_remap(values, bit_axis, upward, crossing):
    lower_half = jnp.take(values, 0, axis=bit_axis)
    upper_half = jnp.take(values, 1, axis=bit_axis)
    nothing = jnp.zeros_like(lower_half)
    if upward:
        shifted = jnp.stack([nothing, lower_half], axis=bit_axis)
    else:
        shifted = jnp.stack([upper_half, nothing], axis=bit_axis)
    return jnp.where(crossing, shifted, values)


def conductance(centre, neighbour):
    total_perm = centre + neighbour
    divisor = jnp.where(total_perm > 0.0, total_perm, 1.0)
    return 2.0 * centre * neighbour / divisor


def stencil_terms(basis_pad, perm_pad, x_start, y_start):
    centre = perm_pad[1:-1, 1:-1]
    count_x, count_y, count_z = centre.shape
    basis_core = basis_pad[:, :, :, 1:-1, 1:-1]
    place_x = (jnp.arange(count_x) + x_start) % CB
    place_y = (jnp.arange(count_y) + y_start) % CB
    place_z = jnp.arange(count_z) % CB
    perm_vert = jnp.pad(centre, ((0, 0), (0, 0), (1, 1)))
    basis_vert = jnp.pad(basis_core, ((0, 0), (0, 0), (0, 0), (0, 0), (0, 0), (1, 1)))
    sides = (
        (perm_pad[2:, 1:-1], basis_pad[:, :, :, 2:, 1:-1], 0, True, (place_x == CB - 1)[:, None, None]),
        (perm_pad[:-2, 1:-1], basis_pad[:, :, :, :-2, 1:-1], 0, False, (place_x == 0)[:, None, None]),
        (perm_pad[1:-1, 2:], basis_pad[:, :, :, 1:-1, 2:], 1, True, (place_y == CB - 1)[None, :, None]),
        (perm_pad[1:-1, :-2], basis_pad[:, :, :, 1:-1, :-2], 1, False, (place_y == 0)[None, :, None]),
        (perm_vert[:, :, 2:], basis_vert[:, :, :, :, :, 2:], 2, True, (place_z == CB - 1)[None, None, :]),
        (perm_vert[:, :, :-2], basis_vert[:, :, :, :, :, :-2], 2, False, (place_z == 0)[None, None, :]),
    )
    diagonal = jnp.zeros_like(centre)
    inflow = jnp.zeros_like(basis_core)
    for neighbour, values, bit_axis, upward, crossing in sides:
        linkage = conductance(centre, neighbour)
        diagonal = diagonal + linkage
        inflow = inflow + linkage * slot_remap(values, bit_axis, upward, crossing)
    return basis_core, diagonal, inflow


def jacobi_step(basis_core, diagonal, inflow, valid):
    divisor = jnp.where(diagonal > 0.0, diagonal, 1.0)
    return (basis_core - omega_jacobi * (diagonal * basis_core - inflow) / divisor) * valid


def renormalize(weights):
    totals = jnp.sum(weights, axis=(0, 1, 2))
    return weights / jnp.maximum(totals, renorm_floor)


def support_mask(support, first_x, first_y, limit_x, limit_y, limit_z):
    count_x, count_y, count_z = support.shape
    block_x = (jnp.arange(count_x) + first_x) // CB
    block_y = (jnp.arange(count_y) + first_y) // CB
    block_z = jnp.arange(count_z) // CB
    layers = []
    for slot_index in range(8):
        corner_x, corner_y, corner_z = corner_of(slot_index)
        present = jnp.right_shift(support, slot_index) & 1
        inside = (((block_x + corner_x) < limit_x)[:, None, None]
                  & ((block_y + corner_y) < limit_y)[None, :, None]
                  & ((block_z + corner_z) < limit_z)[None, None, :])
        layers.append(jnp.where(inside & (present > 0), 1.0, 0.0).astype(jnp.float32))
    return jnp.stack(layers).reshape(2, 2, 2, count_x, count_y, count_z)


def block_products(basis_core, image):
    _, _, _, count_x, count_y, count_z = basis_core.shape
    shape_blocks = (8, count_x // CB, CB, count_y // CB, CB, count_z // CB, CB)
    return jnp.einsum("aiujvkw,biujvkw->abijk", basis_core.reshape(shape_blocks),
                      image.reshape(shape_blocks), precision=lax.Precision.HIGHEST)


def assemble(products):
    _, _, count_x, count_y, count_z = products.shape
    assembled = jnp.zeros((27, count_x + 1, count_y + 1, count_z + 1), jnp.float32)
    for first_slot in range(8):
        for second_slot in range(8):
            one_x, one_y, one_z = corner_of(first_slot)
            two_x, two_y, two_z = corner_of(second_slot)
            offset_index = 9 * (two_x - one_x + 1) + 3 * (two_y - one_y + 1) + (two_z - one_z + 1)
            assembled = assembled.at[offset_index, one_x:one_x + count_x, one_y:one_y + count_y,
                                     one_z:one_z + count_z].add(products[first_slot, second_slot])
    return assembled


def reference(initial_basis, labels, class_perm, support):
    count_x, count_y, count_z = labels.shape
    permeability = class_perm[labels]
    valid = support_mask(support, 0, 0, count_x // CB, count_y // CB, count_z // CB)
    weights = initial_basis.reshape(2, 2, 2, count_x, count_y, count_z) * valid
    perm_pad = jnp.pad(permeability, ((1, 1), (1, 1), (0, 0)))
    lateral = ((0, 0), (0, 0), (0, 0), (1, 1), (1, 1), (0, 0))
    for sweep_step in range(ITERS):
        basis_core, diagonal, inflow = stencil_terms(jnp.pad(weights, lateral), perm_pad, 0, 0)
        weights = jacobi_step(basis_core, diagonal, inflow, valid)
    weights = renormalize(weights)
    basis_core, diagonal, inflow = stencil_terms(jnp.pad(weights, lateral), perm_pad, 0, 0)
    image = diagonal * basis_core - inflow
    coarse = assemble(block_products(basis_core, image))[:, :-1, :-1, :-1]
    return weights.reshape(8, count_x, count_y, count_z), coarse
```

```python
import numpy as np
import jax
import jax.numpy as jnp
from jax import lax
from jax.experimental import pallas as pl
from jax.experimental.pallas import tpu as pltpu
from jax.sharding import PartitionSpec as P

CB = 16
ITERS = 3
HX = ITERS + 1
HY = ITERS + 1

omega_jacobi = 2.0 / 3.0
renorm_floor = 0.5


def with_halo(block, sides, width):
    for axis, dim in sides:
        count = lax.axis_size(axis)
        forward = [(i, i + 1) for i in range(count - 1)]
        backward = [(target, source) for source, target in forward]
        low = lax.ppermute(
            lax.slice_in_dim(block, block.shape[dim] - width, None, axis=dim), axis, forward
        )
        high = lax.ppermute(lax.slice_in_dim(block, 0, width, axis=dim), axis, backward)
        block = jnp.concatenate([low, block, high], axis=dim)
    return block


def from_behind(shard, axis, by):
    peers = lax.axis_size(axis)
    pairs = [(i, i + by) for i in range(peers) if 0 <= i + by < peers]
    return lax.ppermute(shard, axis, pairs)


def corner_of(slot_index):
    return (slot_index >> 2 & 1, slot_index >> 1 & 1, slot_index & 1)


def conductance(centre, neighbour):
    total_perm = centre + neighbour
    divisor = jnp.where(total_perm > 0.0, total_perm, 1.0)
    return 2.0 * centre * neighbour / divisor


def class_lookup(labels, class_perm):
    classes = jnp.arange(class_perm.shape[0])
    hits = labels[None] == classes[:, None, None, None]
    return jnp.sum(jnp.where(hits, class_perm[:, None, None, None], 0.0), axis=0)


def existing_bits(count_x, count_y, count_z, first_x, first_y, limit_x, limit_y, limit_z):
    block_x = (jnp.arange(count_x) + first_x) // CB
    block_y = (jnp.arange(count_y) + first_y) // CB
    block_z = jnp.arange(count_z) // CB
    bits = jnp.zeros((count_x, count_y, count_z), jnp.int32)
    for slot_index in range(8):
        corner_x, corner_y, corner_z = corner_of(slot_index)
        inside = (
            (block_x + corner_x < limit_x)[:, None, None]
            & (block_y + corner_y < limit_y)[None, :, None]
            & (block_z + corner_z < limit_z)[None, None, :]
        )
        bits = bits | jnp.where(inside, 1 << slot_index, 0)
    return bits


def smooth_kernel(ext_ref, basis_ref, prod_ref, tt, aux, valid, wa, wb, img):
    _, XE, YE, L = ext_ref.shape
    NXL = basis_ref.shape[1]
    NYL = basis_ref.shape[2]
    row = lax.broadcasted_iota(jnp.int32, (YE, L), 0)
    lane = lax.broadcasted_iota(jnp.int32, (YE, L), 1)
    ry = (row + (CB - HY)) & (CB - 1)
    m_yhi = ry == CB - 1
    m_ylo = ry == 0
    rz = lane & (CB - 1)
    m_zhi = rz == CB - 1
    m_zlo = rz == 0
    m_rows = (row >= HY) & (row < HY + NYL)

    def xplace(x):
        return (x + (CB - HX)) & (CB - 1)

    def pre(x, carry):
        pc = ext_ref[8, x]
        pxp = jnp.where(x + 1 < XE, ext_ref[8, jnp.minimum(x + 1, XE - 1)], 0.0)
        pxm = jnp.where(x >= 1, ext_ref[8, jnp.maximum(x - 1, 0)], 0.0)
        pyp = pltpu.roll(pc, YE - 1, 0)
        pym = pltpu.roll(pc, 1, 0)
        pzp = pltpu.roll(pc, L - 1, 1)
        pzm = pltpu.roll(pc, 1, 1)
        t_xp = conductance(pc, pxp)
        t_xm = conductance(pc, pxm)
        t_yp = conductance(pc, pyp)
        t_ym = conductance(pc, pym)
        t_zp = jnp.where(lane == L - 1, 0.0, conductance(pc, pzp))
        t_zm = jnp.where(lane == 0, 0.0, conductance(pc, pzm))
        diag = t_xp + t_xm + t_yp + t_ym + t_zp + t_zm
        aux[0, x] = diag
        aux[1, x] = 1.0 / jnp.where(diag > 0.0, diag, 1.0)
        cx_hi = xplace(x) == CB - 1
        cx_lo = xplace(x) == 0
        tt[0, x] = t_xp
        tt[1, x] = jnp.where(cx_hi, 0.0, t_xp)
        tt[2, x] = t_xm
        tt[3, x] = jnp.where(cx_lo, 0.0, t_xm)
        tt[4, x] = t_yp
        tt[5, x] = jnp.where(m_yhi, 0.0, t_yp)
        tt[6, x] = t_ym
        tt[7, x] = jnp.where(m_ylo, 0.0, t_ym)
        tt[8, x] = t_zp
        tt[9, x] = jnp.where(m_zhi, 0.0, t_zp)
        tt[10, x] = t_zm
        tt[11, x] = jnp.where(m_zlo, 0.0, t_zm)
        sup = ext_ref[9, x].astype(jnp.int32)
        for s in range(8):
            v = ((sup >> s) & 1).astype(jnp.float32)
            valid[s, x] = v
            wa[s, x] = ext_ref[s, x] * v
        return carry

    lax.fori_loop(0, XE, pre, 0)

    def inflow_of(src, x, s, c):
        bx, by, bz = corner_of(s)
        cx_hi = xplace(x) == CB - 1
        cx_lo = xplace(x) == 0
        if bx:
            xp = src[jnp.where(cx_hi, s ^ 4, s), x + 1]
            t1 = tt[0, x]
            xm = src[s, x - 1]
            t2 = tt[3, x]
        else:
            xp = src[s, x + 1]
            t1 = tt[1, x]
            xm = src[jnp.where(cx_lo, s ^ 4, s), x - 1]
            t2 = tt[2, x]
        if by:
            yp = pltpu.roll(jnp.where(m_ylo, src[s ^ 2, x], c), YE - 1, 0)
            t3 = tt[4, x]
            ym = pltpu.roll(c, 1, 0)
            t4 = tt[7, x]
        else:
            yp = pltpu.roll(c, YE - 1, 0)
            t3 = tt[5, x]
            ym = pltpu.roll(jnp.where(m_yhi, src[s ^ 2, x], c), 1, 0)
            t4 = tt[6, x]
        if bz:
            zp = pltpu.roll(jnp.where(m_zlo, src[s ^ 1, x], c), L - 1, 1)
            t5 = tt[8, x]
            zm = pltpu.roll(c, 1, 1)
            t6 = tt[11, x]
        else:
            zp = pltpu.roll(c, L - 1, 1)
            t5 = tt[9, x]
            zm = pltpu.roll(jnp.where(m_zhi, src[s ^ 1, x], c), 1, 1)
            t6 = tt[10, x]
        return t1 * xp + t2 * xm + t3 * yp + t4 * ym + t5 * zp + t6 * zm

    def sweep(src, dst, lo, hi):
        def body(x, carry):
            diag = aux[0, x]
            inv = aux[1, x]
            for s in range(8):
                c = src[s, x]
                inflow = inflow_of(src, x, s, c)
                dst[s, x] = (c - omega_jacobi * (diag * c - inflow) * inv) * valid[s, x]
            return carry

        lax.fori_loop(lo, hi, body, 0)

    bufs = (wa, wb)
    for step in range(ITERS):
        sweep(bufs[step % 2], bufs[(step + 1) % 2], step + 1, XE - step - 1)
    last = bufs[ITERS % 2]
    basis_buf = bufs[(ITERS + 1) % 2]

    def normalize(x, carry):
        vals = [last[s, x] for s in range(8)]
        total = vals[0]
        for s in range(1, 8):
            total = total + vals[s]
        scale = jnp.maximum(total, renorm_floor)
        for s in range(8):
            basis_buf[s, x] = vals[s] / scale
        return carry

    lax.fori_loop(ITERS, XE - ITERS, normalize, 0)

    def image(x, carry):
        diag = aux[0, x]
        for s in range(8):
            c = basis_buf[s, x]
            inflow = inflow_of(basis_buf, x, s, c)
            img[s, x - HX] = jnp.where(m_rows, diag * c - inflow, 0.0)
            basis_ref[s, x - HX] = c[HY:HY + NYL, :]
        return carry

    lax.fori_loop(HX, HX + NXL, image, 0)

    for s1 in range(8):
        def pair_sums(x, acc):
            b = basis_buf[s1, x + HX]
            return tuple(acc[s2] + b * img[s2, x] for s2 in range(8))

        acc = lax.fori_loop(
            0, NXL, pair_sums, tuple(jnp.zeros((YE, L), jnp.float32) for _ in range(8))
        )
        for s2 in range(8):
            prod_ref[pl.ds(s1 * 8 + s2, 1), :] = jnp.sum(acc[s2], axis=0, keepdims=True)


def assembly_matrix():
    table = np.zeros((4 * 27 * 2, 64), np.float32)
    for first_slot in range(8):
        for second_slot in range(8):
            one_x, one_y, one_z = corner_of(first_slot)
            two_x, two_y, two_z = corner_of(second_slot)
            offset_index = 9 * (two_x - one_x + 1) + 3 * (two_y - one_y + 1) + (two_z - one_z + 1)
            row = ((one_x * 2 + one_y) * 27 + offset_index) * 2 + one_z
            table[row, first_slot * 8 + second_slot] = 1.0
    return table


def shards(initial_basis, labels, class_perm, support):
    size_x, size_y, size_z = labels.shape
    assert size_x == CB and size_y == CB and size_z % CB == 0
    blocks_z = size_z // CB
    permeability = class_lookup(labels, class_perm)
    keep = existing_bits(
        size_x,
        size_y,
        size_z,
        lax.axis_index("gx") * size_x,
        lax.axis_index("gy") * size_y,
        lax.axis_size("gx") * size_x // CB,
        lax.axis_size("gy") * size_y // CB,
        blocks_z,
    )
    support_f = (support & keep).astype(jnp.float32)
    packed = jnp.concatenate([initial_basis, permeability[None], support_f[None]], axis=0)
    ext = with_halo(packed, (("gx", 1), ("gy", 2)), HX)
    XE, YE = size_x + 2 * HX, size_y + 2 * HY
    f32 = jnp.float32
    basis, prods = pl.pallas_call(
        smooth_kernel,
        out_shape=(
            jax.ShapeDtypeStruct((8, size_x, size_y, size_z), f32),
            jax.ShapeDtypeStruct((64, size_z), f32),
        ),
        in_specs=[pl.BlockSpec(memory_space=pltpu.VMEM)],
        out_specs=(pl.BlockSpec(memory_space=pltpu.VMEM), pl.BlockSpec(memory_space=pltpu.VMEM)),
        scratch_shapes=[
            pltpu.VMEM((12, XE, YE, size_z), f32),
            pltpu.VMEM((2, XE, YE, size_z), f32),
            pltpu.VMEM((8, XE, YE, size_z), f32),
            pltpu.VMEM((8, XE, YE, size_z), f32),
            pltpu.VMEM((8, XE, YE, size_z), f32),
            pltpu.VMEM((8, size_x, YE, size_z), f32),
        ],
    )(ext)
    block_sums = prods.reshape(64, blocks_z, CB).sum(axis=-1)
    placed = jnp.dot(
        jnp.asarray(assembly_matrix()), block_sums, precision=lax.Precision.HIGHEST
    ).reshape(4, 27, 2, blocks_z)
    contrib = placed[:, :, 0] + jnp.pad(placed[:, :, 1, :-1], ((0, 0), (0, 0), (1, 0)))
    nx = lax.axis_size("gx")
    ny = lax.axis_size("gy")
    from_x = from_behind(contrib[2], "gx", 1)
    from_y = from_behind(contrib[1], "gy", 1)
    diagonal_pairs = [
        (i * ny + j, (i + 1) * ny + j + 1) for i in range(nx - 1) for j in range(ny - 1)
    ]
    from_xy = lax.ppermute(contrib[3], ("gx", "gy"), diagonal_pairs)
    owned = contrib[0] + from_x + from_y + from_xy
    return (basis, owned.reshape(27, 1, 1, blocks_z))


def solution(mesh):
    return jax.shard_map(
        shards,
        mesh=mesh,
        in_specs=(P(None, "gx", "gy", None), P("gx", "gy", None), P(), P("gx", "gy", None)),
        out_specs=(P(None, "gx", "gy", None), P(None, "gx", "gy", None)),
        check_vma=False,
    )
```

```python
import functools
import numpy as np
import jax
import jax.numpy as jnp
from jax import lax
from jax.experimental import pallas as pl
from jax.experimental.pallas import tpu as pltpu
from jax.sharding import PartitionSpec as P

CB = 16
ITERS = 3
HX = ITERS + 1
HY = ITERS + 1

omega_jacobi = 2.0 / 3.0
renorm_floor = 0.5


def with_halo(block, sides, width):
    for axis, dim in sides:
        count = lax.axis_size(axis)
        forward = [(i, i + 1) for i in range(count - 1)]
        backward = [(target, source) for source, target in forward]
        low = lax.ppermute(
            lax.slice_in_dim(block, block.shape[dim] - width, None, axis=dim), axis, forward
        )
        high = lax.ppermute(lax.slice_in_dim(block, 0, width, axis=dim), axis, backward)
        block = jnp.concatenate([low, block, high], axis=dim)
    return block


def from_behind(shard, axis, by):
    peers = lax.axis_size(axis)
    pairs = [(i, i + by) for i in range(peers) if 0 <= i + by < peers]
    return lax.ppermute(shard, axis, pairs)


def corner_of(slot_index):
    return (slot_index >> 2 & 1, slot_index >> 1 & 1, slot_index & 1)


def conductance(centre, neighbour):
    total_perm = centre + neighbour
    divisor = jnp.where(total_perm > 0.0, total_perm, 1.0)
    return 2.0 * centre * neighbour / divisor


def class_lookup(labels, class_perm):
    classes = jnp.arange(class_perm.shape[0])
    hits = labels[None] == classes[:, None, None, None]
    return jnp.sum(jnp.where(hits, class_perm[:, None, None, None], 0.0), axis=0)


def existing_bits(count_x, count_y, count_z, first_x, first_y, limit_x, limit_y, limit_z):
    block_x = (jnp.arange(count_x) + first_x) // CB
    block_y = (jnp.arange(count_y) + first_y) // CB
    block_z = jnp.arange(count_z) // CB
    bits = jnp.zeros((count_x, count_y, count_z), jnp.int32)
    for slot_index in range(8):
        corner_x, corner_y, corner_z = corner_of(slot_index)
        inside = (
            (block_x + corner_x < limit_x)[:, None, None]
            & (block_y + corner_y < limit_y)[None, :, None]
            & (block_z + corner_z < limit_z)[None, None, :]
        )
        bits = bits | jnp.where(inside, 1 << slot_index, 0)
    return bits


def smooth_kernel(ext_ref, basis_ref, prod_ref, tt, aux, valid, wa, wb, img):
    _, XE, YE, L = ext_ref.shape
    NXL = basis_ref.shape[1]
    NYL = basis_ref.shape[2]
    row = lax.broadcasted_iota(jnp.int32, (YE, L), 0)
    lane = lax.broadcasted_iota(jnp.int32, (YE, L), 1)
    ry = (row + (CB - HY)) & (CB - 1)
    m_yhi = ry == CB - 1
    m_ylo = ry == 0
    rz = lane & (CB - 1)
    m_zhi = rz == CB - 1
    m_zlo = rz == 0
    m_rows = (row >= HY) & (row < HY + NYL)

    def xplace(x):
        return (x + (CB - HX)) & (CB - 1)

    def pre(x, carry):
        pc = ext_ref[8, x]
        pxp = jnp.where(x + 1 < XE, ext_ref[8, jnp.minimum(x + 1, XE - 1)], 0.0)
        pxm = jnp.where(x >= 1, ext_ref[8, jnp.maximum(x - 1, 0)], 0.0)
        pyp = pltpu.roll(pc, YE - 1, 0)
        pym = pltpu.roll(pc, 1, 0)
        pzp = pltpu.roll(pc, L - 1, 1)
        pzm = pltpu.roll(pc, 1, 1)
        t_xp = conductance(pc, pxp)
        t_xm = conductance(pc, pxm)
        t_yp = conductance(pc, pyp)
        t_ym = conductance(pc, pym)
        t_zp = jnp.where(lane == L - 1, 0.0, conductance(pc, pzp))
        t_zm = jnp.where(lane == 0, 0.0, conductance(pc, pzm))
        diag = t_xp + t_xm + t_yp + t_ym + t_zp + t_zm
        aux[0, x] = diag
        aux[1, x] = 1.0 / jnp.where(diag > 0.0, diag, 1.0)
        cx_hi = xplace(x) == CB - 1
        cx_lo = xplace(x) == 0
        tt[0, x] = t_xp
        tt[1, x] = jnp.where(cx_hi, 0.0, t_xp)
        tt[2, x] = t_xm
        tt[3, x] = jnp.where(cx_lo, 0.0, t_xm)
        tt[4, x] = t_yp
        tt[5, x] = jnp.where(m_yhi, 0.0, t_yp)
        tt[6, x] = t_ym
        tt[7, x] = jnp.where(m_ylo, 0.0, t_ym)
        tt[8, x] = t_zp
        tt[9, x] = jnp.where(m_zhi, 0.0, t_zp)
        tt[10, x] = t_zm
        tt[11, x] = jnp.where(m_zlo, 0.0, t_zm)
        sup = ext_ref[9, x].astype(jnp.int32)
        for s in range(8):
            v = ((sup >> s) & 1).astype(jnp.float32)
            valid[s, x] = v
            wa[s, x] = ext_ref[s, x] * v
        return carry

    lax.fori_loop(0, XE, pre, 0)

    def inflow_of(src, x, s, c):
        bx, by, bz = corner_of(s)
        cx_hi = xplace(x) == CB - 1
        cx_lo = xplace(x) == 0
        if bx:
            xp = src[jnp.where(cx_hi, s ^ 4, s), x + 1]
            t1 = tt[0, x]
            xm = src[s, x - 1]
            t2 = tt[3, x]
        else:
            xp = src[s, x + 1]
            t1 = tt[1, x]
            xm = src[jnp.where(cx_lo, s ^ 4, s), x - 1]
            t2 = tt[2, x]
        if by:
            yp = pltpu.roll(jnp.where(m_ylo, src[s ^ 2, x], c), YE - 1, 0)
            t3 = tt[4, x]
            ym = pltpu.roll(c, 1, 0)
            t4 = tt[7, x]
        else:
            yp = pltpu.roll(c, YE - 1, 0)
            t3 = tt[5, x]
            ym = pltpu.roll(jnp.where(m_yhi, src[s ^ 2, x], c), 1, 0)
            t4 = tt[6, x]
        if bz:
            zp = pltpu.roll(jnp.where(m_zlo, src[s ^ 1, x], c), L - 1, 1)
            t5 = tt[8, x]
            zm = pltpu.roll(c, 1, 1)
            t6 = tt[11, x]
        else:
            zp = pltpu.roll(c, L - 1, 1)
            t5 = tt[9, x]
            zm = pltpu.roll(jnp.where(m_zhi, src[s ^ 1, x], c), 1, 1)
            t6 = tt[10, x]
        return t1 * xp + t2 * xm + t3 * yp + t4 * ym + t5 * zp + t6 * zm

    def sweep(src, dst, lo, hi):
        def body(x, carry):
            diag = aux[0, x]
            inv = aux[1, x]
            for s in range(8):
                c = src[s, x]
                inflow = inflow_of(src, x, s, c)
                dst[s, x] = (c - omega_jacobi * (diag * c - inflow) * inv) * valid[s, x]
            return carry

        lax.fori_loop(lo, hi, body, 0)

    bufs = (wa, wb)
    for step in range(ITERS):
        sweep(bufs[step % 2], bufs[(step + 1) % 2], step + 1, XE - step - 1)
    last = bufs[ITERS % 2]
    basis_buf = bufs[(ITERS + 1) % 2]

    def normalize(x, carry):
        vals = [last[s, x] for s in range(8)]
        total = vals[0]
        for s in range(1, 8):
            total = total + vals[s]
        scale = jnp.maximum(total, renorm_floor)
        for s in range(8):
            basis_buf[s, x] = vals[s] / scale
        return carry

    lax.fori_loop(ITERS, XE - ITERS, normalize, 0)

    def image(x, carry):
        diag = aux[0, x]
        for s in range(8):
            c = basis_buf[s, x]
            inflow = inflow_of(basis_buf, x, s, c)
            img[s, x - HX] = jnp.where(m_rows, diag * c - inflow, 0.0)
            basis_ref[s, x - HX] = c[HY:HY + NYL, :]
        return carry

    lax.fori_loop(HX, HX + NXL, image, 0)

    for s1 in range(8):
        def pair_sums(x, acc):
            b = basis_buf[s1, x + HX]
            return tuple(acc[s2] + b * img[s2, x] for s2 in range(8))

        acc = lax.fori_loop(
            0, NXL, pair_sums, tuple(jnp.zeros((YE, L), jnp.float32) for _ in range(8))
        )
        for s2 in range(8):
            prod_ref[pl.ds(s1 * 8 + s2, 1), :] = jnp.sum(acc[s2], axis=0, keepdims=True)


def assembly_matrix():
    table = np.zeros((4 * 27 * 2, 64), np.float32)
    for first_slot in range(8):
        for second_slot in range(8):
            one_x, one_y, one_z = corner_of(first_slot)
            two_x, two_y, two_z = corner_of(second_slot)
            offset_index = 9 * (two_x - one_x + 1) + 3 * (two_y - one_y + 1) + (two_z - one_z + 1)
            row = ((one_x * 2 + one_y) * 27 + offset_index) * 2 + one_z
            table[row, first_slot * 8 + second_slot] = 1.0
    return table


def shards(initial_basis, labels, class_perm, support):
    size_x, size_y, size_z = labels.shape
    assert size_x == CB and size_y == CB and size_z % CB == 0
    blocks_z = size_z // CB
    permeability = class_lookup(labels, class_perm)
    keep = existing_bits(
        size_x,
        size_y,
        size_z,
        lax.axis_index("gx") * size_x,
        lax.axis_index("gy") * size_y,
        lax.axis_size("gx") * size_x // CB,
        lax.axis_size("gy") * size_y // CB,
        blocks_z,
    )
    support_f = (support & keep).astype(jnp.float32)
    packed = jnp.concatenate([initial_basis, permeability[None], support_f[None]], axis=0)
    ext = with_halo(packed, (("gx", 1), ("gy", 2)), HX)
    XE, YE = size_x + 2 * HX, size_y + 2 * HY
    f32 = jnp.float32
    basis, prods = pl.pallas_call(
        smooth_kernel,
        out_shape=(
            jax.ShapeDtypeStruct((8, size_x, size_y, size_z), f32),
            jax.ShapeDtypeStruct((64, size_z), f32),
        ),
        in_specs=[pl.BlockSpec(memory_space=pltpu.VMEM)],
        out_specs=(pl.BlockSpec(memory_space=pltpu.VMEM), pl.BlockSpec(memory_space=pltpu.VMEM)),
        scratch_shapes=[
            pltpu.VMEM((12, XE, YE, size_z), f32),
            pltpu.VMEM((2, XE, YE, size_z), f32),
            pltpu.VMEM((8, XE, YE, size_z), f32),
            pltpu.VMEM((8, XE, YE, size_z), f32),
            pltpu.VMEM((8, XE, YE, size_z), f32),
            pltpu.VMEM((8, size_x, YE, size_z), f32),
        ],
    )(ext)
    block_sums = prods.reshape(64, blocks_z, CB).sum(axis=-1)
    placed = jnp.dot(
        jnp.asarray(assembly_matrix()), block_sums, precision=lax.Precision.HIGHEST
    ).reshape(4, 27, 2, blocks_z)
    contrib = placed[:, :, 0] + jnp.pad(placed[:, :, 1, :-1], ((0, 0), (0, 0), (1, 0)))
    owned = exchange_coarse(contrib, lax.axis_size("gx"), lax.axis_size("gy"))
    return (basis, owned.reshape(27, 1, 1, blocks_z))


def coarse_kernel(nx, ny, c_ref, o_ref, recv, send_sem, recv_sem):
    i = lax.axis_index("gx")
    j = lax.axis_index("gy")
    mesh_id = pl.DeviceIdType.MESH
    recv[...] = jnp.zeros_like(recv)
    routes = ((2, 0, 1, 0), (1, 1, 0, 1), (3, 2, 1, 1))
    barrier = pltpu.get_barrier_semaphore()
    for _, _, dx, dy in routes:
        has_dst = (i + dx < nx) & (j + dy < ny)
        has_src = (i - dx >= 0) & (j - dy >= 0)

        @pl.when(has_dst)
        def _():
            pl.semaphore_signal(barrier, 1, device_id=(i + dx, j + dy), device_id_type=mesh_id)

        @pl.when(has_src)
        def _():
            pl.semaphore_signal(barrier, 1, device_id=(i - dx, j - dy), device_id_type=mesh_id)

    peers = jnp.int32(0)
    for _, _, dx, dy in routes:
        has_dst = (i + dx < nx) & (j + dy < ny)
        has_src = (i - dx >= 0) & (j - dy >= 0)
        peers = peers + has_dst.astype(jnp.int32) + has_src.astype(jnp.int32)
    pl.semaphore_wait(barrier, peers)

    copies = []
    for slot, k, dx, dy in routes:
        has_dst = (i + dx < nx) & (j + dy < ny)
        has_src = (i - dx >= 0) & (j - dy >= 0)
        out_copy = pltpu.make_async_remote_copy(
            src_ref=c_ref.at[slot],
            dst_ref=recv.at[k],
            send_sem=send_sem.at[k],
            recv_sem=recv_sem.at[k],
            device_id=(jnp.minimum(i + dx, nx - 1), jnp.minimum(j + dy, ny - 1)),
            device_id_type=mesh_id,
        )
        copies.append((out_copy, has_dst, has_src))

        @pl.when(has_dst)
        def _():
            out_copy.start()

    for out_copy, has_dst, has_src in copies:
        @pl.when(has_dst)
        def _():
            out_copy.wait_send()

        @pl.when(has_src)
        def _():
            out_copy.wait_recv()

    o_ref[...] = c_ref[0] + recv[0] + recv[1] + recv[2]


def exchange_coarse(contrib, nx, ny):
    _, rows, cols = contrib.shape
    return pl.pallas_call(
        functools.partial(coarse_kernel, nx, ny),
        out_shape=jax.ShapeDtypeStruct((rows, cols), jnp.float32),
        in_specs=[pl.BlockSpec(memory_space=pltpu.VMEM)],
        out_specs=pl.BlockSpec(memory_space=pltpu.VMEM),
        scratch_shapes=[
            pltpu.VMEM((3, rows, cols), jnp.float32),
            pltpu.SemaphoreType.DMA((3,)),
            pltpu.SemaphoreType.DMA((3,)),
        ],
        compiler_params=pltpu.CompilerParams(collective_id=0, has_side_effects=True),
    )(contrib)


def solution(mesh):
    return jax.shard_map(
        shards,
        mesh=mesh,
        in_specs=(P(None, "gx", "gy", None), P("gx", "gy", None), P(), P("gx", "gy", None)),
        out_specs=(P(None, "gx", "gy", None), P(None, "gx", "gy", None)),
        check_vma=False,
    )
```

```python
import functools
import numpy as np
import jax
import jax.numpy as jnp
from jax import lax
from jax.experimental import pallas as pl
from jax.experimental.pallas import tpu as pltpu
from jax.sharding import PartitionSpec as P

CB = 16
ITERS = 3
HX = ITERS + 1
HY = ITERS + 1

omega_jacobi = 2.0 / 3.0
renorm_floor = 0.5


def with_halo(block, sides, width):
    for axis, dim in sides:
        count = lax.axis_size(axis)
        forward = [(i, i + 1) for i in range(count - 1)]
        backward = [(target, source) for source, target in forward]
        low = lax.ppermute(
            lax.slice_in_dim(block, block.shape[dim] - width, None, axis=dim), axis, forward
        )
        high = lax.ppermute(lax.slice_in_dim(block, 0, width, axis=dim), axis, backward)
        block = jnp.concatenate([low, block, high], axis=dim)
    return block


def from_behind(shard, axis, by):
    peers = lax.axis_size(axis)
    pairs = [(i, i + by) for i in range(peers) if 0 <= i + by < peers]
    return lax.ppermute(shard, axis, pairs)


def corner_of(slot_index):
    return (slot_index >> 2 & 1, slot_index >> 1 & 1, slot_index & 1)


def conductance(centre, neighbour):
    total_perm = centre + neighbour
    divisor = jnp.where(total_perm > 0.0, total_perm, 1.0)
    return 2.0 * centre * neighbour / divisor


def class_lookup(labels, class_perm):
    classes = jnp.arange(class_perm.shape[0])
    hits = labels[None] == classes[:, None, None, None]
    return jnp.sum(jnp.where(hits, class_perm[:, None, None, None], 0.0), axis=0)


def existing_bits(count_x, count_y, count_z, first_x, first_y, limit_x, limit_y, limit_z):
    block_x = (jnp.arange(count_x) + first_x) // CB
    block_y = (jnp.arange(count_y) + first_y) // CB
    block_z = jnp.arange(count_z) // CB
    bits = jnp.zeros((count_x, count_y, count_z), jnp.int32)
    for slot_index in range(8):
        corner_x, corner_y, corner_z = corner_of(slot_index)
        inside = (
            (block_x + corner_x < limit_x)[:, None, None]
            & (block_y + corner_y < limit_y)[None, :, None]
            & (block_z + corner_z < limit_z)[None, None, :]
        )
        bits = bits | jnp.where(inside, 1 << slot_index, 0)
    return bits


def halo_window(ref, xs, ys):
    if len(ref.shape) == 4:
        return ref.at[:, xs, ys, :]
    return ref.at[xs, ys, :]


def halo_range(d, count, halo):
    if d > 0:
        return pl.ds(count - halo, halo), pl.ds(0, halo)
    if d < 0:
        return pl.ds(0, halo), pl.ds(halo + count, halo)
    return pl.ds(0, count), pl.ds(halo, count)


def smooth_kernel(
    nx, ny,
    basis_in, labels_in, class_perm, support_in, basis_ref, prod_ref,
    eb, el, es, pm, tt, aux, valid, wa, wb, img, send_sem, recv_sem, local_sem,
):
    gi = lax.axis_index("gx")
    gj = lax.axis_index("gy")
    _, XE, YE, L = eb.shape
    NXL = basis_ref.shape[1]
    NYL = basis_ref.shape[2]
    mesh_id = pl.DeviceIdType.MESH
    sources = (basis_in, labels_in, support_in)
    targets = (eb, el, es)
    local_copies = []
    for a in range(3):
        local_copy = pltpu.make_async_copy(
            sources[a], halo_window(targets[a], pl.ds(HX, NXL), pl.ds(HY, NYL)), local_sem.at[a]
        )
        local_copy.start()
        local_copies.append(local_copy)

    directions = [(dx, dy) for dx in (-1, 0, 1) for dy in (-1, 0, 1) if (dx, dy) != (0, 0)]

    def has_device(x, y):
        return (x >= 0) & (x < nx) & (y >= 0) & (y < ny)

    peers = jnp.int32(0)
    for dx, dy in directions:
        _, to_x = halo_range(dx, NXL, HX)
        _, to_y = halo_range(dy, NYL, HY)
        from_here = has_device(gi - dx, gj - dy)
        peers = peers + from_here.astype(jnp.int32)

        @pl.when(jnp.logical_not(from_here))
        def _():
            for a in range(3):
                window = halo_window(targets[a], to_x, to_y)
                window[...] = jnp.zeros(window.shape, window.dtype)

    barrier = pltpu.get_barrier_semaphore()
    for dx, dy in directions:
        @pl.when(has_device(gi + dx, gj + dy))
        def _():
            pl.semaphore_signal(barrier, 1, device_id=(gi + dx, gj + dy), device_id_type=mesh_id)

    pl.semaphore_wait(barrier, peers)

    def remote_copy(k, a, dx, dy, target_x, target_y):
        from_x, to_x = halo_range(dx, NXL, HX)
        from_y, to_y = halo_range(dy, NYL, HY)
        return pltpu.make_async_remote_copy(
            src_ref=halo_window(sources[a], from_x, from_y),
            dst_ref=halo_window(targets[a], to_x, to_y),
            send_sem=send_sem.at[3 * k + a],
            recv_sem=recv_sem.at[3 * k + a],
            device_id=(target_x, target_y),
            device_id_type=mesh_id,
        )

    for k, (dx, dy) in enumerate(directions):
        @pl.when(has_device(gi + dx, gj + dy))
        def _():
            for a in range(3):
                remote_copy(k, a, dx, dy, gi + dx, gj + dy).start()

    for local_copy in local_copies:
        local_copy.wait()
    for k, (dx, dy) in enumerate(directions):
        @pl.when(has_device(gi + dx, gj + dy))
        def _():
            for a in range(3):
                remote_copy(k, a, dx, dy, gi + dx, gj + dy).wait_send()

        @pl.when(has_device(gi - dx, gj - dy))
        def _():
            for a in range(3):
                remote_copy(k, a, dx, dy, gi - dx, gj - dy).wait_recv()

    row = lax.broadcasted_iota(jnp.int32, (YE, L), 0)
    lane = lax.broadcasted_iota(jnp.int32, (YE, L), 1)
    ry = (row + (CB - HY)) & (CB - 1)
    m_yhi = ry == CB - 1
    m_ylo = ry == 0
    rz = lane & (CB - 1)
    m_zhi = rz == CB - 1
    m_zlo = rz == 0
    m_rows = (row >= HY) & (row < HY + NYL)
    global_y = gj * NYL + row - HY
    inside_y = (global_y >= 0) & (global_y < ny * NYL)
    node_y = gj + ((row + (CB - HY)) >> 4) < ny
    node_z = (lane >> 4) + 1 < L // CB

    def lookup(x, carry):
        labels = el[x]
        perm = jnp.zeros((YE, L), jnp.float32)
        for c in range(class_perm.shape[0]):
            perm = jnp.where(labels == c, class_perm[c], perm)
        global_x = gi * NXL + x - HX
        inside = inside_y & (global_x >= 0) & (global_x < nx * NXL)
        pm[x] = jnp.where(inside, perm, 0.0)
        return carry

    lax.fori_loop(0, XE, lookup, 0)

    def xplace(x):
        return (x + (CB - HX)) & (CB - 1)

    def pre(x, carry):
        pc = pm[x]
        pxp = jnp.where(x + 1 < XE, pm[jnp.minimum(x + 1, XE - 1)], 0.0)
        pxm = jnp.where(x >= 1, pm[jnp.maximum(x - 1, 0)], 0.0)
        pyp = pltpu.roll(pc, YE - 1, 0)
        pym = pltpu.roll(pc, 1, 0)
        pzp = pltpu.roll(pc, L - 1, 1)
        pzm = pltpu.roll(pc, 1, 1)
        t_xp = conductance(pc, pxp)
        t_xm = conductance(pc, pxm)
        t_yp = conductance(pc, pyp)
        t_ym = conductance(pc, pym)
        t_zp = jnp.where(lane == L - 1, 0.0, conductance(pc, pzp))
        t_zm = jnp.where(lane == 0, 0.0, conductance(pc, pzm))
        diag = t_xp + t_xm + t_yp + t_ym + t_zp + t_zm
        aux[0, x] = diag
        aux[1, x] = 1.0 / jnp.where(diag > 0.0, diag, 1.0)
        cx_hi = xplace(x) == CB - 1
        cx_lo = xplace(x) == 0
        tt[0, x] = t_xp
        tt[1, x] = jnp.where(cx_hi, 0.0, t_xp)
        tt[2, x] = t_xm
        tt[3, x] = jnp.where(cx_lo, 0.0, t_xm)
        tt[4, x] = t_yp
        tt[5, x] = jnp.where(m_yhi, 0.0, t_yp)
        tt[6, x] = t_ym
        tt[7, x] = jnp.where(m_ylo, 0.0, t_ym)
        tt[8, x] = t_zp
        tt[9, x] = jnp.where(m_zhi, 0.0, t_zp)
        tt[10, x] = t_zm
        tt[11, x] = jnp.where(m_zlo, 0.0, t_zm)
        sup = es[x]
        node_x = gi + ((x + (CB - HX)) >> 4) < nx
        for s in range(8):
            bx, by, bz = corner_of(s)
            keep = ((sup >> s) & 1) > 0
            if bx:
                keep = keep & node_x
            if by:
                keep = keep & node_y
            if bz:
                keep = keep & node_z
            v = jnp.where(keep, 1.0, 0.0)
            valid[s, x] = v
            wa[s, x] = eb[s, x] * v
        return carry

    lax.fori_loop(0, XE, pre, 0)

    def inflow_of(src, x, s, c):
        bx, by, bz = corner_of(s)
        cx_hi = xplace(x) == CB - 1
        cx_lo = xplace(x) == 0
        if bx:
            xp = src[jnp.where(cx_hi, s ^ 4, s), x + 1]
            t1 = tt[0, x]
            xm = src[s, x - 1]
            t2 = tt[3, x]
        else:
            xp = src[s, x + 1]
            t1 = tt[1, x]
            xm = src[jnp.where(cx_lo, s ^ 4, s), x - 1]
            t2 = tt[2, x]
        if by:
            yp = pltpu.roll(jnp.where(m_ylo, src[s ^ 2, x], c), YE - 1, 0)
            t3 = tt[4, x]
            ym = pltpu.roll(c, 1, 0)
            t4 = tt[7, x]
        else:
            yp = pltpu.roll(c, YE - 1, 0)
            t3 = tt[5, x]
            ym = pltpu.roll(jnp.where(m_yhi, src[s ^ 2, x], c), 1, 0)
            t4 = tt[6, x]
        if bz:
            zp = pltpu.roll(jnp.where(m_zlo, src[s ^ 1, x], c), L - 1, 1)
            t5 = tt[8, x]
            zm = pltpu.roll(c, 1, 1)
            t6 = tt[11, x]
        else:
            zp = pltpu.roll(c, L - 1, 1)
            t5 = tt[9, x]
            zm = pltpu.roll(jnp.where(m_zhi, src[s ^ 1, x], c), 1, 1)
            t6 = tt[10, x]
        return t1 * xp + t2 * xm + t3 * yp + t4 * ym + t5 * zp + t6 * zm

    def sweep(src, dst, lo, hi):
        def body(x, carry):
            diag = aux[0, x]
            inv = aux[1, x]
            for s in range(8):
                c = src[s, x]
                inflow = inflow_of(src, x, s, c)
                dst[s, x] = (c - omega_jacobi * (diag * c - inflow) * inv) * valid[s, x]
            return carry

        lax.fori_loop(lo, hi, body, 0)

    bufs = (wa, wb)
    for step in range(ITERS):
        sweep(bufs[step % 2], bufs[(step + 1) % 2], step + 1, XE - step - 1)
    last = bufs[ITERS % 2]
    basis_buf = bufs[(ITERS + 1) % 2]

    def normalize(x, carry):
        vals = [last[s, x] for s in range(8)]
        total = vals[0]
        for s in range(1, 8):
            total = total + vals[s]
        scale = jnp.maximum(total, renorm_floor)
        for s in range(8):
            basis_buf[s, x] = vals[s] / scale
        return carry

    lax.fori_loop(ITERS, XE - ITERS, normalize, 0)

    def image(x, carry):
        diag = aux[0, x]
        for s in range(8):
            c = basis_buf[s, x]
            inflow = inflow_of(basis_buf, x, s, c)
            img[s, x - HX] = jnp.where(m_rows, diag * c - inflow, 0.0)
            basis_ref[s, x - HX] = c[HY:HY + NYL, :]
        return carry

    lax.fori_loop(HX, HX + NXL, image, 0)

    for s1 in range(8):
        def pair_sums(x, acc):
            b = basis_buf[s1, x + HX]
            return tuple(acc[s2] + b * img[s2, x] for s2 in range(8))

        acc = lax.fori_loop(
            0, NXL, pair_sums, tuple(jnp.zeros((YE, L), jnp.float32) for _ in range(8))
        )
        for s2 in range(8):
            prod_ref[pl.ds(s1 * 8 + s2, 1), :] = jnp.sum(acc[s2], axis=0, keepdims=True)


def assembly_matrix():
    table = np.zeros((4 * 27 * 2, 64), np.float32)
    for first_slot in range(8):
        for second_slot in range(8):
            one_x, one_y, one_z = corner_of(first_slot)
            two_x, two_y, two_z = corner_of(second_slot)
            offset_index = 9 * (two_x - one_x + 1) + 3 * (two_y - one_y + 1) + (two_z - one_z + 1)
            row = ((one_x * 2 + one_y) * 27 + offset_index) * 2 + one_z
            table[row, first_slot * 8 + second_slot] = 1.0
    return table


def shards(initial_basis, labels, class_perm, support):
    size_x, size_y, size_z = labels.shape
    assert size_x == CB and size_y == CB and size_z % CB == 0
    blocks_z = size_z // CB
    nx = lax.axis_size("gx")
    ny = lax.axis_size("gy")
    XE, YE = size_x + 2 * HX, size_y + 2 * HY
    f32 = jnp.float32
    vmem = pl.BlockSpec(memory_space=pltpu.VMEM)
    basis, prods = pl.pallas_call(
        functools.partial(smooth_kernel, nx, ny),
        out_shape=(
            jax.ShapeDtypeStruct((8, size_x, size_y, size_z), f32),
            jax.ShapeDtypeStruct((64, size_z), f32),
        ),
        in_specs=[vmem, vmem, pl.BlockSpec(memory_space=pltpu.SMEM), vmem],
        out_specs=(vmem, vmem),
        scratch_shapes=[
            pltpu.VMEM((8, XE, YE, size_z), f32),
            pltpu.VMEM((XE, YE, size_z), jnp.int32),
            pltpu.VMEM((XE, YE, size_z), jnp.int32),
            pltpu.VMEM((XE, YE, size_z), f32),
            pltpu.VMEM((12, XE, YE, size_z), f32),
            pltpu.VMEM((2, XE, YE, size_z), f32),
            pltpu.VMEM((8, XE, YE, size_z), f32),
            pltpu.VMEM((8, XE, YE, size_z), f32),
            pltpu.VMEM((8, XE, YE, size_z), f32),
            pltpu.VMEM((8, size_x, YE, size_z), f32),
            pltpu.SemaphoreType.DMA((24,)),
            pltpu.SemaphoreType.DMA((24,)),
            pltpu.SemaphoreType.DMA((3,)),
        ],
        compiler_params=pltpu.CompilerParams(collective_id=1, has_side_effects=True),
    )(initial_basis, labels, class_perm, support)
    block_sums = prods.reshape(64, blocks_z, CB).sum(axis=-1)
    placed = jnp.dot(
        jnp.asarray(assembly_matrix()), block_sums, precision=lax.Precision.HIGHEST
    ).reshape(4, 27, 2, blocks_z)
    contrib = placed[:, :, 0] + jnp.pad(placed[:, :, 1, :-1], ((0, 0), (0, 0), (1, 0)))
    owned = exchange_coarse(contrib, lax.axis_size("gx"), lax.axis_size("gy"))
    return (basis, owned.reshape(27, 1, 1, blocks_z))


def coarse_kernel(nx, ny, c_ref, o_ref, recv, send_sem, recv_sem):
    i = lax.axis_index("gx")
    j = lax.axis_index("gy")
    mesh_id = pl.DeviceIdType.MESH
    recv[...] = jnp.zeros_like(recv)
    routes = ((2, 0, 1, 0), (1, 1, 0, 1), (3, 2, 1, 1))
    barrier = pltpu.get_barrier_semaphore()
    for _, _, dx, dy in routes:
        has_dst = (i + dx < nx) & (j + dy < ny)
        has_src = (i - dx >= 0) & (j - dy >= 0)

        @pl.when(has_dst)
        def _():
            pl.semaphore_signal(barrier, 1, device_id=(i + dx, j + dy), device_id_type=mesh_id)

        @pl.when(has_src)
        def _():
            pl.semaphore_signal(barrier, 1, device_id=(i - dx, j - dy), device_id_type=mesh_id)

    peers = jnp.int32(0)
    for _, _, dx, dy in routes:
        has_dst = (i + dx < nx) & (j + dy < ny)
        has_src = (i - dx >= 0) & (j - dy >= 0)
        peers = peers + has_dst.astype(jnp.int32) + has_src.astype(jnp.int32)
    pl.semaphore_wait(barrier, peers)

    copies = []
    for slot, k, dx, dy in routes:
        has_dst = (i + dx < nx) & (j + dy < ny)
        has_src = (i - dx >= 0) & (j - dy >= 0)
        out_copy = pltpu.make_async_remote_copy(
            src_ref=c_ref.at[slot],
            dst_ref=recv.at[k],
            send_sem=send_sem.at[k],
            recv_sem=recv_sem.at[k],
            device_id=(jnp.minimum(i + dx, nx - 1), jnp.minimum(j + dy, ny - 1)),
            device_id_type=mesh_id,
        )
        copies.append((out_copy, has_dst, has_src))

        @pl.when(has_dst)
        def _():
            out_copy.start()

    for out_copy, has_dst, has_src in copies:
        @pl.when(has_dst)
        def _():
            out_copy.wait_send()

        @pl.when(has_src)
        def _():
            out_copy.wait_recv()

    o_ref[...] = c_ref[0] + recv[0] + recv[1] + recv[2]


def exchange_coarse(contrib, nx, ny):
    _, rows, cols = contrib.shape
    return pl.pallas_call(
        functools.partial(coarse_kernel, nx, ny),
        out_shape=jax.ShapeDtypeStruct((rows, cols), jnp.float32),
        in_specs=[pl.BlockSpec(memory_space=pltpu.VMEM)],
        out_specs=pl.BlockSpec(memory_space=pltpu.VMEM),
        scratch_shapes=[
            pltpu.VMEM((3, rows, cols), jnp.float32),
            pltpu.SemaphoreType.DMA((3,)),
            pltpu.SemaphoreType.DMA((3,)),
        ],
        compiler_params=pltpu.CompilerParams(collective_id=0, has_side_effects=True),
    )(contrib)


def solution(mesh):
    return jax.shard_map(
        shards,
        mesh=mesh,
        in_specs=(P(None, "gx", "gy", None), P("gx", "gy", None), P(), P("gx", "gy", None)),
        out_specs=(P(None, "gx", "gy", None), P(None, "gx", "gy", None)),
        check_vma=False,
    )
```

```python
import functools
import numpy as np
import jax
import jax.numpy as jnp
from jax import lax
from jax.experimental import pallas as pl
from jax.experimental.pallas import tpu as pltpu
from jax.sharding import PartitionSpec as P

CB = 16
ITERS = 3
HX = ITERS + 1
HY = ITERS + 1

omega_jacobi = 2.0 / 3.0
renorm_floor = 0.5


def with_halo(block, sides, width):
    for axis, dim in sides:
        count = lax.axis_size(axis)
        forward = [(i, i + 1) for i in range(count - 1)]
        backward = [(target, source) for source, target in forward]
        low = lax.ppermute(
            lax.slice_in_dim(block, block.shape[dim] - width, None, axis=dim), axis, forward
        )
        high = lax.ppermute(lax.slice_in_dim(block, 0, width, axis=dim), axis, backward)
        block = jnp.concatenate([low, block, high], axis=dim)
    return block


def from_behind(shard, axis, by):
    peers = lax.axis_size(axis)
    pairs = [(i, i + by) for i in range(peers) if 0 <= i + by < peers]
    return lax.ppermute(shard, axis, pairs)


def corner_of(slot_index):
    return (slot_index >> 2 & 1, slot_index >> 1 & 1, slot_index & 1)


def conductance(centre, neighbour):
    total_perm = centre + neighbour
    divisor = jnp.where(total_perm > 0.0, total_perm, 1.0)
    return 2.0 * centre * neighbour / divisor


def class_lookup(labels, class_perm):
    classes = jnp.arange(class_perm.shape[0])
    hits = labels[None] == classes[:, None, None, None]
    return jnp.sum(jnp.where(hits, class_perm[:, None, None, None], 0.0), axis=0)


def existing_bits(count_x, count_y, count_z, first_x, first_y, limit_x, limit_y, limit_z):
    block_x = (jnp.arange(count_x) + first_x) // CB
    block_y = (jnp.arange(count_y) + first_y) // CB
    block_z = jnp.arange(count_z) // CB
    bits = jnp.zeros((count_x, count_y, count_z), jnp.int32)
    for slot_index in range(8):
        corner_x, corner_y, corner_z = corner_of(slot_index)
        inside = (
            (block_x + corner_x < limit_x)[:, None, None]
            & (block_y + corner_y < limit_y)[None, :, None]
            & (block_z + corner_z < limit_z)[None, None, :]
        )
        bits = bits | jnp.where(inside, 1 << slot_index, 0)
    return bits


def halo_window(ref, xs, ys):
    if len(ref.shape) == 4:
        return ref.at[:, xs, ys, :]
    return ref.at[xs, ys, :]


def halo_range(d, count, halo):
    if d > 0:
        return pl.ds(count - halo, halo), pl.ds(0, halo)
    if d < 0:
        return pl.ds(0, halo), pl.ds(halo + count, halo)
    return pl.ds(0, count), pl.ds(halo, count)


def halo_rows(d, count, halo):
    if d > 0:
        return pl.ds(count - halo, halo), pl.ds(count + halo, halo)
    if d < 0:
        return pl.ds(0, halo), pl.ds(count, halo)
    return pl.ds(0, count), pl.ds(0, count)


def smooth_kernel(
    nx, ny,
    basis_in, labels_in, class_perm, support_in, basis_ref, prod_ref,
    eb, el, es, pm, tt, aux, valid, wa, wb, img, send_sem, recv_sem, local_sem,
):
    gi = lax.axis_index("gx")
    gj = lax.axis_index("gy")
    _, XE, YE, L = eb.shape
    NXL = basis_ref.shape[1]
    NYL = basis_ref.shape[2]
    mesh_id = pl.DeviceIdType.MESH
    sources = (basis_in, labels_in, support_in)
    targets = (eb, el, es)
    local_copies = []
    for a in range(3):
        local_copy = pltpu.make_async_copy(
            sources[a], halo_window(targets[a], pl.ds(HX, NXL), pl.ds(0, NYL)), local_sem.at[a]
        )
        local_copy.start()
        local_copies.append(local_copy)

    directions = [(dx, dy) for dx in (-1, 0, 1) for dy in (-1, 0, 1) if (dx, dy) != (0, 0)]

    def has_device(x, y):
        return (x >= 0) & (x < nx) & (y >= 0) & (y < ny)

    peers = jnp.int32(0)
    for dx, dy in directions:
        _, to_x = halo_range(dx, NXL, HX)
        _, to_y = halo_rows(dy, NYL, HY)
        from_here = has_device(gi - dx, gj - dy)
        peers = peers + from_here.astype(jnp.int32)

        @pl.when(jnp.logical_not(from_here))
        def _():
            for a in range(3):
                window = halo_window(targets[a], to_x, to_y)
                window[...] = jnp.zeros(window.shape, window.dtype)

    barrier = pltpu.get_barrier_semaphore()
    for dx, dy in directions:
        @pl.when(has_device(gi + dx, gj + dy))
        def _():
            pl.semaphore_signal(barrier, 1, device_id=(gi + dx, gj + dy), device_id_type=mesh_id)

    pl.semaphore_wait(barrier, peers)

    def remote_copy(k, a, dx, dy, target_x, target_y):
        from_x, to_x = halo_range(dx, NXL, HX)
        from_y, to_y = halo_rows(dy, NYL, HY)
        return pltpu.make_async_remote_copy(
            src_ref=halo_window(sources[a], from_x, from_y),
            dst_ref=halo_window(targets[a], to_x, to_y),
            send_sem=send_sem.at[3 * k + a],
            recv_sem=recv_sem.at[3 * k + a],
            device_id=(target_x, target_y),
            device_id_type=mesh_id,
        )

    for k, (dx, dy) in enumerate(directions):
        @pl.when(has_device(gi + dx, gj + dy))
        def _():
            for a in range(3):
                remote_copy(k, a, dx, dy, gi + dx, gj + dy).start()

    for local_copy in local_copies:
        local_copy.wait()
    for k, (dx, dy) in enumerate(directions):
        @pl.when(has_device(gi + dx, gj + dy))
        def _():
            for a in range(3):
                remote_copy(k, a, dx, dy, gi + dx, gj + dy).wait_send()

        @pl.when(has_device(gi - dx, gj - dy))
        def _():
            for a in range(3):
                remote_copy(k, a, dx, dy, gi - dx, gj - dy).wait_recv()

    row = lax.broadcasted_iota(jnp.int32, (YE, L), 0)
    lane = lax.broadcasted_iota(jnp.int32, (YE, L), 1)
    m_yhi = (row == NYL - 1) | (row == YE - 1)
    m_ylo = (row == 0) | (row == NYL)
    rz = lane & (CB - 1)
    m_zhi = rz == CB - 1
    m_zlo = rz == 0
    m_rows = row < NYL
    block_y = gj + jnp.where(row < NYL, 0, jnp.where(row < NYL + HY, 1, -1))
    global_y = jnp.where(row < NYL + HY, gj * NYL + row, gj * NYL + row - YE)
    inside_y = (global_y >= 0) & (global_y < ny * NYL)
    node_y = block_y + 1 < ny
    node_z = (lane >> 4) + 1 < L // CB

    def lookup(x, carry):
        labels = el[x]
        perm = jnp.zeros((YE, L), jnp.float32)
        for c in range(class_perm.shape[0]):
            perm = jnp.where(labels == c, class_perm[c], perm)
        global_x = gi * NXL + x - HX
        inside = inside_y & (global_x >= 0) & (global_x < nx * NXL)
        pm[x] = jnp.where(inside, perm, 0.0)
        return carry

    lax.fori_loop(0, XE, lookup, 0)

    def xplace(x):
        return (x + (CB - HX)) & (CB - 1)

    def pre(x, carry):
        pc = pm[x]
        pxp = jnp.where(x + 1 < XE, pm[jnp.minimum(x + 1, XE - 1)], 0.0)
        pxm = jnp.where(x >= 1, pm[jnp.maximum(x - 1, 0)], 0.0)
        pyp = pltpu.roll(pc, YE - 1, 0)
        pym = pltpu.roll(pc, 1, 0)
        pzp = pltpu.roll(pc, L - 1, 1)
        pzm = pltpu.roll(pc, 1, 1)
        t_xp = conductance(pc, pxp)
        t_xm = conductance(pc, pxm)
        t_yp = conductance(pc, pyp)
        t_ym = conductance(pc, pym)
        t_zp = jnp.where(lane == L - 1, 0.0, conductance(pc, pzp))
        t_zm = jnp.where(lane == 0, 0.0, conductance(pc, pzm))
        diag = t_xp + t_xm + t_yp + t_ym + t_zp + t_zm
        aux[0, x] = diag
        aux[1, x] = 1.0 / jnp.where(diag > 0.0, diag, 1.0)
        cx_hi = xplace(x) == CB - 1
        cx_lo = xplace(x) == 0
        tt[0, x] = t_xp
        tt[1, x] = jnp.where(cx_hi, 0.0, t_xp)
        tt[2, x] = t_xm
        tt[3, x] = jnp.where(cx_lo, 0.0, t_xm)
        tt[4, x] = t_yp
        tt[5, x] = jnp.where(m_yhi, 0.0, t_yp)
        tt[6, x] = t_ym
        tt[7, x] = jnp.where(m_ylo, 0.0, t_ym)
        tt[8, x] = t_zp
        tt[9, x] = jnp.where(m_zhi, 0.0, t_zp)
        tt[10, x] = t_zm
        tt[11, x] = jnp.where(m_zlo, 0.0, t_zm)
        sup = es[x]
        node_x = gi + ((x + (CB - HX)) >> 4) < nx
        for s in range(8):
            bx, by, bz = corner_of(s)
            keep = ((sup >> s) & 1) > 0
            if bx:
                keep = keep & node_x
            if by:
                keep = keep & node_y
            if bz:
                keep = keep & node_z
            v = jnp.where(keep, 1.0, 0.0)
            valid[s, x] = v
            wa[s, x] = eb[s, x] * v
        return carry

    lax.fori_loop(0, XE, pre, 0)

    def inflow_of(src, x, s, c):
        bx, by, bz = corner_of(s)
        cx_hi = xplace(x) == CB - 1
        cx_lo = xplace(x) == 0
        if bx:
            xp = src[jnp.where(cx_hi, s ^ 4, s), x + 1]
            t1 = tt[0, x]
            xm = src[s, x - 1]
            t2 = tt[3, x]
        else:
            xp = src[s, x + 1]
            t1 = tt[1, x]
            xm = src[jnp.where(cx_lo, s ^ 4, s), x - 1]
            t2 = tt[2, x]
        if by:
            yp = pltpu.roll(jnp.where(m_ylo, src[s ^ 2, x], c), YE - 1, 0)
            t3 = tt[4, x]
            ym = pltpu.roll(c, 1, 0)
            t4 = tt[7, x]
        else:
            yp = pltpu.roll(c, YE - 1, 0)
            t3 = tt[5, x]
            ym = pltpu.roll(jnp.where(m_yhi, src[s ^ 2, x], c), 1, 0)
            t4 = tt[6, x]
        if bz:
            zp = pltpu.roll(jnp.where(m_zlo, src[s ^ 1, x], c), L - 1, 1)
            t5 = tt[8, x]
            zm = pltpu.roll(c, 1, 1)
            t6 = tt[11, x]
        else:
            zp = pltpu.roll(c, L - 1, 1)
            t5 = tt[9, x]
            zm = pltpu.roll(jnp.where(m_zhi, src[s ^ 1, x], c), 1, 1)
            t6 = tt[10, x]
        return t1 * xp + t2 * xm + t3 * yp + t4 * ym + t5 * zp + t6 * zm

    def sweep(src, dst, lo, hi):
        def body(x, carry):
            diag = aux[0, x]
            inv = aux[1, x]
            for s in range(8):
                c = src[s, x]
                inflow = inflow_of(src, x, s, c)
                dst[s, x] = (c - omega_jacobi * (diag * c - inflow) * inv) * valid[s, x]
            return carry

        lax.fori_loop(lo, hi, body, 0)

    bufs = (wa, wb)
    for step in range(ITERS):
        sweep(bufs[step % 2], bufs[(step + 1) % 2], step + 1, XE - step - 1)
    last = bufs[ITERS % 2]
    basis_buf = bufs[(ITERS + 1) % 2]

    def normalize(x, carry):
        vals = [last[s, x] for s in range(8)]
        total = vals[0]
        for s in range(1, 8):
            total = total + vals[s]
        scale = jnp.maximum(total, renorm_floor)
        for s in range(8):
            basis_buf[s, x] = vals[s] / scale
        return carry

    lax.fori_loop(ITERS, XE - ITERS, normalize, 0)

    def image(x, carry):
        diag = aux[0, x]
        for s in range(8):
            c = basis_buf[s, x]
            inflow = inflow_of(basis_buf, x, s, c)
            img[s, x - HX] = jnp.where(m_rows, diag * c - inflow, 0.0)
            basis_ref[s, x - HX] = c[:NYL, :]
        return carry

    lax.fori_loop(HX, HX + NXL, image, 0)

    for s1 in range(8):
        def pair_sums(x, acc):
            b = basis_buf[s1, x + HX]
            return tuple(acc[s2] + b * img[s2, x] for s2 in range(8))

        acc = lax.fori_loop(
            0, NXL, pair_sums, tuple(jnp.zeros((YE, L), jnp.float32) for _ in range(8))
        )
        for s2 in range(8):
            prod_ref[pl.ds(s1 * 8 + s2, 1), :] = jnp.sum(acc[s2], axis=0, keepdims=True)


def assembly_matrix():
    table = np.zeros((4 * 27 * 2, 64), np.float32)
    for first_slot in range(8):
        for second_slot in range(8):
            one_x, one_y, one_z = corner_of(first_slot)
            two_x, two_y, two_z = corner_of(second_slot)
            offset_index = 9 * (two_x - one_x + 1) + 3 * (two_y - one_y + 1) + (two_z - one_z + 1)
            row = ((one_x * 2 + one_y) * 27 + offset_index) * 2 + one_z
            table[row, first_slot * 8 + second_slot] = 1.0
    return table


def shards(initial_basis, labels, class_perm, support):
    size_x, size_y, size_z = labels.shape
    assert size_x == CB and size_y == CB and size_z % CB == 0
    blocks_z = size_z // CB
    nx = lax.axis_size("gx")
    ny = lax.axis_size("gy")
    XE, YE = size_x + 2 * HX, size_y + 2 * HY
    f32 = jnp.float32
    vmem = pl.BlockSpec(memory_space=pltpu.VMEM)
    basis, prods = pl.pallas_call(
        functools.partial(smooth_kernel, nx, ny),
        out_shape=(
            jax.ShapeDtypeStruct((8, size_x, size_y, size_z), f32),
            jax.ShapeDtypeStruct((64, size_z), f32),
        ),
        in_specs=[vmem, vmem, pl.BlockSpec(memory_space=pltpu.SMEM), vmem],
        out_specs=(vmem, vmem),
        scratch_shapes=[
            pltpu.VMEM((8, XE, YE, size_z), f32),
            pltpu.VMEM((XE, YE, size_z), jnp.int32),
            pltpu.VMEM((XE, YE, size_z), jnp.int32),
            pltpu.VMEM((XE, YE, size_z), f32),
            pltpu.VMEM((12, XE, YE, size_z), f32),
            pltpu.VMEM((2, XE, YE, size_z), f32),
            pltpu.VMEM((8, XE, YE, size_z), f32),
            pltpu.VMEM((8, XE, YE, size_z), f32),
            pltpu.VMEM((8, XE, YE, size_z), f32),
            pltpu.VMEM((8, size_x, YE, size_z), f32),
            pltpu.SemaphoreType.DMA((24,)),
            pltpu.SemaphoreType.DMA((24,)),
            pltpu.SemaphoreType.DMA((3,)),
        ],
        compiler_params=pltpu.CompilerParams(collective_id=1, has_side_effects=True),
    )(initial_basis, labels, class_perm, support)
    block_sums = prods.reshape(64, blocks_z, CB).sum(axis=-1)
    placed = jnp.dot(
        jnp.asarray(assembly_matrix()), block_sums, precision=lax.Precision.HIGHEST
    ).reshape(4, 27, 2, blocks_z)
    contrib = placed[:, :, 0] + jnp.pad(placed[:, :, 1, :-1], ((0, 0), (0, 0), (1, 0)))
    owned = exchange_coarse(contrib, lax.axis_size("gx"), lax.axis_size("gy"))
    return (basis, owned.reshape(27, 1, 1, blocks_z))


def coarse_kernel(nx, ny, c_ref, o_ref, recv, send_sem, recv_sem):
    i = lax.axis_index("gx")
    j = lax.axis_index("gy")
    mesh_id = pl.DeviceIdType.MESH
    recv[...] = jnp.zeros_like(recv)
    routes = ((2, 0, 1, 0), (1, 1, 0, 1), (3, 2, 1, 1))
    barrier = pltpu.get_barrier_semaphore()
    for _, _, dx, dy in routes:
        has_dst = (i + dx < nx) & (j + dy < ny)
        has_src = (i - dx >= 0) & (j - dy >= 0)

        @pl.when(has_dst)
        def _():
            pl.semaphore_signal(barrier, 1, device_id=(i + dx, j + dy), device_id_type=mesh_id)

        @pl.when(has_src)
        def _():
            pl.semaphore_signal(barrier, 1, device_id=(i - dx, j - dy), device_id_type=mesh_id)

    peers = jnp.int32(0)
    for _, _, dx, dy in routes:
        has_dst = (i + dx < nx) & (j + dy < ny)
        has_src = (i - dx >= 0) & (j - dy >= 0)
        peers = peers + has_dst.astype(jnp.int32) + has_src.astype(jnp.int32)
    pl.semaphore_wait(barrier, peers)

    copies = []
    for slot, k, dx, dy in routes:
        has_dst = (i + dx < nx) & (j + dy < ny)
        has_src = (i - dx >= 0) & (j - dy >= 0)
        out_copy = pltpu.make_async_remote_copy(
            src_ref=c_ref.at[slot],
            dst_ref=recv.at[k],
            send_sem=send_sem.at[k],
            recv_sem=recv_sem.at[k],
            device_id=(jnp.minimum(i + dx, nx - 1), jnp.minimum(j + dy, ny - 1)),
            device_id_type=mesh_id,
        )
        copies.append((out_copy, has_dst, has_src))

        @pl.when(has_dst)
        def _():
            out_copy.start()

    for out_copy, has_dst, has_src in copies:
        @pl.when(has_dst)
        def _():
            out_copy.wait_send()

        @pl.when(has_src)
        def _():
            out_copy.wait_recv()

    o_ref[...] = c_ref[0] + recv[0] + recv[1] + recv[2]


def exchange_coarse(contrib, nx, ny):
    _, rows, cols = contrib.shape
    return pl.pallas_call(
        functools.partial(coarse_kernel, nx, ny),
        out_shape=jax.ShapeDtypeStruct((rows, cols), jnp.float32),
        in_specs=[pl.BlockSpec(memory_space=pltpu.VMEM)],
        out_specs=pl.BlockSpec(memory_space=pltpu.VMEM),
        scratch_shapes=[
            pltpu.VMEM((3, rows, cols), jnp.float32),
            pltpu.SemaphoreType.DMA((3,)),
            pltpu.SemaphoreType.DMA((3,)),
        ],
        compiler_params=pltpu.CompilerParams(collective_id=0, has_side_effects=True),
    )(contrib)


def solution(mesh):
    return jax.shard_map(
        shards,
        mesh=mesh,
        in_specs=(P(None, "gx", "gy", None), P("gx", "gy", None), P(), P("gx", "gy", None)),
        out_specs=(P(None, "gx", "gy", None), P(None, "gx", "gy", None)),
        check_vma=False,
    )
```

```python
import functools
import numpy as np
import jax
import jax.numpy as jnp
from jax import lax
from jax.experimental import pallas as pl
from jax.experimental.pallas import tpu as pltpu
from jax.sharding import PartitionSpec as P

CB = 16
ITERS = 3
HX = ITERS + 1
HY = ITERS + 1

omega_jacobi = 2.0 / 3.0
renorm_floor = 0.5


def with_halo(block, sides, width):
    for axis, dim in sides:
        count = lax.axis_size(axis)
        forward = [(i, i + 1) for i in range(count - 1)]
        backward = [(target, source) for source, target in forward]
        low = lax.ppermute(
            lax.slice_in_dim(block, block.shape[dim] - width, None, axis=dim), axis, forward
        )
        high = lax.ppermute(lax.slice_in_dim(block, 0, width, axis=dim), axis, backward)
        block = jnp.concatenate([low, block, high], axis=dim)
    return block


def from_behind(shard, axis, by):
    peers = lax.axis_size(axis)
    pairs = [(i, i + by) for i in range(peers) if 0 <= i + by < peers]
    return lax.ppermute(shard, axis, pairs)


def corner_of(slot_index):
    return (slot_index >> 2 & 1, slot_index >> 1 & 1, slot_index & 1)


def conductance(centre, neighbour):
    total_perm = centre + neighbour
    divisor = jnp.where(total_perm > 0.0, total_perm, 1.0)
    return 2.0 * centre * neighbour / divisor


def class_lookup(labels, class_perm):
    classes = jnp.arange(class_perm.shape[0])
    hits = labels[None] == classes[:, None, None, None]
    return jnp.sum(jnp.where(hits, class_perm[:, None, None, None], 0.0), axis=0)


def existing_bits(count_x, count_y, count_z, first_x, first_y, limit_x, limit_y, limit_z):
    block_x = (jnp.arange(count_x) + first_x) // CB
    block_y = (jnp.arange(count_y) + first_y) // CB
    block_z = jnp.arange(count_z) // CB
    bits = jnp.zeros((count_x, count_y, count_z), jnp.int32)
    for slot_index in range(8):
        corner_x, corner_y, corner_z = corner_of(slot_index)
        inside = (
            (block_x + corner_x < limit_x)[:, None, None]
            & (block_y + corner_y < limit_y)[None, :, None]
            & (block_z + corner_z < limit_z)[None, None, :]
        )
        bits = bits | jnp.where(inside, 1 << slot_index, 0)
    return bits


def halo_window(ref, xs, ys):
    if len(ref.shape) == 4:
        return ref.at[:, xs, ys, :]
    return ref.at[xs, ys, :]


def halo_range(d, count, halo):
    if d > 0:
        return pl.ds(count - halo, halo), pl.ds(0, halo)
    if d < 0:
        return pl.ds(0, halo), pl.ds(halo + count, halo)
    return pl.ds(0, count), pl.ds(halo, count)


def halo_rows(d, count, halo):
    if d > 0:
        return pl.ds(count - halo, halo), pl.ds(count + halo, halo)
    if d < 0:
        return pl.ds(0, halo), pl.ds(count, halo)
    return pl.ds(0, count), pl.ds(0, count)


def smooth_kernel(
    nx, ny,
    basis_in, labels_in, class_perm, support_in, placing, basis_ref, coarse_ref,
    eb, el, es, pm, tt, aux, valid, wa, wb, img, prod_ref, terms, received,
    send_sem, recv_sem, local_sem, coarse_send, coarse_recv,
):
    gi = lax.axis_index("gx")
    gj = lax.axis_index("gy")
    _, XE, YE, L = eb.shape
    NXL = basis_ref.shape[1]
    NYL = basis_ref.shape[2]
    mesh_id = pl.DeviceIdType.MESH
    sources = (basis_in, labels_in, support_in)
    targets = (eb, el, es)
    local_copies = []
    for a in range(3):
        local_copy = pltpu.make_async_copy(
            sources[a], halo_window(targets[a], pl.ds(HX, NXL), pl.ds(0, NYL)), local_sem.at[a]
        )
        local_copy.start()
        local_copies.append(local_copy)

    directions = [(dx, dy) for dx in (-1, 0, 1) for dy in (-1, 0, 1) if (dx, dy) != (0, 0)]

    def has_device(x, y):
        return (x >= 0) & (x < nx) & (y >= 0) & (y < ny)

    peers = jnp.int32(0)
    for dx, dy in directions:
        _, to_x = halo_range(dx, NXL, HX)
        _, to_y = halo_rows(dy, NYL, HY)
        from_here = has_device(gi - dx, gj - dy)
        peers = peers + from_here.astype(jnp.int32)

        @pl.when(jnp.logical_not(from_here))
        def _():
            for a in range(3):
                window = halo_window(targets[a], to_x, to_y)
                window[...] = jnp.zeros(window.shape, window.dtype)

    coarse_routes = ((2, 1, 0), (1, 0, 1), (3, 1, 1))
    for k, (_, dx, dy) in enumerate(coarse_routes):
        @pl.when(jnp.logical_not(has_device(gi - dx, gj - dy)))
        def _():
            received[k] = jnp.zeros(received.shape[1:], received.dtype)

    barrier = pltpu.get_barrier_semaphore()
    for dx, dy in directions:
        @pl.when(has_device(gi + dx, gj + dy))
        def _():
            pl.semaphore_signal(barrier, 1, device_id=(gi + dx, gj + dy), device_id_type=mesh_id)

    pl.semaphore_wait(barrier, peers)

    def remote_copy(k, a, dx, dy, target_x, target_y):
        from_x, to_x = halo_range(dx, NXL, HX)
        from_y, to_y = halo_rows(dy, NYL, HY)
        return pltpu.make_async_remote_copy(
            src_ref=halo_window(sources[a], from_x, from_y),
            dst_ref=halo_window(targets[a], to_x, to_y),
            send_sem=send_sem.at[3 * k + a],
            recv_sem=recv_sem.at[3 * k + a],
            device_id=(target_x, target_y),
            device_id_type=mesh_id,
        )

    for k, (dx, dy) in enumerate(directions):
        @pl.when(has_device(gi + dx, gj + dy))
        def _():
            for a in range(3):
                remote_copy(k, a, dx, dy, gi + dx, gj + dy).start()

    for local_copy in local_copies:
        local_copy.wait()
    for k, (dx, dy) in enumerate(directions):
        @pl.when(has_device(gi + dx, gj + dy))
        def _():
            for a in range(3):
                remote_copy(k, a, dx, dy, gi + dx, gj + dy).wait_send()

        @pl.when(has_device(gi - dx, gj - dy))
        def _():
            for a in range(3):
                remote_copy(k, a, dx, dy, gi - dx, gj - dy).wait_recv()

    row = lax.broadcasted_iota(jnp.int32, (YE, L), 0)
    lane = lax.broadcasted_iota(jnp.int32, (YE, L), 1)
    m_yhi = (row == NYL - 1) | (row == YE - 1)
    m_ylo = (row == 0) | (row == NYL)
    rz = lane & (CB - 1)
    m_zhi = rz == CB - 1
    m_zlo = rz == 0
    m_rows = row < NYL
    block_y = gj + jnp.where(row < NYL, 0, jnp.where(row < NYL + HY, 1, -1))
    global_y = jnp.where(row < NYL + HY, gj * NYL + row, gj * NYL + row - YE)
    inside_y = (global_y >= 0) & (global_y < ny * NYL)
    node_y = block_y + 1 < ny
    node_z = (lane >> 4) + 1 < L // CB

    def lookup(x, carry):
        labels = el[x]
        perm = jnp.zeros((YE, L), jnp.float32)
        for c in range(class_perm.shape[0]):
            perm = jnp.where(labels == c, class_perm[c], perm)
        global_x = gi * NXL + x - HX
        inside = inside_y & (global_x >= 0) & (global_x < nx * NXL)
        pm[x] = jnp.where(inside, perm, 0.0)
        return carry

    lax.fori_loop(0, XE, lookup, 0)

    def xplace(x):
        return (x + (CB - HX)) & (CB - 1)

    def pre(x, carry):
        pc = pm[x]
        pxp = jnp.where(x + 1 < XE, pm[jnp.minimum(x + 1, XE - 1)], 0.0)
        pxm = jnp.where(x >= 1, pm[jnp.maximum(x - 1, 0)], 0.0)
        pyp = pltpu.roll(pc, YE - 1, 0)
        pym = pltpu.roll(pc, 1, 0)
        pzp = pltpu.roll(pc, L - 1, 1)
        pzm = pltpu.roll(pc, 1, 1)
        t_xp = conductance(pc, pxp)
        t_xm = conductance(pc, pxm)
        t_yp = conductance(pc, pyp)
        t_ym = conductance(pc, pym)
        t_zp = jnp.where(lane == L - 1, 0.0, conductance(pc, pzp))
        t_zm = jnp.where(lane == 0, 0.0, conductance(pc, pzm))
        diag = t_xp + t_xm + t_yp + t_ym + t_zp + t_zm
        aux[0, x] = diag
        aux[1, x] = 1.0 / jnp.where(diag > 0.0, diag, 1.0)
        cx_hi = xplace(x) == CB - 1
        cx_lo = xplace(x) == 0
        tt[0, x] = t_xp
        tt[1, x] = jnp.where(cx_hi, 0.0, t_xp)
        tt[2, x] = t_xm
        tt[3, x] = jnp.where(cx_lo, 0.0, t_xm)
        tt[4, x] = t_yp
        tt[5, x] = jnp.where(m_yhi, 0.0, t_yp)
        tt[6, x] = t_ym
        tt[7, x] = jnp.where(m_ylo, 0.0, t_ym)
        tt[8, x] = t_zp
        tt[9, x] = jnp.where(m_zhi, 0.0, t_zp)
        tt[10, x] = t_zm
        tt[11, x] = jnp.where(m_zlo, 0.0, t_zm)
        sup = es[x]
        node_x = gi + ((x + (CB - HX)) >> 4) < nx
        for s in range(8):
            bx, by, bz = corner_of(s)
            keep = ((sup >> s) & 1) > 0
            if bx:
                keep = keep & node_x
            if by:
                keep = keep & node_y
            if bz:
                keep = keep & node_z
            v = jnp.where(keep, 1.0, 0.0)
            valid[s, x] = v
            wa[s, x] = eb[s, x] * v
        return carry

    lax.fori_loop(0, XE, pre, 0)

    def inflow_of(src, x, s, c):
        bx, by, bz = corner_of(s)
        cx_hi = xplace(x) == CB - 1
        cx_lo = xplace(x) == 0
        if bx:
            xp = src[jnp.where(cx_hi, s ^ 4, s), x + 1]
            t1 = tt[0, x]
            xm = src[s, x - 1]
            t2 = tt[3, x]
        else:
            xp = src[s, x + 1]
            t1 = tt[1, x]
            xm = src[jnp.where(cx_lo, s ^ 4, s), x - 1]
            t2 = tt[2, x]
        if by:
            yp = pltpu.roll(jnp.where(m_ylo, src[s ^ 2, x], c), YE - 1, 0)
            t3 = tt[4, x]
            ym = pltpu.roll(c, 1, 0)
            t4 = tt[7, x]
        else:
            yp = pltpu.roll(c, YE - 1, 0)
            t3 = tt[5, x]
            ym = pltpu.roll(jnp.where(m_yhi, src[s ^ 2, x], c), 1, 0)
            t4 = tt[6, x]
        if bz:
            zp = pltpu.roll(jnp.where(m_zlo, src[s ^ 1, x], c), L - 1, 1)
            t5 = tt[8, x]
            zm = pltpu.roll(c, 1, 1)
            t6 = tt[11, x]
        else:
            zp = pltpu.roll(c, L - 1, 1)
            t5 = tt[9, x]
            zm = pltpu.roll(jnp.where(m_zhi, src[s ^ 1, x], c), 1, 1)
            t6 = tt[10, x]
        return t1 * xp + t2 * xm + t3 * yp + t4 * ym + t5 * zp + t6 * zm

    def sweep(src, dst, lo, hi):
        def body(x, carry):
            diag = aux[0, x]
            inv = aux[1, x]
            for s in range(8):
                c = src[s, x]
                inflow = inflow_of(src, x, s, c)
                dst[s, x] = (c - omega_jacobi * (diag * c - inflow) * inv) * valid[s, x]
            return carry

        lax.fori_loop(lo, hi, body, 0)

    bufs = (wa, wb)
    for step in range(ITERS):
        sweep(bufs[step % 2], bufs[(step + 1) % 2], step + 1, XE - step - 1)
    last = bufs[ITERS % 2]
    basis_buf = bufs[(ITERS + 1) % 2]

    def normalize(x, carry):
        vals = [last[s, x] for s in range(8)]
        total = vals[0]
        for s in range(1, 8):
            total = total + vals[s]
        scale = jnp.maximum(total, renorm_floor)
        for s in range(8):
            basis_buf[s, x] = vals[s] / scale
        return carry

    lax.fori_loop(ITERS, XE - ITERS, normalize, 0)

    def image(x, carry):
        diag = aux[0, x]
        for s in range(8):
            c = basis_buf[s, x]
            inflow = inflow_of(basis_buf, x, s, c)
            img[s, x - HX] = jnp.where(m_rows, diag * c - inflow, 0.0)
            basis_ref[s, x - HX] = c[:NYL, :]
        return carry

    lax.fori_loop(HX, HX + NXL, image, 0)

    for s1 in range(8):
        def pair_sums(x, acc):
            b = basis_buf[s1, x + HX]
            return tuple(acc[s2] + b * img[s2, x] for s2 in range(8))

        acc = lax.fori_loop(
            0, NXL, pair_sums, tuple(jnp.zeros((YE, L), jnp.float32) for _ in range(8))
        )
        for s2 in range(8):
            prod_ref[pl.ds(s1 * 8 + s2, 1), :] = jnp.sum(acc[s2], axis=0, keepdims=True)

    nbz = L // CB
    node = lax.broadcasted_iota(jnp.int32, (nbz, L), 0)
    block = lax.broadcasted_iota(jnp.int32, (nbz, L), 1) >> 4
    same_node = jnp.where(block == node, 1.0, 0.0)
    node_above = jnp.where(block + 1 == node, 1.0, 0.0)
    pairs = prod_ref[...]
    along_lanes = (((1,), (1,)), ((), ()))
    exact = lax.Precision.HIGHEST
    low = lax.dot_general(same_node, pairs, along_lanes, precision=exact,
                          preferred_element_type=jnp.float32)
    high = lax.dot_general(node_above, pairs, along_lanes, precision=exact,
                           preferred_element_type=jnp.float32)
    for c in range(4):
        terms[c] = jnp.dot(low, placing[c, 0], precision=exact,
                           preferred_element_type=jnp.float32) + jnp.dot(
            high, placing[c, 1], precision=exact, preferred_element_type=jnp.float32)

    def coarse_copy(k, c, target_x, target_y):
        return pltpu.make_async_remote_copy(
            src_ref=terms.at[c],
            dst_ref=received.at[k],
            send_sem=coarse_send.at[k],
            recv_sem=coarse_recv.at[k],
            device_id=(target_x, target_y),
            device_id_type=mesh_id,
        )

    for k, (c, dx, dy) in enumerate(coarse_routes):
        @pl.when(has_device(gi + dx, gj + dy))
        def _():
            coarse_copy(k, c, gi + dx, gj + dy).start()

    for k, (c, dx, dy) in enumerate(coarse_routes):
        @pl.when(has_device(gi + dx, gj + dy))
        def _():
            coarse_copy(k, c, gi + dx, gj + dy).wait_send()

        @pl.when(has_device(gi - dx, gj - dy))
        def _():
            coarse_copy(k, c, gi - dx, gj - dy).wait_recv()

    total = terms[0] + received[0] + received[1] + received[2]
    coarse_ref[...] = total[:, : coarse_ref.shape[1]]


def placing_matrix():
    table = np.zeros((4, 2, 64, 32), np.float32)
    for first_slot in range(8):
        for second_slot in range(8):
            one_x, one_y, one_z = corner_of(first_slot)
            two_x, two_y, two_z = corner_of(second_slot)
            offset_index = 9 * (two_x - one_x + 1) + 3 * (two_y - one_y + 1) + (two_z - one_z + 1)
            table[one_x * 2 + one_y, one_z, first_slot * 8 + second_slot, offset_index] = 1.0
    return table


def shards(initial_basis, labels, class_perm, support):
    size_x, size_y, size_z = labels.shape
    assert size_x == CB and size_y == CB and size_z % CB == 0
    blocks_z = size_z // CB
    nx = lax.axis_size("gx")
    ny = lax.axis_size("gy")
    XE, YE = size_x + 2 * HX, size_y + 2 * HY
    f32 = jnp.float32
    vmem = pl.BlockSpec(memory_space=pltpu.VMEM)
    blocks_z = size_z // CB
    basis, coarse = pl.pallas_call(
        functools.partial(smooth_kernel, nx, ny),
        out_shape=(
            jax.ShapeDtypeStruct((8, size_x, size_y, size_z), f32),
            jax.ShapeDtypeStruct((blocks_z, 27), f32),
        ),
        in_specs=[vmem, vmem, pl.BlockSpec(memory_space=pltpu.SMEM), vmem, vmem],
        out_specs=(vmem, vmem),
        scratch_shapes=[
            pltpu.VMEM((8, XE, YE, size_z), f32),
            pltpu.VMEM((XE, YE, size_z), jnp.int32),
            pltpu.VMEM((XE, YE, size_z), jnp.int32),
            pltpu.VMEM((XE, YE, size_z), f32),
            pltpu.VMEM((12, XE, YE, size_z), f32),
            pltpu.VMEM((2, XE, YE, size_z), f32),
            pltpu.VMEM((8, XE, YE, size_z), f32),
            pltpu.VMEM((8, XE, YE, size_z), f32),
            pltpu.VMEM((8, XE, YE, size_z), f32),
            pltpu.VMEM((8, size_x, YE, size_z), f32),
            pltpu.VMEM((64, size_z), f32),
            pltpu.VMEM((4, blocks_z, 32), f32),
            pltpu.VMEM((3, blocks_z, 32), f32),
            pltpu.SemaphoreType.DMA((24,)),
            pltpu.SemaphoreType.DMA((24,)),
            pltpu.SemaphoreType.DMA((3,)),
            pltpu.SemaphoreType.DMA((3,)),
            pltpu.SemaphoreType.DMA((3,)),
        ],
        compiler_params=pltpu.CompilerParams(collective_id=1, has_side_effects=True),
    )(initial_basis, labels, class_perm, support, jnp.asarray(placing_matrix()))
    return (basis, coarse.T.reshape(27, 1, 1, blocks_z))


def solution(mesh):
    return jax.shard_map(
        shards,
        mesh=mesh,
        in_specs=(P(None, "gx", "gy", None), P("gx", "gy", None), P(), P("gx", "gy", None)),
        out_specs=(P(None, "gx", "gy", None), P(None, "gx", "gy", None)),
        check_vma=False,
    )
```

```python
import functools
import numpy as np
import jax
import jax.numpy as jnp
from jax import lax
from jax.experimental import pallas as pl
from jax.experimental.pallas import tpu as pltpu
from jax.sharding import PartitionSpec as P

CB = 16
ITERS = 3
HX = ITERS
HY = ITERS

omega_jacobi = 2.0 / 3.0
renorm_floor = 0.5


def with_halo(block, sides, width):
    for axis, dim in sides:
        count = lax.axis_size(axis)
        forward = [(i, i + 1) for i in range(count - 1)]
        backward = [(target, source) for source, target in forward]
        low = lax.ppermute(
            lax.slice_in_dim(block, block.shape[dim] - width, None, axis=dim), axis, forward
        )
        high = lax.ppermute(lax.slice_in_dim(block, 0, width, axis=dim), axis, backward)
        block = jnp.concatenate([low, block, high], axis=dim)
    return block


def from_behind(shard, axis, by):
    peers = lax.axis_size(axis)
    pairs = [(i, i + by) for i in range(peers) if 0 <= i + by < peers]
    return lax.ppermute(shard, axis, pairs)


def corner_of(slot_index):
    return (slot_index >> 2 & 1, slot_index >> 1 & 1, slot_index & 1)


def conductance(centre, neighbour):
    total_perm = centre + neighbour
    divisor = jnp.where(total_perm > 0.0, total_perm, 1.0)
    return 2.0 * centre * neighbour / divisor


def class_lookup(labels, class_perm):
    classes = jnp.arange(class_perm.shape[0])
    hits = labels[None] == classes[:, None, None, None]
    return jnp.sum(jnp.where(hits, class_perm[:, None, None, None], 0.0), axis=0)


def existing_bits(count_x, count_y, count_z, first_x, first_y, limit_x, limit_y, limit_z):
    block_x = (jnp.arange(count_x) + first_x) // CB
    block_y = (jnp.arange(count_y) + first_y) // CB
    block_z = jnp.arange(count_z) // CB
    bits = jnp.zeros((count_x, count_y, count_z), jnp.int32)
    for slot_index in range(8):
        corner_x, corner_y, corner_z = corner_of(slot_index)
        inside = (
            (block_x + corner_x < limit_x)[:, None, None]
            & (block_y + corner_y < limit_y)[None, :, None]
            & (block_z + corner_z < limit_z)[None, None, :]
        )
        bits = bits | jnp.where(inside, 1 << slot_index, 0)
    return bits


def halo_window(ref, xs, ys, slots=None):
    if len(ref.shape) == 4:
        return ref.at[slots if slots is not None else slice(None), xs, ys, :]
    return ref.at[xs, ys, :]


def halo_range(d, count, halo):
    if d > 0:
        return pl.ds(count - halo, halo), pl.ds(0, halo)
    if d < 0:
        return pl.ds(0, halo), pl.ds(halo + count, halo)
    return pl.ds(0, count), pl.ds(halo, count)


def halo_rows(d, count, halo, total):
    if d > 0:
        return pl.ds(count - halo, halo), pl.ds(total - halo, halo)
    if d < 0:
        return pl.ds(0, halo), pl.ds(count, halo)
    return pl.ds(0, count), pl.ds(0, count)


def slot_runs(slots):
    runs = []
    for s in sorted(slots):
        if runs and runs[-1][1] == s:
            runs[-1][1] = s + 1
        else:
            runs.append([s, s + 1])
    return [pl.ds(lo, hi - lo) for lo, hi in runs]


def shared_slots(dx, dy):
    keep = []
    for s in range(8):
        bx, by, _ = corner_of(s)
        if (dx > 0 and not bx) or (dx < 0 and bx) or (dy > 0 and not by) or (dy < 0 and by):
            continue
        keep.append(s)
    return keep


def smooth_kernel(
    nx, ny,
    basis_in, labels_in, class_perm, support_in, placing, basis_ref, coarse_ref,
    eb, el, es, pm, tt, aux, valid, wa, wb, wc, img, prod_ref, terms, received,
    send_sem, recv_sem, local_sem, coarse_send, coarse_recv, edge_send, edge_recv,
):
    gi = lax.axis_index("gx")
    gj = lax.axis_index("gy")
    _, XE, YE, L = eb.shape
    NXL = basis_ref.shape[1]
    NYL = basis_ref.shape[2]
    mesh_id = pl.DeviceIdType.MESH
    sources = (basis_in, labels_in, support_in)
    targets = (eb, el, es)
    local_copies = []
    for a in range(3):
        local_copy = pltpu.make_async_copy(
            sources[a], halo_window(targets[a], pl.ds(HX, NXL), pl.ds(0, NYL)), local_sem.at[a]
        )
        local_copy.start()
        local_copies.append(local_copy)

    directions = [(dx, dy) for dx in (-1, 0, 1) for dy in (-1, 0, 1) if (dx, dy) != (0, 0)]

    def has_device(x, y):
        return (x >= 0) & (x < nx) & (y >= 0) & (y < ny)

    def pieces(dx, dy):
        return [(0, run) for run in slot_runs(shared_slots(dx, dy))] + [(1, None), (2, None)]

    def edge_pieces(dx, dy):
        from_x = {1: pl.ds(HX + NXL - 1, 1), -1: pl.ds(HX, 1), 0: pl.ds(HX, NXL)}[dx]
        to_x = {1: pl.ds(HX - 1, 1), -1: pl.ds(HX + NXL, 1), 0: pl.ds(HX, NXL)}[dx]
        from_y = {1: pl.ds(NYL - 1, 1), -1: pl.ds(0, 1), 0: pl.ds(0, NYL)}[dy]
        to_y = {1: pl.ds(YE - 1, 1), -1: pl.ds(NYL, 1), 0: pl.ds(0, NYL)}[dy]
        return [(run, from_x, to_x, from_y, to_y) for run in slot_runs(shared_slots(dx, dy))]

    faces = ((1, 0), (-1, 0), (0, 1), (0, -1))
    peers = jnp.int32(0)
    for dx, dy in directions:
        _, to_x = halo_range(dx, NXL, HX)
        _, to_y = halo_rows(dy, NYL, HY, YE)
        from_here = has_device(gi - dx, gj - dy)
        peers = peers + from_here.astype(jnp.int32)
        unshared = [s for s in range(8) if s not in shared_slots(dx, dy)]
        for run in slot_runs(unshared):
            window = halo_window(eb, to_x, to_y, run)
            window[...] = jnp.zeros(window.shape, window.dtype)

        @pl.when(jnp.logical_not(from_here))
        def _():
            for a in range(3):
                window = halo_window(targets[a], to_x, to_y)
                window[...] = jnp.zeros(window.shape, window.dtype)

    if NYL + HY < YE - HY:
        junction = pl.ds(NYL + HY, YE - 2 * HY - NYL)
        for a in range(3):
            window = halo_window(targets[a], pl.ds(0, XE), junction)
            window[...] = jnp.zeros(window.shape, window.dtype)
    window = wc.at[:, pl.ds(HX, NXL), pl.ds(NYL, YE - NYL), :]
    window[...] = jnp.zeros(window.shape, window.dtype)
    for dx, dy in faces:
        @pl.when(jnp.logical_not(has_device(gi - dx, gj - dy)))
        def _():
            for run, _, to_x, _, to_y in edge_pieces(dx, dy):
                window = wc.at[run, to_x, to_y, :]
                window[...] = jnp.zeros(window.shape, window.dtype)

    coarse_routes = ((2, 1, 0), (1, 0, 1), (3, 1, 1))
    for k, (_, dx, dy) in enumerate(coarse_routes):
        @pl.when(jnp.logical_not(has_device(gi - dx, gj - dy)))
        def _():
            received[k] = jnp.zeros(received.shape[1:], received.dtype)

    barrier = pltpu.get_barrier_semaphore()
    for dx, dy in directions:
        @pl.when(has_device(gi + dx, gj + dy))
        def _():
            pl.semaphore_signal(barrier, 1, device_id=(gi + dx, gj + dy), device_id_type=mesh_id)

    pl.semaphore_wait(barrier, peers)

    def remote_copy(k, p, dx, dy, target_x, target_y):
        from_x, to_x = halo_range(dx, NXL, HX)
        from_y, to_y = halo_rows(dy, NYL, HY, YE)
        a, run = pieces(dx, dy)[p]
        return pltpu.make_async_remote_copy(
            src_ref=halo_window(sources[a], from_x, from_y, run),
            dst_ref=halo_window(targets[a], to_x, to_y, run),
            send_sem=send_sem.at[4 * k + p],
            recv_sem=recv_sem.at[4 * k + p],
            device_id=(target_x, target_y),
            device_id_type=mesh_id,
        )

    for k, (dx, dy) in enumerate(directions):
        @pl.when(has_device(gi + dx, gj + dy))
        def _():
            for p in range(len(pieces(dx, dy))):
                remote_copy(k, p, dx, dy, gi + dx, gj + dy).start()

    for local_copy in local_copies:
        local_copy.wait()
    for k, (dx, dy) in enumerate(directions):
        @pl.when(has_device(gi + dx, gj + dy))
        def _():
            for p in range(len(pieces(dx, dy))):
                remote_copy(k, p, dx, dy, gi + dx, gj + dy).wait_send()

        @pl.when(has_device(gi - dx, gj - dy))
        def _():
            for p in range(len(pieces(dx, dy))):
                remote_copy(k, p, dx, dy, gi - dx, gj - dy).wait_recv()

    row = lax.broadcasted_iota(jnp.int32, (YE, L), 0)
    lane = lax.broadcasted_iota(jnp.int32, (YE, L), 1)
    m_yhi = (row == NYL - 1) | (row == YE - 1)
    m_ylo = (row == 0) | (row == NYL)
    rz = lane & (CB - 1)
    m_zhi = rz == CB - 1
    m_zlo = rz == 0
    m_rows = row < NYL
    block_y = gj + jnp.where(row < NYL, 0, jnp.where(row < YE - HY, 1, -1))
    global_y = jnp.where(row < YE - HY, gj * NYL + row, gj * NYL + row - YE)
    inside_y = (global_y >= 0) & (global_y < ny * NYL)
    node_y = block_y + 1 < ny
    node_z = (lane >> 4) + 1 < L // CB

    def lookup(x, carry):
        labels = el[x]
        perm = jnp.zeros((YE, L), jnp.float32)
        for c in range(class_perm.shape[0]):
            perm = jnp.where(labels == c, class_perm[c], perm)
        global_x = gi * NXL + x - HX
        inside = inside_y & (global_x >= 0) & (global_x < nx * NXL)
        pm[x] = jnp.where(inside, perm, 0.0)
        return carry

    lax.fori_loop(0, XE, lookup, 0)

    def xplace(x):
        return (x + (CB - HX)) & (CB - 1)

    def pre(x, carry):
        pc = pm[x]
        pxp = jnp.where(x + 1 < XE, pm[jnp.minimum(x + 1, XE - 1)], 0.0)
        pxm = jnp.where(x >= 1, pm[jnp.maximum(x - 1, 0)], 0.0)
        pyp = pltpu.roll(pc, YE - 1, 0)
        pym = pltpu.roll(pc, 1, 0)
        pzp = pltpu.roll(pc, L - 1, 1)
        pzm = pltpu.roll(pc, 1, 1)
        t_xp = conductance(pc, pxp)
        t_xm = conductance(pc, pxm)
        t_yp = conductance(pc, pyp)
        t_ym = conductance(pc, pym)
        t_zp = jnp.where(lane == L - 1, 0.0, conductance(pc, pzp))
        t_zm = jnp.where(lane == 0, 0.0, conductance(pc, pzm))
        diag = t_xp + t_xm + t_yp + t_ym + t_zp + t_zm
        aux[0, x] = diag
        aux[1, x] = 1.0 / jnp.where(diag > 0.0, diag, 1.0)
        cx_hi = xplace(x) == CB - 1
        cx_lo = xplace(x) == 0
        tt[0, x] = t_xp
        tt[1, x] = jnp.where(cx_hi, 0.0, t_xp)
        tt[2, x] = t_xm
        tt[3, x] = jnp.where(cx_lo, 0.0, t_xm)
        tt[4, x] = t_yp
        tt[5, x] = jnp.where(m_yhi, 0.0, t_yp)
        tt[6, x] = t_ym
        tt[7, x] = jnp.where(m_ylo, 0.0, t_ym)
        tt[8, x] = t_zp
        tt[9, x] = jnp.where(m_zhi, 0.0, t_zp)
        tt[10, x] = t_zm
        tt[11, x] = jnp.where(m_zlo, 0.0, t_zm)
        sup = es[x]
        node_x = gi + ((x + (CB - HX)) >> 4) < nx
        for s in range(8):
            bx, by, bz = corner_of(s)
            keep = ((sup >> s) & 1) > 0
            if bx:
                keep = keep & node_x
            if by:
                keep = keep & node_y
            if bz:
                keep = keep & node_z
            v = jnp.where(keep, 1.0, 0.0)
            valid[s, x] = v
            wa[s, x] = eb[s, x] * v
        return carry

    lax.fori_loop(0, XE, pre, 0)

    def inflow_of(src, x, s, c):
        bx, by, bz = corner_of(s)
        cx_hi = xplace(x) == CB - 1
        cx_lo = xplace(x) == 0
        if bx:
            xp = src[jnp.where(cx_hi, s ^ 4, s), x + 1]
            t1 = tt[0, x]
            xm = src[s, x - 1]
            t2 = tt[3, x]
        else:
            xp = src[s, x + 1]
            t1 = tt[1, x]
            xm = src[jnp.where(cx_lo, s ^ 4, s), x - 1]
            t2 = tt[2, x]
        if by:
            yp = pltpu.roll(jnp.where(m_ylo, src[s ^ 2, x], c), YE - 1, 0)
            t3 = tt[4, x]
            ym = pltpu.roll(c, 1, 0)
            t4 = tt[7, x]
        else:
            yp = pltpu.roll(c, YE - 1, 0)
            t3 = tt[5, x]
            ym = pltpu.roll(jnp.where(m_yhi, src[s ^ 2, x], c), 1, 0)
            t4 = tt[6, x]
        if bz:
            zp = pltpu.roll(jnp.where(m_zlo, src[s ^ 1, x], c), L - 1, 1)
            t5 = tt[8, x]
            zm = pltpu.roll(c, 1, 1)
            t6 = tt[11, x]
        else:
            zp = pltpu.roll(c, L - 1, 1)
            t5 = tt[9, x]
            zm = pltpu.roll(jnp.where(m_zhi, src[s ^ 1, x], c), 1, 1)
            t6 = tt[10, x]
        return t1 * xp + t2 * xm + t3 * yp + t4 * ym + t5 * zp + t6 * zm

    def sweep(src, dst, lo, hi):
        def body(x, carry):
            diag = aux[0, x]
            inv = aux[1, x]
            for s in range(8):
                c = src[s, x]
                inflow = inflow_of(src, x, s, c)
                dst[s, x] = (c - omega_jacobi * (diag * c - inflow) * inv) * valid[s, x]
            return carry

        lax.fori_loop(lo, hi, body, 0)

    bufs = (wa, wb)
    for step in range(ITERS):
        sweep(bufs[step % 2], bufs[(step + 1) % 2], step + 1, XE - step - 1)
    last = bufs[ITERS % 2]
    basis_buf = wc

    def normalize(x, carry):
        vals = [last[s, x] for s in range(8)]
        total = vals[0]
        for s in range(1, 8):
            total = total + vals[s]
        scale = jnp.maximum(total, renorm_floor)
        for s in range(8):
            basis_buf[s, x, pl.ds(0, NYL), :] = (vals[s] / scale)[:NYL, :]
        return carry

    lax.fori_loop(HX, HX + NXL, normalize, 0)

    def edge_copy(k, p, dx, dy, target_x, target_y):
        run, from_x, to_x, from_y, to_y = edge_pieces(dx, dy)[p]
        return pltpu.make_async_remote_copy(
            src_ref=wc.at[run, from_x, from_y, :],
            dst_ref=wc.at[run, to_x, to_y, :],
            send_sem=edge_send.at[2 * k + p],
            recv_sem=edge_recv.at[2 * k + p],
            device_id=(target_x, target_y),
            device_id_type=mesh_id,
        )

    for k, (dx, dy) in enumerate(faces):
        @pl.when(has_device(gi + dx, gj + dy))
        def _():
            for p in range(len(edge_pieces(dx, dy))):
                edge_copy(k, p, dx, dy, gi + dx, gj + dy).start()

    for k, (dx, dy) in enumerate(faces):
        @pl.when(has_device(gi + dx, gj + dy))
        def _():
            for p in range(len(edge_pieces(dx, dy))):
                edge_copy(k, p, dx, dy, gi + dx, gj + dy).wait_send()

        @pl.when(has_device(gi - dx, gj - dy))
        def _():
            for p in range(len(edge_pieces(dx, dy))):
                edge_copy(k, p, dx, dy, gi - dx, gj - dy).wait_recv()

    def image(x, carry):
        diag = aux[0, x]
        for s in range(8):
            c = basis_buf[s, x]
            inflow = inflow_of(basis_buf, x, s, c)
            img[s, x - HX] = jnp.where(m_rows, diag * c - inflow, 0.0)
            basis_ref[s, x - HX] = c[:NYL, :]
        return carry

    lax.fori_loop(HX, HX + NXL, image, 0)

    for s1 in range(8):
        def pair_sums(x, acc):
            b = basis_buf[s1, x + HX]
            return tuple(acc[s2] + b * img[s2, x] for s2 in range(8))

        acc = lax.fori_loop(
            0, NXL, pair_sums, tuple(jnp.zeros((YE, L), jnp.float32) for _ in range(8))
        )
        for s2 in range(8):
            prod_ref[pl.ds(s1 * 8 + s2, 1), :] = jnp.sum(acc[s2], axis=0, keepdims=True)

    nbz = L // CB
    node = lax.broadcasted_iota(jnp.int32, (nbz, L), 0)
    block = lax.broadcasted_iota(jnp.int32, (nbz, L), 1) >> 4
    same_node = jnp.where(block == node, 1.0, 0.0)
    node_above = jnp.where(block + 1 == node, 1.0, 0.0)
    pairs = prod_ref[...]
    along_lanes = (((1,), (1,)), ((), ()))
    exact = lax.Precision.HIGHEST
    low = lax.dot_general(same_node, pairs, along_lanes, precision=exact,
                          preferred_element_type=jnp.float32)
    high = lax.dot_general(node_above, pairs, along_lanes, precision=exact,
                           preferred_element_type=jnp.float32)
    for c in range(4):
        terms[c] = jnp.dot(low, placing[c, 0], precision=exact,
                           preferred_element_type=jnp.float32) + jnp.dot(
            high, placing[c, 1], precision=exact, preferred_element_type=jnp.float32)

    def coarse_copy(k, c, target_x, target_y):
        return pltpu.make_async_remote_copy(
            src_ref=terms.at[c],
            dst_ref=received.at[k],
            send_sem=coarse_send.at[k],
            recv_sem=coarse_recv.at[k],
            device_id=(target_x, target_y),
            device_id_type=mesh_id,
        )

    for k, (c, dx, dy) in enumerate(coarse_routes):
        @pl.when(has_device(gi + dx, gj + dy))
        def _():
            coarse_copy(k, c, gi + dx, gj + dy).start()

    for k, (c, dx, dy) in enumerate(coarse_routes):
        @pl.when(has_device(gi + dx, gj + dy))
        def _():
            coarse_copy(k, c, gi + dx, gj + dy).wait_send()

        @pl.when(has_device(gi - dx, gj - dy))
        def _():
            coarse_copy(k, c, gi - dx, gj - dy).wait_recv()

    total = terms[0] + received[0] + received[1] + received[2]
    coarse_ref[...] = total[:, : coarse_ref.shape[1]]


def placing_matrix():
    table = np.zeros((4, 2, 64, 32), np.float32)
    for first_slot in range(8):
        for second_slot in range(8):
            one_x, one_y, one_z = corner_of(first_slot)
            two_x, two_y, two_z = corner_of(second_slot)
            offset_index = 9 * (two_x - one_x + 1) + 3 * (two_y - one_y + 1) + (two_z - one_z + 1)
            table[one_x * 2 + one_y, one_z, first_slot * 8 + second_slot, offset_index] = 1.0
    return table


def shards(initial_basis, labels, class_perm, support):
    size_x, size_y, size_z = labels.shape
    assert size_x == CB and size_y == CB and size_z % CB == 0
    blocks_z = size_z // CB
    nx = lax.axis_size("gx")
    ny = lax.axis_size("gy")
    XE = size_x + 2 * HX
    YE = -(-(size_y + 2 * HY) // 8) * 8
    f32 = jnp.float32
    vmem = pl.BlockSpec(memory_space=pltpu.VMEM)
    blocks_z = size_z // CB
    basis, coarse = pl.pallas_call(
        functools.partial(smooth_kernel, nx, ny),
        out_shape=(
            jax.ShapeDtypeStruct((8, size_x, size_y, size_z), f32),
            jax.ShapeDtypeStruct((blocks_z, 27), f32),
        ),
        in_specs=[vmem, vmem, pl.BlockSpec(memory_space=pltpu.SMEM), vmem, vmem],
        out_specs=(vmem, vmem),
        scratch_shapes=[
            pltpu.VMEM((8, XE, YE, size_z), f32),
            pltpu.VMEM((XE, YE, size_z), jnp.int32),
            pltpu.VMEM((XE, YE, size_z), jnp.int32),
            pltpu.VMEM((XE, YE, size_z), f32),
            pltpu.VMEM((12, XE, YE, size_z), f32),
            pltpu.VMEM((2, XE, YE, size_z), f32),
            pltpu.VMEM((8, XE, YE, size_z), f32),
            pltpu.VMEM((8, XE, YE, size_z), f32),
            pltpu.VMEM((8, XE, YE, size_z), f32),
            pltpu.VMEM((8, XE, YE, size_z), f32),
            pltpu.VMEM((8, size_x, YE, size_z), f32),
            pltpu.VMEM((64, size_z), f32),
            pltpu.VMEM((4, blocks_z, 32), f32),
            pltpu.VMEM((3, blocks_z, 32), f32),
            pltpu.SemaphoreType.DMA((32,)),
            pltpu.SemaphoreType.DMA((32,)),
            pltpu.SemaphoreType.DMA((3,)),
            pltpu.SemaphoreType.DMA((3,)),
            pltpu.SemaphoreType.DMA((3,)),
            pltpu.SemaphoreType.DMA((8,)),
            pltpu.SemaphoreType.DMA((8,)),
        ],
        compiler_params=pltpu.CompilerParams(collective_id=1, has_side_effects=True),
    )(initial_basis, labels, class_perm, support, jnp.asarray(placing_matrix()))
    return (basis, coarse.T.reshape(27, 1, 1, blocks_z))


def solution(mesh):
    return jax.shard_map(
        shards,
        mesh=mesh,
        in_specs=(P(None, "gx", "gy", None), P("gx", "gy", None), P(), P("gx", "gy", None)),
        out_specs=(P(None, "gx", "gy", None), P(None, "gx", "gy", None)),
        check_vma=False,
    )
```

```python
import functools
import numpy as np
import jax
import jax.numpy as jnp
from jax import lax
from jax.experimental import pallas as pl
from jax.experimental.pallas import tpu as pltpu
from jax.sharding import PartitionSpec as P

CB = 16
ITERS = 3
HX = ITERS
HY = ITERS

omega_jacobi = 2.0 / 3.0
renorm_floor = 0.5


def with_halo(block, sides, width):
    for axis, dim in sides:
        count = lax.axis_size(axis)
        forward = [(i, i + 1) for i in range(count - 1)]
        backward = [(target, source) for source, target in forward]
        low = lax.ppermute(
            lax.slice_in_dim(block, block.shape[dim] - width, None, axis=dim), axis, forward
        )
        high = lax.ppermute(lax.slice_in_dim(block, 0, width, axis=dim), axis, backward)
        block = jnp.concatenate([low, block, high], axis=dim)
    return block


def from_behind(shard, axis, by):
    peers = lax.axis_size(axis)
    pairs = [(i, i + by) for i in range(peers) if 0 <= i + by < peers]
    return lax.ppermute(shard, axis, pairs)


def corner_of(slot_index):
    return (slot_index >> 2 & 1, slot_index >> 1 & 1, slot_index & 1)


def conductance(centre, neighbour):
    total_perm = centre + neighbour
    divisor = jnp.where(total_perm > 0.0, total_perm, 1.0)
    return 2.0 * centre * neighbour / divisor


def class_lookup(labels, class_perm):
    classes = jnp.arange(class_perm.shape[0])
    hits = labels[None] == classes[:, None, None, None]
    return jnp.sum(jnp.where(hits, class_perm[:, None, None, None], 0.0), axis=0)


def existing_bits(count_x, count_y, count_z, first_x, first_y, limit_x, limit_y, limit_z):
    block_x = (jnp.arange(count_x) + first_x) // CB
    block_y = (jnp.arange(count_y) + first_y) // CB
    block_z = jnp.arange(count_z) // CB
    bits = jnp.zeros((count_x, count_y, count_z), jnp.int32)
    for slot_index in range(8):
        corner_x, corner_y, corner_z = corner_of(slot_index)
        inside = (
            (block_x + corner_x < limit_x)[:, None, None]
            & (block_y + corner_y < limit_y)[None, :, None]
            & (block_z + corner_z < limit_z)[None, None, :]
        )
        bits = bits | jnp.where(inside, 1 << slot_index, 0)
    return bits


def halo_window(ref, xs, ys, slots=None):
    if len(ref.shape) == 4:
        return ref.at[slots if slots is not None else slice(None), xs, ys, :]
    return ref.at[xs, ys, :]


def halo_range(d, count, halo):
    if d > 0:
        return pl.ds(count - halo, halo), pl.ds(0, halo)
    if d < 0:
        return pl.ds(0, halo), pl.ds(halo + count, halo)
    return pl.ds(0, count), pl.ds(halo, count)


def halo_rows(d, count, halo, total):
    if d > 0:
        return pl.ds(count - halo, halo), pl.ds(total - halo, halo)
    if d < 0:
        return pl.ds(0, halo), pl.ds(count, halo)
    return pl.ds(0, count), pl.ds(0, count)


def slot_runs(slots):
    runs = []
    for s in sorted(slots):
        if runs and runs[-1][1] == s:
            runs[-1][1] = s + 1
        else:
            runs.append([s, s + 1])
    return [pl.ds(lo, hi - lo) for lo, hi in runs]


def shared_slots(dx, dy):
    keep = []
    for s in range(8):
        bx, by, _ = corner_of(s)
        if (dx > 0 and not bx) or (dx < 0 and bx) or (dy > 0 and not by) or (dy < 0 and by):
            continue
        keep.append(s)
    return keep


def smooth_kernel(
    nx, ny,
    basis_in, labels_in, class_perm, support_in, placing, basis_ref, coarse_ref,
    eb, el, es, pm, tt, aux, valid, wa, wb, wc, img, prod_ref, terms, received,
    send_sem, recv_sem, local_sem, coarse_send, coarse_recv, edge_send, edge_recv,
):
    gi = lax.axis_index("gx")
    gj = lax.axis_index("gy")
    _, XE, YE, L = eb.shape
    NXL = basis_ref.shape[1]
    NYL = basis_ref.shape[2]
    mesh_id = pl.DeviceIdType.MESH
    sources = (basis_in, labels_in, support_in)
    targets = (eb, el, es)
    local_copies = []
    for a in range(3):
        local_copy = pltpu.make_async_copy(
            sources[a], halo_window(targets[a], pl.ds(HX, NXL), pl.ds(0, NYL)), local_sem.at[a]
        )
        local_copy.start()
        local_copies.append(local_copy)

    directions = [(dx, dy) for dx in (-1, 0, 1) for dy in (-1, 0, 1) if (dx, dy) != (0, 0)]

    def has_device(x, y):
        return (x >= 0) & (x < nx) & (y >= 0) & (y < ny)

    barrier = pltpu.get_barrier_semaphore()
    for dx, dy in directions:
        @pl.when(has_device(gi + dx, gj + dy))
        def _():
            pl.semaphore_signal(barrier, 1, device_id=(gi + dx, gj + dy), device_id_type=mesh_id)

    def pieces(dx, dy):
        return [(0, run) for run in slot_runs(shared_slots(dx, dy))] + [(1, None), (2, None)]

    def edge_pieces(dx, dy):
        from_x = {1: pl.ds(HX + NXL - 1, 1), -1: pl.ds(HX, 1), 0: pl.ds(HX, NXL)}[dx]
        to_x = {1: pl.ds(HX - 1, 1), -1: pl.ds(HX + NXL, 1), 0: pl.ds(HX, NXL)}[dx]
        from_y = {1: pl.ds(NYL - 1, 1), -1: pl.ds(0, 1), 0: pl.ds(0, NYL)}[dy]
        to_y = {1: pl.ds(YE - 1, 1), -1: pl.ds(NYL, 1), 0: pl.ds(0, NYL)}[dy]
        return [(run, from_x, to_x, from_y, to_y) for run in slot_runs(shared_slots(dx, dy))]

    faces = ((1, 0), (-1, 0), (0, 1), (0, -1))
    peers = jnp.int32(0)
    for dx, dy in directions:
        _, to_x = halo_range(dx, NXL, HX)
        _, to_y = halo_rows(dy, NYL, HY, YE)
        from_here = has_device(gi - dx, gj - dy)
        peers = peers + from_here.astype(jnp.int32)
        unshared = [s for s in range(8) if s not in shared_slots(dx, dy)]
        for run in slot_runs(unshared):
            window = halo_window(eb, to_x, to_y, run)
            window[...] = jnp.zeros(window.shape, window.dtype)

        @pl.when(jnp.logical_not(from_here))
        def _():
            for a in range(3):
                window = halo_window(targets[a], to_x, to_y)
                window[...] = jnp.zeros(window.shape, window.dtype)

    if NYL + HY < YE - HY:
        junction = pl.ds(NYL + HY, YE - 2 * HY - NYL)
        for a in range(3):
            window = halo_window(targets[a], pl.ds(0, XE), junction)
            window[...] = jnp.zeros(window.shape, window.dtype)
    window = wc.at[:, pl.ds(HX, NXL), pl.ds(NYL, YE - NYL), :]
    window[...] = jnp.zeros(window.shape, window.dtype)
    for dx, dy in faces:
        @pl.when(jnp.logical_not(has_device(gi - dx, gj - dy)))
        def _():
            for run, _, to_x, _, to_y in edge_pieces(dx, dy):
                window = wc.at[run, to_x, to_y, :]
                window[...] = jnp.zeros(window.shape, window.dtype)

    coarse_routes = ((2, 1, 0), (1, 0, 1), (3, 1, 1))
    for k, (_, dx, dy) in enumerate(coarse_routes):
        @pl.when(jnp.logical_not(has_device(gi - dx, gj - dy)))
        def _():
            received[k] = jnp.zeros(received.shape[1:], received.dtype)

    pl.semaphore_wait(barrier, peers)

    def remote_copy(k, p, dx, dy, target_x, target_y):
        from_x, to_x = halo_range(dx, NXL, HX)
        from_y, to_y = halo_rows(dy, NYL, HY, YE)
        a, run = pieces(dx, dy)[p]
        return pltpu.make_async_remote_copy(
            src_ref=halo_window(sources[a], from_x, from_y, run),
            dst_ref=halo_window(targets[a], to_x, to_y, run),
            send_sem=send_sem.at[4 * k + p],
            recv_sem=recv_sem.at[4 * k + p],
            device_id=(target_x, target_y),
            device_id_type=mesh_id,
        )

    for k, (dx, dy) in enumerate(directions):
        @pl.when(has_device(gi + dx, gj + dy))
        def _():
            for p in range(len(pieces(dx, dy))):
                remote_copy(k, p, dx, dy, gi + dx, gj + dy).start()

    def wait_halo(chosen):
        for k, (dx, dy) in enumerate(directions):
            if not chosen(dx, dy):
                continue

            @pl.when(has_device(gi + dx, gj + dy))
            def _():
                for p in range(len(pieces(dx, dy))):
                    remote_copy(k, p, dx, dy, gi + dx, gj + dy).wait_send()

            @pl.when(has_device(gi - dx, gj - dy))
            def _():
                for p in range(len(pieces(dx, dy))):
                    remote_copy(k, p, dx, dy, gi - dx, gj - dy).wait_recv()

    row = lax.broadcasted_iota(jnp.int32, (YE, L), 0)
    lane = lax.broadcasted_iota(jnp.int32, (YE, L), 1)
    m_yhi = (row == NYL - 1) | (row == YE - 1)
    m_ylo = (row == 0) | (row == NYL)
    rz = lane & (CB - 1)
    m_zhi = rz == CB - 1
    m_zlo = rz == 0
    m_rows = row < NYL
    block_y = gj + jnp.where(row < NYL, 0, jnp.where(row < YE - HY, 1, -1))
    global_y = jnp.where(row < YE - HY, gj * NYL + row, gj * NYL + row - YE)
    inside_y = (global_y >= 0) & (global_y < ny * NYL)
    node_y = block_y + 1 < ny
    node_z = (lane >> 4) + 1 < L // CB

    def lookup(x, carry):
        labels = el[x]
        perm = jnp.zeros((YE, L), jnp.float32)
        for c in range(class_perm.shape[0]):
            perm = jnp.where(labels == c, class_perm[c], perm)
        global_x = gi * NXL + x - HX
        inside = inside_y & (global_x >= 0) & (global_x < nx * NXL)
        pm[x] = jnp.where(inside, perm, 0.0)
        return carry

    for local_copy in local_copies:
        local_copy.wait()
    wait_halo(lambda dx, dy: dx == 0)
    lax.fori_loop(HX, HX + NXL, lookup, 0)

    def xplace(x):
        return (x + (CB - HX)) & (CB - 1)

    def pre(x, carry):
        pc = pm[x]
        pxp = jnp.where(x + 1 < XE, pm[jnp.minimum(x + 1, XE - 1)], 0.0)
        pxm = jnp.where(x >= 1, pm[jnp.maximum(x - 1, 0)], 0.0)
        pyp = pltpu.roll(pc, YE - 1, 0)
        pym = pltpu.roll(pc, 1, 0)
        pzp = pltpu.roll(pc, L - 1, 1)
        pzm = pltpu.roll(pc, 1, 1)
        t_xp = conductance(pc, pxp)
        t_xm = conductance(pc, pxm)
        t_yp = conductance(pc, pyp)
        t_ym = conductance(pc, pym)
        t_zp = jnp.where(lane == L - 1, 0.0, conductance(pc, pzp))
        t_zm = jnp.where(lane == 0, 0.0, conductance(pc, pzm))
        diag = t_xp + t_xm + t_yp + t_ym + t_zp + t_zm
        aux[0, x] = diag
        aux[1, x] = 1.0 / jnp.where(diag > 0.0, diag, 1.0)
        cx_hi = xplace(x) == CB - 1
        cx_lo = xplace(x) == 0
        tt[0, x] = t_xp
        tt[1, x] = jnp.where(cx_hi, 0.0, t_xp)
        tt[2, x] = t_xm
        tt[3, x] = jnp.where(cx_lo, 0.0, t_xm)
        tt[4, x] = t_yp
        tt[5, x] = jnp.where(m_yhi, 0.0, t_yp)
        tt[6, x] = t_ym
        tt[7, x] = jnp.where(m_ylo, 0.0, t_ym)
        tt[8, x] = t_zp
        tt[9, x] = jnp.where(m_zhi, 0.0, t_zp)
        tt[10, x] = t_zm
        tt[11, x] = jnp.where(m_zlo, 0.0, t_zm)
        sup = es[x]
        node_x = gi + ((x + (CB - HX)) >> 4) < nx
        for s in range(8):
            bx, by, bz = corner_of(s)
            keep = ((sup >> s) & 1) > 0
            if bx:
                keep = keep & node_x
            if by:
                keep = keep & node_y
            if bz:
                keep = keep & node_z
            v = jnp.where(keep, 1.0, 0.0)
            valid[s, x] = v
            wa[s, x] = eb[s, x] * v
        return carry

    lax.fori_loop(HX + 1, HX + NXL - 1, pre, 0)
    wait_halo(lambda dx, dy: dx != 0)
    lax.fori_loop(0, HX, lookup, 0)
    lax.fori_loop(HX + NXL, XE, lookup, 0)
    lax.fori_loop(0, HX + 1, pre, 0)
    lax.fori_loop(HX + NXL - 1, XE, pre, 0)

    def inflow_of(src, x, s, c):
        bx, by, bz = corner_of(s)
        cx_hi = xplace(x) == CB - 1
        cx_lo = xplace(x) == 0
        if bx:
            xp = src[jnp.where(cx_hi, s ^ 4, s), x + 1]
            t1 = tt[0, x]
            xm = src[s, x - 1]
            t2 = tt[3, x]
        else:
            xp = src[s, x + 1]
            t1 = tt[1, x]
            xm = src[jnp.where(cx_lo, s ^ 4, s), x - 1]
            t2 = tt[2, x]
        if by:
            yp = pltpu.roll(jnp.where(m_ylo, src[s ^ 2, x], c), YE - 1, 0)
            t3 = tt[4, x]
            ym = pltpu.roll(c, 1, 0)
            t4 = tt[7, x]
        else:
            yp = pltpu.roll(c, YE - 1, 0)
            t3 = tt[5, x]
            ym = pltpu.roll(jnp.where(m_yhi, src[s ^ 2, x], c), 1, 0)
            t4 = tt[6, x]
        if bz:
            zp = pltpu.roll(jnp.where(m_zlo, src[s ^ 1, x], c), L - 1, 1)
            t5 = tt[8, x]
            zm = pltpu.roll(c, 1, 1)
            t6 = tt[11, x]
        else:
            zp = pltpu.roll(c, L - 1, 1)
            t5 = tt[9, x]
            zm = pltpu.roll(jnp.where(m_zhi, src[s ^ 1, x], c), 1, 1)
            t6 = tt[10, x]
        return t1 * xp + t2 * xm + t3 * yp + t4 * ym + t5 * zp + t6 * zm

    def sweep(src, dst, lo, hi):
        def body(x, carry):
            diag = aux[0, x]
            inv = aux[1, x]
            for s in range(8):
                c = src[s, x]
                inflow = inflow_of(src, x, s, c)
                dst[s, x] = (c - omega_jacobi * (diag * c - inflow) * inv) * valid[s, x]
            return carry

        lax.fori_loop(lo, hi, body, 0)

    bufs = (wa, wb)
    for step in range(ITERS):
        sweep(bufs[step % 2], bufs[(step + 1) % 2], step + 1, XE - step - 1)
    last = bufs[ITERS % 2]
    basis_buf = wc

    def normalize(x, carry):
        vals = [last[s, x] for s in range(8)]
        total = vals[0]
        for s in range(1, 8):
            total = total + vals[s]
        scale = jnp.maximum(total, renorm_floor)
        for s in range(8):
            basis_buf[s, x, pl.ds(0, NYL), :] = (vals[s] / scale)[:NYL, :]
        return carry

    lax.fori_loop(HX, HX + NXL, normalize, 0)

    def edge_copy(k, p, dx, dy, target_x, target_y):
        run, from_x, to_x, from_y, to_y = edge_pieces(dx, dy)[p]
        return pltpu.make_async_remote_copy(
            src_ref=wc.at[run, from_x, from_y, :],
            dst_ref=wc.at[run, to_x, to_y, :],
            send_sem=edge_send.at[2 * k + p],
            recv_sem=edge_recv.at[2 * k + p],
            device_id=(target_x, target_y),
            device_id_type=mesh_id,
        )

    for k, (dx, dy) in enumerate(faces):
        @pl.when(has_device(gi + dx, gj + dy))
        def _():
            for p in range(len(edge_pieces(dx, dy))):
                edge_copy(k, p, dx, dy, gi + dx, gj + dy).start()

    for k, (dx, dy) in enumerate(faces):
        @pl.when(has_device(gi + dx, gj + dy))
        def _():
            for p in range(len(edge_pieces(dx, dy))):
                edge_copy(k, p, dx, dy, gi + dx, gj + dy).wait_send()

        @pl.when(has_device(gi - dx, gj - dy))
        def _():
            for p in range(len(edge_pieces(dx, dy))):
                edge_copy(k, p, dx, dy, gi - dx, gj - dy).wait_recv()

    def image(x, carry):
        diag = aux[0, x]
        for s in range(8):
            c = basis_buf[s, x]
            inflow = inflow_of(basis_buf, x, s, c)
            img[s, x - HX] = jnp.where(m_rows, diag * c - inflow, 0.0)
            basis_ref[s, x - HX] = c[:NYL, :]
        return carry

    lax.fori_loop(HX, HX + NXL, image, 0)

    for s1 in range(8):
        def pair_sums(x, acc):
            b = basis_buf[s1, x + HX]
            return tuple(acc[s2] + b * img[s2, x] for s2 in range(8))

        acc = lax.fori_loop(
            0, NXL, pair_sums, tuple(jnp.zeros((YE, L), jnp.float32) for _ in range(8))
        )
        for s2 in range(8):
            prod_ref[pl.ds(s1 * 8 + s2, 1), :] = jnp.sum(acc[s2], axis=0, keepdims=True)

    nbz = L // CB
    node = lax.broadcasted_iota(jnp.int32, (nbz, L), 0)
    block = lax.broadcasted_iota(jnp.int32, (nbz, L), 1) >> 4
    same_node = jnp.where(block == node, 1.0, 0.0)
    node_above = jnp.where(block + 1 == node, 1.0, 0.0)
    pairs = prod_ref[...]
    along_lanes = (((1,), (1,)), ((), ()))
    exact = lax.Precision.HIGHEST
    low = lax.dot_general(same_node, pairs, along_lanes, precision=exact,
                          preferred_element_type=jnp.float32)
    high = lax.dot_general(node_above, pairs, along_lanes, precision=exact,
                           preferred_element_type=jnp.float32)
    for c in range(4):
        terms[c] = jnp.dot(low, placing[c, 0], precision=exact,
                           preferred_element_type=jnp.float32) + jnp.dot(
            high, placing[c, 1], precision=exact, preferred_element_type=jnp.float32)

    def coarse_copy(k, c, target_x, target_y):
        return pltpu.make_async_remote_copy(
            src_ref=terms.at[c],
            dst_ref=received.at[k],
            send_sem=coarse_send.at[k],
            recv_sem=coarse_recv.at[k],
            device_id=(target_x, target_y),
            device_id_type=mesh_id,
        )

    for k, (c, dx, dy) in enumerate(coarse_routes):
        @pl.when(has_device(gi + dx, gj + dy))
        def _():
            coarse_copy(k, c, gi + dx, gj + dy).start()

    for k, (c, dx, dy) in enumerate(coarse_routes):
        @pl.when(has_device(gi + dx, gj + dy))
        def _():
            coarse_copy(k, c, gi + dx, gj + dy).wait_send()

        @pl.when(has_device(gi - dx, gj - dy))
        def _():
            coarse_copy(k, c, gi - dx, gj - dy).wait_recv()

    total = terms[0] + received[0] + received[1] + received[2]
    coarse_ref[...] = total[:, : coarse_ref.shape[1]]


def placing_matrix():
    table = np.zeros((4, 2, 64, 32), np.float32)
    for first_slot in range(8):
        for second_slot in range(8):
            one_x, one_y, one_z = corner_of(first_slot)
            two_x, two_y, two_z = corner_of(second_slot)
            offset_index = 9 * (two_x - one_x + 1) + 3 * (two_y - one_y + 1) + (two_z - one_z + 1)
            table[one_x * 2 + one_y, one_z, first_slot * 8 + second_slot, offset_index] = 1.0
    return table


def shards(initial_basis, labels, class_perm, support):
    size_x, size_y, size_z = labels.shape
    assert size_x == CB and size_y == CB and size_z % CB == 0
    blocks_z = size_z // CB
    nx = lax.axis_size("gx")
    ny = lax.axis_size("gy")
    XE = size_x + 2 * HX
    YE = -(-(size_y + 2 * HY) // 8) * 8
    f32 = jnp.float32
    vmem = pl.BlockSpec(memory_space=pltpu.VMEM)
    blocks_z = size_z // CB
    basis, coarse = pl.pallas_call(
        functools.partial(smooth_kernel, nx, ny),
        out_shape=(
            jax.ShapeDtypeStruct((8, size_x, size_y, size_z), f32),
            jax.ShapeDtypeStruct((blocks_z, 27), f32),
        ),
        in_specs=[vmem, vmem, pl.BlockSpec(memory_space=pltpu.SMEM), vmem, vmem],
        out_specs=(vmem, vmem),
        scratch_shapes=[
            pltpu.VMEM((8, XE, YE, size_z), f32),
            pltpu.VMEM((XE, YE, size_z), jnp.int32),
            pltpu.VMEM((XE, YE, size_z), jnp.int32),
            pltpu.VMEM((XE, YE, size_z), f32),
            pltpu.VMEM((12, XE, YE, size_z), f32),
            pltpu.VMEM((2, XE, YE, size_z), f32),
            pltpu.VMEM((8, XE, YE, size_z), f32),
            pltpu.VMEM((8, XE, YE, size_z), f32),
            pltpu.VMEM((8, XE, YE, size_z), f32),
            pltpu.VMEM((8, XE, YE, size_z), f32),
            pltpu.VMEM((8, size_x, YE, size_z), f32),
            pltpu.VMEM((64, size_z), f32),
            pltpu.VMEM((4, blocks_z, 32), f32),
            pltpu.VMEM((3, blocks_z, 32), f32),
            pltpu.SemaphoreType.DMA((32,)),
            pltpu.SemaphoreType.DMA((32,)),
            pltpu.SemaphoreType.DMA((3,)),
            pltpu.SemaphoreType.DMA((3,)),
            pltpu.SemaphoreType.DMA((3,)),
            pltpu.SemaphoreType.DMA((8,)),
            pltpu.SemaphoreType.DMA((8,)),
        ],
        compiler_params=pltpu.CompilerParams(collective_id=1, has_side_effects=True),
    )(initial_basis, labels, class_perm, support, jnp.asarray(placing_matrix()))
    return (basis, coarse.T.reshape(27, 1, 1, blocks_z))


def solution(mesh):
    return jax.shard_map(
        shards,
        mesh=mesh,
        in_specs=(P(None, "gx", "gy", None), P("gx", "gy", None), P(), P("gx", "gy", None)),
        out_specs=(P(None, "gx", "gy", None), P(None, "gx", "gy", None)),
        check_vma=False,
    )
```

```python
import functools
import numpy as np
import jax
import jax.numpy as jnp
from jax import lax
from jax.experimental import pallas as pl
from jax.experimental.pallas import tpu as pltpu
from jax.sharding import PartitionSpec as P

CB = 16
ITERS = 3
HX = ITERS
HY = ITERS

omega_jacobi = 2.0 / 3.0
renorm_floor = 0.5


def with_halo(block, sides, width):
    for axis, dim in sides:
        count = lax.axis_size(axis)
        forward = [(i, i + 1) for i in range(count - 1)]
        backward = [(target, source) for source, target in forward]
        low = lax.ppermute(
            lax.slice_in_dim(block, block.shape[dim] - width, None, axis=dim), axis, forward
        )
        high = lax.ppermute(lax.slice_in_dim(block, 0, width, axis=dim), axis, backward)
        block = jnp.concatenate([low, block, high], axis=dim)
    return block


def from_behind(shard, axis, by):
    peers = lax.axis_size(axis)
    pairs = [(i, i + by) for i in range(peers) if 0 <= i + by < peers]
    return lax.ppermute(shard, axis, pairs)


def corner_of(slot_index):
    return (slot_index >> 2 & 1, slot_index >> 1 & 1, slot_index & 1)


def conductance(centre, neighbour):
    total_perm = centre + neighbour
    divisor = jnp.where(total_perm > 0.0, total_perm, 1.0)
    return 2.0 * centre * neighbour / divisor


def class_lookup(labels, class_perm):
    classes = jnp.arange(class_perm.shape[0])
    hits = labels[None] == classes[:, None, None, None]
    return jnp.sum(jnp.where(hits, class_perm[:, None, None, None], 0.0), axis=0)


def existing_bits(count_x, count_y, count_z, first_x, first_y, limit_x, limit_y, limit_z):
    block_x = (jnp.arange(count_x) + first_x) // CB
    block_y = (jnp.arange(count_y) + first_y) // CB
    block_z = jnp.arange(count_z) // CB
    bits = jnp.zeros((count_x, count_y, count_z), jnp.int32)
    for slot_index in range(8):
        corner_x, corner_y, corner_z = corner_of(slot_index)
        inside = (
            (block_x + corner_x < limit_x)[:, None, None]
            & (block_y + corner_y < limit_y)[None, :, None]
            & (block_z + corner_z < limit_z)[None, None, :]
        )
        bits = bits | jnp.where(inside, 1 << slot_index, 0)
    return bits


def halo_window(ref, xs, ys, slots=None):
    if len(ref.shape) == 4:
        return ref.at[slots if slots is not None else slice(None), xs, ys, :]
    return ref.at[xs, ys, :]


def halo_range(d, count, halo):
    if d > 0:
        return pl.ds(count - halo, halo), pl.ds(0, halo)
    if d < 0:
        return pl.ds(0, halo), pl.ds(halo + count, halo)
    return pl.ds(0, count), pl.ds(halo, count)


def halo_rows(d, count, halo, total):
    if d > 0:
        return pl.ds(count - halo, halo), pl.ds(total - halo, halo)
    if d < 0:
        return pl.ds(0, halo), pl.ds(count, halo)
    return pl.ds(0, count), pl.ds(0, count)


def slot_runs(slots):
    runs = []
    for s in sorted(slots):
        if runs and runs[-1][1] == s:
            runs[-1][1] = s + 1
        else:
            runs.append([s, s + 1])
    return [pl.ds(lo, hi - lo) for lo, hi in runs]


def shared_slots(dx, dy):
    keep = []
    for s in range(8):
        bx, by, _ = corner_of(s)
        if (dx > 0 and not bx) or (dx < 0 and bx) or (dy > 0 and not by) or (dy < 0 and by):
            continue
        keep.append(s)
    return keep


def smooth_kernel(
    nx, ny,
    basis_in, labels_in, class_perm, support_in, placing, basis_ref, coarse_ref,
    eb, el, es, pm, tt, aux, valid, wa, wb, wc, img, prod_ref, terms, received,
    send_sem, recv_sem, local_sem, coarse_send, coarse_recv, edge_send, edge_recv,
):
    gi = lax.axis_index("gx")
    gj = lax.axis_index("gy")
    _, XE, YE, L = eb.shape
    NXL = basis_ref.shape[1]
    NYL = basis_ref.shape[2]
    mesh_id = pl.DeviceIdType.MESH
    sources = (basis_in, labels_in, support_in)
    targets = (eb, el, es)
    local_copies = []
    for a in range(3):
        local_copy = pltpu.make_async_copy(
            sources[a], halo_window(targets[a], pl.ds(HX, NXL), pl.ds(0, NYL)), local_sem.at[a]
        )
        local_copy.start()
        local_copies.append(local_copy)

    directions = [(dx, dy) for dx in (-1, 0, 1) for dy in (-1, 0, 1) if (dx, dy) != (0, 0)]

    def has_device(x, y):
        return (x >= 0) & (x < nx) & (y >= 0) & (y < ny)

    barrier = pltpu.get_barrier_semaphore()
    for dx, dy in directions:
        @pl.when(has_device(gi + dx, gj + dy))
        def _():
            pl.semaphore_signal(barrier, 1, device_id=(gi + dx, gj + dy), device_id_type=mesh_id)

    def pieces(dx, dy):
        return [(0, run) for run in slot_runs(shared_slots(dx, dy))] + [(1, None), (2, None)]

    def edge_pieces(dx, dy):
        from_x = {1: pl.ds(HX + NXL - 1, 1), -1: pl.ds(HX, 1), 0: pl.ds(HX, NXL)}[dx]
        to_x = {1: pl.ds(HX - 1, 1), -1: pl.ds(HX + NXL, 1), 0: pl.ds(HX, NXL)}[dx]
        from_y = {1: pl.ds(NYL - 1, 1), -1: pl.ds(0, 1), 0: pl.ds(0, NYL)}[dy]
        to_y = {1: pl.ds(YE - 1, 1), -1: pl.ds(NYL, 1), 0: pl.ds(0, NYL)}[dy]
        return [(run, from_x, to_x, from_y, to_y) for run in slot_runs(shared_slots(dx, dy))]

    faces = ((1, 0), (-1, 0), (0, 1), (0, -1))
    peers = jnp.int32(0)
    for dx, dy in directions:
        _, to_x = halo_range(dx, NXL, HX)
        _, to_y = halo_rows(dy, NYL, HY, YE)
        from_here = has_device(gi - dx, gj - dy)
        peers = peers + from_here.astype(jnp.int32)
        unshared = [s for s in range(8) if s not in shared_slots(dx, dy)]
        for run in slot_runs(unshared):
            window = halo_window(eb, to_x, to_y, run)
            window[...] = jnp.zeros(window.shape, window.dtype)

        @pl.when(jnp.logical_not(from_here))
        def _():
            for a in range(3):
                window = halo_window(targets[a], to_x, to_y)
                window[...] = jnp.zeros(window.shape, window.dtype)

    if NYL + HY < YE - HY:
        junction = pl.ds(NYL + HY, YE - 2 * HY - NYL)
        for a in range(3):
            window = halo_window(targets[a], pl.ds(0, XE), junction)
            window[...] = jnp.zeros(window.shape, window.dtype)
    window = wc.at[:, pl.ds(HX, NXL), pl.ds(NYL, YE - NYL), :]
    window[...] = jnp.zeros(window.shape, window.dtype)
    for dx, dy in faces:
        @pl.when(jnp.logical_not(has_device(gi - dx, gj - dy)))
        def _():
            for run, _, to_x, _, to_y in edge_pieces(dx, dy):
                window = wc.at[run, to_x, to_y, :]
                window[...] = jnp.zeros(window.shape, window.dtype)

    coarse_routes = ((2, 1, 0), (1, 0, 1), (3, 1, 1))
    for k, (_, dx, dy) in enumerate(coarse_routes):
        @pl.when(jnp.logical_not(has_device(gi - dx, gj - dy)))
        def _():
            received[k] = jnp.zeros(received.shape[1:], received.dtype)

    pl.semaphore_wait(barrier, peers)

    def remote_copy(k, p, dx, dy, target_x, target_y):
        from_x, to_x = halo_range(dx, NXL, HX)
        from_y, to_y = halo_rows(dy, NYL, HY, YE)
        a, run = pieces(dx, dy)[p]
        return pltpu.make_async_remote_copy(
            src_ref=halo_window(sources[a], from_x, from_y, run),
            dst_ref=halo_window(targets[a], to_x, to_y, run),
            send_sem=send_sem.at[4 * k + p],
            recv_sem=recv_sem.at[4 * k + p],
            device_id=(target_x, target_y),
            device_id_type=mesh_id,
        )

    for k, (dx, dy) in enumerate(directions):
        @pl.when(has_device(gi + dx, gj + dy))
        def _():
            for p in range(len(pieces(dx, dy))):
                remote_copy(k, p, dx, dy, gi + dx, gj + dy).start()

    def wait_halo(chosen):
        for k, (dx, dy) in enumerate(directions):
            if not chosen(dx, dy):
                continue

            @pl.when(has_device(gi + dx, gj + dy))
            def _():
                for p in range(len(pieces(dx, dy))):
                    remote_copy(k, p, dx, dy, gi + dx, gj + dy).wait_send()

            @pl.when(has_device(gi - dx, gj - dy))
            def _():
                for p in range(len(pieces(dx, dy))):
                    remote_copy(k, p, dx, dy, gi - dx, gj - dy).wait_recv()

    row = lax.broadcasted_iota(jnp.int32, (YE, L), 0)
    lane = lax.broadcasted_iota(jnp.int32, (YE, L), 1)
    m_yhi = (row == NYL - 1) | (row == YE - 1)
    m_ylo = (row == 0) | (row == NYL)
    rz = lane & (CB - 1)
    m_zhi = rz == CB - 1
    m_zlo = rz == 0
    m_rows = row < NYL
    block_y = gj + jnp.where(row < NYL, 0, jnp.where(row < YE - HY, 1, -1))
    global_y = jnp.where(row < YE - HY, gj * NYL + row, gj * NYL + row - YE)
    inside_y = (global_y >= 0) & (global_y < ny * NYL)
    node_y = block_y + 1 < ny
    node_z = (lane >> 4) + 1 < L // CB

    def lookup(x, carry):
        labels = el[x]
        perm = jnp.zeros((YE, L), jnp.float32)
        for c in range(class_perm.shape[0]):
            perm = jnp.where(labels == c, class_perm[c], perm)
        global_x = gi * NXL + x - HX
        inside = inside_y & (global_x >= 0) & (global_x < nx * NXL)
        pm[x] = jnp.where(inside, perm, 0.0)
        return carry

    for local_copy in local_copies:
        local_copy.wait()
    wait_halo(lambda dx, dy: dx == 0)
    lax.fori_loop(HX, HX + NXL, lookup, 0)

    def xplace(x):
        return (x + (CB - HX)) & (CB - 1)

    def pre(x, carry):
        pc = pm[x]
        pxp = jnp.where(x + 1 < XE, pm[jnp.minimum(x + 1, XE - 1)], 0.0)
        pxm = jnp.where(x >= 1, pm[jnp.maximum(x - 1, 0)], 0.0)
        pyp = pltpu.roll(pc, YE - 1, 0)
        pym = pltpu.roll(pc, 1, 0)
        pzp = pltpu.roll(pc, L - 1, 1)
        pzm = pltpu.roll(pc, 1, 1)
        t_xp = conductance(pc, pxp)
        t_xm = conductance(pc, pxm)
        t_yp = conductance(pc, pyp)
        t_ym = conductance(pc, pym)
        t_zp = jnp.where(lane == L - 1, 0.0, conductance(pc, pzp))
        t_zm = jnp.where(lane == 0, 0.0, conductance(pc, pzm))
        diag = t_xp + t_xm + t_yp + t_ym + t_zp + t_zm
        aux[0, x] = diag
        aux[1, x] = 1.0 / jnp.where(diag > 0.0, diag, 1.0)
        cx_hi = xplace(x) == CB - 1
        cx_lo = xplace(x) == 0
        tt[0, x] = t_xp
        tt[1, x] = jnp.where(cx_hi, 0.0, t_xp)
        tt[2, x] = t_xm
        tt[3, x] = jnp.where(cx_lo, 0.0, t_xm)
        tt[4, x] = t_yp
        tt[5, x] = jnp.where(m_yhi, 0.0, t_yp)
        tt[6, x] = t_ym
        tt[7, x] = jnp.where(m_ylo, 0.0, t_ym)
        tt[8, x] = t_zp
        tt[9, x] = jnp.where(m_zhi, 0.0, t_zp)
        tt[10, x] = t_zm
        tt[11, x] = jnp.where(m_zlo, 0.0, t_zm)
        return carry

    def pre_w(x, carry):
        sup = es[x]
        node_x = gi + ((x + (CB - HX)) >> 4) < nx
        for s in range(8):
            bx, by, bz = corner_of(s)
            keep = ((sup >> s) & 1) > 0
            if bx:
                keep = keep & node_x
            if by:
                keep = keep & node_y
            if bz:
                keep = keep & node_z
            v = jnp.where(keep, 1.0, 0.0)
            valid[s, x] = v
            wa[s, x] = eb[s, x] * v
        return carry

    lax.fori_loop(HX, HX + NXL, pre_w, 0)
    lax.fori_loop(HX + 1, HX + NXL - 1, pre, 0)

    def inflow_of(src, x, s, c):
        bx, by, bz = corner_of(s)
        cx_hi = xplace(x) == CB - 1
        cx_lo = xplace(x) == 0
        if bx:
            xp = src[jnp.where(cx_hi, s ^ 4, s), x + 1]
            t1 = tt[0, x]
            xm = src[s, x - 1]
            t2 = tt[3, x]
        else:
            xp = src[s, x + 1]
            t1 = tt[1, x]
            xm = src[jnp.where(cx_lo, s ^ 4, s), x - 1]
            t2 = tt[2, x]
        if by:
            yp = pltpu.roll(jnp.where(m_ylo, src[s ^ 2, x], c), YE - 1, 0)
            t3 = tt[4, x]
            ym = pltpu.roll(c, 1, 0)
            t4 = tt[7, x]
        else:
            yp = pltpu.roll(c, YE - 1, 0)
            t3 = tt[5, x]
            ym = pltpu.roll(jnp.where(m_yhi, src[s ^ 2, x], c), 1, 0)
            t4 = tt[6, x]
        if bz:
            zp = pltpu.roll(jnp.where(m_zlo, src[s ^ 1, x], c), L - 1, 1)
            t5 = tt[8, x]
            zm = pltpu.roll(c, 1, 1)
            t6 = tt[11, x]
        else:
            zp = pltpu.roll(c, L - 1, 1)
            t5 = tt[9, x]
            zm = pltpu.roll(jnp.where(m_zhi, src[s ^ 1, x], c), 1, 1)
            t6 = tt[10, x]
        return t1 * xp + t2 * xm + t3 * yp + t4 * ym + t5 * zp + t6 * zm

    def sweep(src, dst, lo, hi):
        def body(x, carry):
            diag = aux[0, x]
            inv = aux[1, x]
            for s in range(8):
                c = src[s, x]
                inflow = inflow_of(src, x, s, c)
                dst[s, x] = (c - omega_jacobi * (diag * c - inflow) * inv) * valid[s, x]
            return carry

        lax.fori_loop(lo, hi, body, 0)

    bufs = (wa, wb)
    for step in range(ITERS):
        sweep(bufs[step % 2], bufs[(step + 1) % 2], HX + step + 1, HX + NXL - step - 1)
    wait_halo(lambda dx, dy: dx != 0)
    lax.fori_loop(0, HX, lookup, 0)
    lax.fori_loop(HX + NXL, XE, lookup, 0)
    lax.fori_loop(0, HX, pre_w, 0)
    lax.fori_loop(HX + NXL, XE, pre_w, 0)
    lax.fori_loop(0, HX + 1, pre, 0)
    lax.fori_loop(HX + NXL - 1, XE, pre, 0)
    for step in range(ITERS):
        sweep(bufs[step % 2], bufs[(step + 1) % 2], step + 1, HX + step + 1)
        sweep(bufs[step % 2], bufs[(step + 1) % 2], HX + NXL - step - 1, XE - step - 1)
    last = bufs[ITERS % 2]
    basis_buf = wc

    def normalize(x, carry):
        vals = [last[s, x] for s in range(8)]
        total = vals[0]
        for s in range(1, 8):
            total = total + vals[s]
        scale = jnp.maximum(total, renorm_floor)
        for s in range(8):
            basis_buf[s, x, pl.ds(0, NYL), :] = (vals[s] / scale)[:NYL, :]
        return carry

    lax.fori_loop(HX, HX + NXL, normalize, 0)

    def edge_copy(k, p, dx, dy, target_x, target_y):
        run, from_x, to_x, from_y, to_y = edge_pieces(dx, dy)[p]
        return pltpu.make_async_remote_copy(
            src_ref=wc.at[run, from_x, from_y, :],
            dst_ref=wc.at[run, to_x, to_y, :],
            send_sem=edge_send.at[2 * k + p],
            recv_sem=edge_recv.at[2 * k + p],
            device_id=(target_x, target_y),
            device_id_type=mesh_id,
        )

    for k, (dx, dy) in enumerate(faces):
        @pl.when(has_device(gi + dx, gj + dy))
        def _():
            for p in range(len(edge_pieces(dx, dy))):
                edge_copy(k, p, dx, dy, gi + dx, gj + dy).start()

    for k, (dx, dy) in enumerate(faces):
        @pl.when(has_device(gi + dx, gj + dy))
        def _():
            for p in range(len(edge_pieces(dx, dy))):
                edge_copy(k, p, dx, dy, gi + dx, gj + dy).wait_send()

        @pl.when(has_device(gi - dx, gj - dy))
        def _():
            for p in range(len(edge_pieces(dx, dy))):
                edge_copy(k, p, dx, dy, gi - dx, gj - dy).wait_recv()

    def image(x, carry):
        diag = aux[0, x]
        for s in range(8):
            c = basis_buf[s, x]
            inflow = inflow_of(basis_buf, x, s, c)
            img[s, x - HX] = jnp.where(m_rows, diag * c - inflow, 0.0)
            basis_ref[s, x - HX] = c[:NYL, :]
        return carry

    lax.fori_loop(HX, HX + NXL, image, 0)

    for s1 in range(8):
        def pair_sums(x, acc):
            b = basis_buf[s1, x + HX]
            return tuple(acc[s2] + b * img[s2, x] for s2 in range(8))

        acc = lax.fori_loop(
            0, NXL, pair_sums, tuple(jnp.zeros((YE, L), jnp.float32) for _ in range(8))
        )
        for s2 in range(8):
            prod_ref[pl.ds(s1 * 8 + s2, 1), :] = jnp.sum(acc[s2], axis=0, keepdims=True)

    nbz = L // CB
    node = lax.broadcasted_iota(jnp.int32, (nbz, L), 0)
    block = lax.broadcasted_iota(jnp.int32, (nbz, L), 1) >> 4
    same_node = jnp.where(block == node, 1.0, 0.0)
    node_above = jnp.where(block + 1 == node, 1.0, 0.0)
    pairs = prod_ref[...]
    along_lanes = (((1,), (1,)), ((), ()))
    exact = lax.Precision.HIGHEST
    low = lax.dot_general(same_node, pairs, along_lanes, precision=exact,
                          preferred_element_type=jnp.float32)
    high = lax.dot_general(node_above, pairs, along_lanes, precision=exact,
                           preferred_element_type=jnp.float32)
    for c in range(4):
        terms[c] = jnp.dot(low, placing[c, 0], precision=exact,
                           preferred_element_type=jnp.float32) + jnp.dot(
            high, placing[c, 1], precision=exact, preferred_element_type=jnp.float32)

    def coarse_copy(k, c, target_x, target_y):
        return pltpu.make_async_remote_copy(
            src_ref=terms.at[c],
            dst_ref=received.at[k],
            send_sem=coarse_send.at[k],
            recv_sem=coarse_recv.at[k],
            device_id=(target_x, target_y),
            device_id_type=mesh_id,
        )

    for k, (c, dx, dy) in enumerate(coarse_routes):
        @pl.when(has_device(gi + dx, gj + dy))
        def _():
            coarse_copy(k, c, gi + dx, gj + dy).start()

    for k, (c, dx, dy) in enumerate(coarse_routes):
        @pl.when(has_device(gi + dx, gj + dy))
        def _():
            coarse_copy(k, c, gi + dx, gj + dy).wait_send()

        @pl.when(has_device(gi - dx, gj - dy))
        def _():
            coarse_copy(k, c, gi - dx, gj - dy).wait_recv()

    total = terms[0] + received[0] + received[1] + received[2]
    coarse_ref[...] = total[:, : coarse_ref.shape[1]]


def placing_matrix():
    table = np.zeros((4, 2, 64, 32), np.float32)
    for first_slot in range(8):
        for second_slot in range(8):
            one_x, one_y, one_z = corner_of(first_slot)
            two_x, two_y, two_z = corner_of(second_slot)
            offset_index = 9 * (two_x - one_x + 1) + 3 * (two_y - one_y + 1) + (two_z - one_z + 1)
            table[one_x * 2 + one_y, one_z, first_slot * 8 + second_slot, offset_index] = 1.0
    return table


def shards(initial_basis, labels, class_perm, support):
    size_x, size_y, size_z = labels.shape
    assert size_x == CB and size_y == CB and size_z % CB == 0
    blocks_z = size_z // CB
    nx = lax.axis_size("gx")
    ny = lax.axis_size("gy")
    XE = size_x + 2 * HX
    YE = -(-(size_y + 2 * HY) // 8) * 8
    f32 = jnp.float32
    vmem = pl.BlockSpec(memory_space=pltpu.VMEM)
    blocks_z = size_z // CB
    basis, coarse = pl.pallas_call(
        functools.partial(smooth_kernel, nx, ny),
        out_shape=(
            jax.ShapeDtypeStruct((8, size_x, size_y, size_z), f32),
            jax.ShapeDtypeStruct((blocks_z, 27), f32),
        ),
        in_specs=[vmem, vmem, pl.BlockSpec(memory_space=pltpu.SMEM), vmem, vmem],
        out_specs=(vmem, vmem),
        scratch_shapes=[
            pltpu.VMEM((8, XE, YE, size_z), f32),
            pltpu.VMEM((XE, YE, size_z), jnp.int32),
            pltpu.VMEM((XE, YE, size_z), jnp.int32),
            pltpu.VMEM((XE, YE, size_z), f32),
            pltpu.VMEM((12, XE, YE, size_z), f32),
            pltpu.VMEM((2, XE, YE, size_z), f32),
            pltpu.VMEM((8, XE, YE, size_z), f32),
            pltpu.VMEM((8, XE, YE, size_z), f32),
            pltpu.VMEM((8, XE, YE, size_z), f32),
            pltpu.VMEM((8, XE, YE, size_z), f32),
            pltpu.VMEM((8, size_x, YE, size_z), f32),
            pltpu.VMEM((64, size_z), f32),
            pltpu.VMEM((4, blocks_z, 32), f32),
            pltpu.VMEM((3, blocks_z, 32), f32),
            pltpu.SemaphoreType.DMA((32,)),
            pltpu.SemaphoreType.DMA((32,)),
            pltpu.SemaphoreType.DMA((3,)),
            pltpu.SemaphoreType.DMA((3,)),
            pltpu.SemaphoreType.DMA((3,)),
            pltpu.SemaphoreType.DMA((8,)),
            pltpu.SemaphoreType.DMA((8,)),
        ],
        compiler_params=pltpu.CompilerParams(collective_id=1, has_side_effects=True),
    )(initial_basis, labels, class_perm, support, jnp.asarray(placing_matrix()))
    return (basis, coarse.T.reshape(27, 1, 1, blocks_z))


def solution(mesh):
    return jax.shard_map(
        shards,
        mesh=mesh,
        in_specs=(P(None, "gx", "gy", None), P("gx", "gy", None), P(), P("gx", "gy", None)),
        out_specs=(P(None, "gx", "gy", None), P(None, "gx", "gy", None)),
        check_vma=False,
    )
```

```python
import functools
import numpy as np
import jax
import jax.numpy as jnp
from jax import lax
from jax.experimental import pallas as pl
from jax.experimental.pallas import tpu as pltpu
from jax.sharding import PartitionSpec as P

CB = 16
ITERS = 3
HX = ITERS
HY = ITERS

omega_jacobi = 2.0 / 3.0
renorm_floor = 0.5


def with_halo(block, sides, width):
    for axis, dim in sides:
        count = lax.axis_size(axis)
        forward = [(i, i + 1) for i in range(count - 1)]
        backward = [(target, source) for source, target in forward]
        low = lax.ppermute(
            lax.slice_in_dim(block, block.shape[dim] - width, None, axis=dim), axis, forward
        )
        high = lax.ppermute(lax.slice_in_dim(block, 0, width, axis=dim), axis, backward)
        block = jnp.concatenate([low, block, high], axis=dim)
    return block


def from_behind(shard, axis, by):
    peers = lax.axis_size(axis)
    pairs = [(i, i + by) for i in range(peers) if 0 <= i + by < peers]
    return lax.ppermute(shard, axis, pairs)


def corner_of(slot_index):
    return (slot_index >> 2 & 1, slot_index >> 1 & 1, slot_index & 1)


def conductance(centre, neighbour):
    total_perm = centre + neighbour
    divisor = jnp.where(total_perm > 0.0, total_perm, 1.0)
    return 2.0 * centre * neighbour / divisor


def class_lookup(labels, class_perm):
    classes = jnp.arange(class_perm.shape[0])
    hits = labels[None] == classes[:, None, None, None]
    return jnp.sum(jnp.where(hits, class_perm[:, None, None, None], 0.0), axis=0)


def existing_bits(count_x, count_y, count_z, first_x, first_y, limit_x, limit_y, limit_z):
    block_x = (jnp.arange(count_x) + first_x) // CB
    block_y = (jnp.arange(count_y) + first_y) // CB
    block_z = jnp.arange(count_z) // CB
    bits = jnp.zeros((count_x, count_y, count_z), jnp.int32)
    for slot_index in range(8):
        corner_x, corner_y, corner_z = corner_of(slot_index)
        inside = (
            (block_x + corner_x < limit_x)[:, None, None]
            & (block_y + corner_y < limit_y)[None, :, None]
            & (block_z + corner_z < limit_z)[None, None, :]
        )
        bits = bits | jnp.where(inside, 1 << slot_index, 0)
    return bits


def halo_window(ref, xs, ys, slots=None):
    if len(ref.shape) == 4:
        return ref.at[slots if slots is not None else slice(None), xs, ys, :]
    return ref.at[xs, ys, :]


def halo_range(d, count, halo):
    if d > 0:
        return pl.ds(count - halo, halo), pl.ds(0, halo)
    if d < 0:
        return pl.ds(0, halo), pl.ds(halo + count, halo)
    return pl.ds(0, count), pl.ds(halo, count)


def halo_rows(d, count, halo, total):
    if d > 0:
        return pl.ds(count - halo, halo), pl.ds(total - halo, halo)
    if d < 0:
        return pl.ds(0, halo), pl.ds(count, halo)
    return pl.ds(0, count), pl.ds(0, count)


def slot_runs(slots):
    runs = []
    for s in sorted(slots):
        if runs and runs[-1][1] == s:
            runs[-1][1] = s + 1
        else:
            runs.append([s, s + 1])
    return [pl.ds(lo, hi - lo) for lo, hi in runs]


def shared_slots(dx, dy):
    keep = []
    for s in range(8):
        bx, by, _ = corner_of(s)
        if (dx > 0 and not bx) or (dx < 0 and bx) or (dy > 0 and not by) or (dy < 0 and by):
            continue
        keep.append(s)
    return keep


def smooth_kernel(
    nx, ny,
    basis_in, labels_in, class_perm, support_in, placing, basis_ref, coarse_ref,
    eb, el, es, pm, tt, aux, valid, wa, wb, wc, img, prod_ref, terms, received,
    send_sem, recv_sem, local_sem, coarse_send, coarse_recv, edge_send, edge_recv,
):
    gi = lax.axis_index("gx")
    gj = lax.axis_index("gy")
    _, XE, YE, L = eb.shape
    NXL = basis_ref.shape[1]
    NYL = basis_ref.shape[2]
    mesh_id = pl.DeviceIdType.MESH
    sources = (basis_in, labels_in, support_in)
    targets = (eb, el, es)
    local_copies = []
    for a in range(3):
        local_copy = pltpu.make_async_copy(
            sources[a], halo_window(targets[a], pl.ds(HX, NXL), pl.ds(0, NYL)), local_sem.at[a]
        )
        local_copy.start()
        local_copies.append(local_copy)

    directions = [(dx, dy) for dx in (-1, 0, 1) for dy in (-1, 0, 1) if (dx, dy) != (0, 0)]

    def has_device(x, y):
        return (x >= 0) & (x < nx) & (y >= 0) & (y < ny)

    barrier = pltpu.get_barrier_semaphore()
    for dx, dy in directions:
        @pl.when(has_device(gi + dx, gj + dy))
        def _():
            pl.semaphore_signal(barrier, 1, device_id=(gi + dx, gj + dy), device_id_type=mesh_id)

    def pieces(dx, dy):
        return [(0, run) for run in slot_runs(shared_slots(dx, dy))] + [(1, None), (2, None)]

    def edge_pieces(dx, dy):
        from_x = {1: pl.ds(HX + NXL - 1, 1), -1: pl.ds(HX, 1), 0: pl.ds(HX, NXL)}[dx]
        to_x = {1: pl.ds(HX - 1, 1), -1: pl.ds(HX + NXL, 1), 0: pl.ds(HX, NXL)}[dx]
        from_y = {1: pl.ds(NYL - 1, 1), -1: pl.ds(0, 1), 0: pl.ds(0, NYL)}[dy]
        to_y = {1: pl.ds(YE - 1, 1), -1: pl.ds(NYL, 1), 0: pl.ds(0, NYL)}[dy]
        return [(run, from_x, to_x, from_y, to_y) for run in slot_runs(shared_slots(dx, dy))]

    faces = ((1, 0), (-1, 0), (0, 1), (0, -1))
    peers = jnp.int32(0)
    for dx, dy in directions:
        _, to_x = halo_range(dx, NXL, HX)
        _, to_y = halo_rows(dy, NYL, HY, YE)
        from_here = has_device(gi - dx, gj - dy)
        peers = peers + from_here.astype(jnp.int32)
        unshared = [s for s in range(8) if s not in shared_slots(dx, dy)]
        for run in slot_runs(unshared):
            window = halo_window(eb, to_x, to_y, run)
            window[...] = jnp.zeros(window.shape, window.dtype)

        @pl.when(jnp.logical_not(from_here))
        def _():
            for a in range(3):
                window = halo_window(targets[a], to_x, to_y)
                window[...] = jnp.zeros(window.shape, window.dtype)

    if NYL + HY < YE - HY:
        junction = pl.ds(NYL + HY, YE - 2 * HY - NYL)
        for a in range(3):
            window = halo_window(targets[a], pl.ds(0, XE), junction)
            window[...] = jnp.zeros(window.shape, window.dtype)
    window = wc.at[:, pl.ds(HX, NXL), pl.ds(NYL, YE - NYL), :]
    window[...] = jnp.zeros(window.shape, window.dtype)
    for dx, dy in faces:
        @pl.when(jnp.logical_not(has_device(gi - dx, gj - dy)))
        def _():
            for run, _, to_x, _, to_y in edge_pieces(dx, dy):
                window = wc.at[run, to_x, to_y, :]
                window[...] = jnp.zeros(window.shape, window.dtype)

    coarse_routes = ((2, 1, 0), (1, 0, 1), (3, 1, 1))
    for k, (_, dx, dy) in enumerate(coarse_routes):
        @pl.when(jnp.logical_not(has_device(gi - dx, gj - dy)))
        def _():
            received[k] = jnp.zeros(received.shape[1:], received.dtype)

    pl.semaphore_wait(barrier, peers)

    def remote_copy(k, p, dx, dy, target_x, target_y):
        from_x, to_x = halo_range(dx, NXL, HX)
        from_y, to_y = halo_rows(dy, NYL, HY, YE)
        a, run = pieces(dx, dy)[p]
        return pltpu.make_async_remote_copy(
            src_ref=halo_window(sources[a], from_x, from_y, run),
            dst_ref=halo_window(targets[a], to_x, to_y, run),
            send_sem=send_sem.at[4 * k + p],
            recv_sem=recv_sem.at[4 * k + p],
            device_id=(target_x, target_y),
            device_id_type=mesh_id,
        )

    for k, (dx, dy) in enumerate(directions):
        @pl.when(has_device(gi + dx, gj + dy))
        def _():
            for p in range(len(pieces(dx, dy))):
                remote_copy(k, p, dx, dy, gi + dx, gj + dy).start()

    def wait_halo(chosen):
        for k, (dx, dy) in enumerate(directions):
            if not chosen(dx, dy):
                continue

            @pl.when(has_device(gi + dx, gj + dy))
            def _():
                for p in range(len(pieces(dx, dy))):
                    remote_copy(k, p, dx, dy, gi + dx, gj + dy).wait_send()

            @pl.when(has_device(gi - dx, gj - dy))
            def _():
                for p in range(len(pieces(dx, dy))):
                    remote_copy(k, p, dx, dy, gi - dx, gj - dy).wait_recv()

    row = lax.broadcasted_iota(jnp.int32, (YE, L), 0)
    lane = lax.broadcasted_iota(jnp.int32, (YE, L), 1)
    m_yhi = (row == NYL - 1) | (row == YE - 1)
    m_ylo = (row == 0) | (row == NYL)
    rz = lane & (CB - 1)
    m_zhi = rz == CB - 1
    m_zlo = rz == 0
    m_rows = row < NYL
    block_y = gj + jnp.where(row < NYL, 0, jnp.where(row < YE - HY, 1, -1))
    global_y = jnp.where(row < YE - HY, gj * NYL + row, gj * NYL + row - YE)
    inside_y = (global_y >= 0) & (global_y < ny * NYL)
    node_y = block_y + 1 < ny
    node_z = (lane >> 4) + 1 < L // CB

    def lookup(x, carry):
        labels = el[x]
        perm = jnp.zeros((YE, L), jnp.float32)
        for c in range(class_perm.shape[0]):
            perm = jnp.where(labels == c, class_perm[c], perm)
        global_x = gi * NXL + x - HX
        inside = inside_y & (global_x >= 0) & (global_x < nx * NXL)
        pm[x] = jnp.where(inside, perm, 0.0)
        return carry

    for local_copy in local_copies:
        local_copy.wait()
    wait_halo(lambda dx, dy: dx == 0)
    lax.fori_loop(HX, HX + NXL, lookup, 0)

    def xplace(x):
        return (x + (CB - HX)) & (CB - 1)

    def pre(x, carry):
        pc = pm[x]
        pxp = jnp.where(x + 1 < XE, pm[jnp.minimum(x + 1, XE - 1)], 0.0)
        pxm = jnp.where(x >= 1, pm[jnp.maximum(x - 1, 0)], 0.0)
        pyp = pltpu.roll(pc, YE - 1, 0)
        pym = pltpu.roll(pc, 1, 0)
        pzp = pltpu.roll(pc, L - 1, 1)
        pzm = pltpu.roll(pc, 1, 1)
        t_xp = conductance(pc, pxp)
        t_xm = conductance(pc, pxm)
        t_yp = conductance(pc, pyp)
        t_ym = conductance(pc, pym)
        t_zp = jnp.where(lane == L - 1, 0.0, conductance(pc, pzp))
        t_zm = jnp.where(lane == 0, 0.0, conductance(pc, pzm))
        diag = t_xp + t_xm + t_yp + t_ym + t_zp + t_zm
        aux[0, x] = diag
        aux[1, x] = 1.0 / jnp.where(diag > 0.0, diag, 1.0)
        cx_hi = xplace(x) == CB - 1
        cx_lo = xplace(x) == 0
        tt[0, x] = t_xp
        tt[1, x] = jnp.where(cx_hi, 0.0, t_xp)
        tt[2, x] = t_xm
        tt[3, x] = jnp.where(cx_lo, 0.0, t_xm)
        tt[4, x] = t_yp
        tt[5, x] = jnp.where(m_yhi, 0.0, t_yp)
        tt[6, x] = t_ym
        tt[7, x] = jnp.where(m_ylo, 0.0, t_ym)
        tt[8, x] = t_zp
        tt[9, x] = jnp.where(m_zhi, 0.0, t_zp)
        tt[10, x] = t_zm
        tt[11, x] = jnp.where(m_zlo, 0.0, t_zm)
        return carry

    def pre_w(x, carry):
        sup = es[x]
        node_x = gi + ((x + (CB - HX)) >> 4) < nx
        for s in range(8):
            bx, by, bz = corner_of(s)
            keep = ((sup >> s) & 1) > 0
            if bx:
                keep = keep & node_x
            if by:
                keep = keep & node_y
            if bz:
                keep = keep & node_z
            v = jnp.where(keep, 1.0, 0.0)
            valid[s, x] = v
            wa[s, x] = eb[s, x] * v
        return carry

    lax.fori_loop(HX, HX + NXL, pre_w, 0)
    lax.fori_loop(HX + 1, HX + NXL - 1, pre, 0)

    def inflow_of(src, x, s, c):
        bx, by, bz = corner_of(s)
        cx_hi = xplace(x) == CB - 1
        cx_lo = xplace(x) == 0
        if bx:
            xp = src[jnp.where(cx_hi, s ^ 4, s), x + 1]
            t1 = tt[0, x]
            xm = src[s, x - 1]
            t2 = tt[3, x]
        else:
            xp = src[s, x + 1]
            t1 = tt[1, x]
            xm = src[jnp.where(cx_lo, s ^ 4, s), x - 1]
            t2 = tt[2, x]
        if by:
            yp = pltpu.roll(jnp.where(m_ylo, src[s ^ 2, x], c), YE - 1, 0)
            t3 = tt[4, x]
            ym = pltpu.roll(c, 1, 0)
            t4 = tt[7, x]
        else:
            yp = pltpu.roll(c, YE - 1, 0)
            t3 = tt[5, x]
            ym = pltpu.roll(jnp.where(m_yhi, src[s ^ 2, x], c), 1, 0)
            t4 = tt[6, x]
        if bz:
            zp = pltpu.roll(jnp.where(m_zlo, src[s ^ 1, x], c), L - 1, 1)
            t5 = tt[8, x]
            zm = pltpu.roll(c, 1, 1)
            t6 = tt[11, x]
        else:
            zp = pltpu.roll(c, L - 1, 1)
            t5 = tt[9, x]
            zm = pltpu.roll(jnp.where(m_zhi, src[s ^ 1, x], c), 1, 1)
            t6 = tt[10, x]
        return t1 * xp + t2 * xm + t3 * yp + t4 * ym + t5 * zp + t6 * zm

    def sweep(src, dst, lo, hi):
        def body(x, carry):
            diag = aux[0, x]
            inv = aux[1, x]
            for s in range(8):
                c = src[s, x]
                inflow = inflow_of(src, x, s, c)
                dst[s, x] = (c - omega_jacobi * (diag * c - inflow) * inv) * valid[s, x]
            return carry

        lax.fori_loop(lo, hi, body, 0)

    bufs = (wa, wb)
    for step in range(ITERS):
        sweep(bufs[step % 2], bufs[(step + 1) % 2], HX + step + 1, HX + NXL - step - 1)
    wait_halo(lambda dx, dy: dx != 0)
    lax.fori_loop(0, HX, lookup, 0)
    lax.fori_loop(HX + NXL, XE, lookup, 0)
    lax.fori_loop(0, HX, pre_w, 0)
    lax.fori_loop(HX + NXL, XE, pre_w, 0)
    lax.fori_loop(0, HX + 1, pre, 0)
    lax.fori_loop(HX + NXL - 1, XE, pre, 0)
    for step in range(ITERS):
        sweep(bufs[step % 2], bufs[(step + 1) % 2], step + 1, HX + step + 1)
        sweep(bufs[step % 2], bufs[(step + 1) % 2], HX + NXL - step - 1, XE - step - 1)
    last = bufs[ITERS % 2]
    basis_buf = wc

    def normalize(x, carry):
        vals = [last[s, x] for s in range(8)]
        total = vals[0]
        for s in range(1, 8):
            total = total + vals[s]
        scale = jnp.maximum(total, renorm_floor)
        for s in range(8):
            basis_buf[s, x, pl.ds(0, NYL), :] = (vals[s] / scale)[:NYL, :]
        return carry

    lax.fori_loop(HX, HX + NXL, normalize, 0)

    def edge_copy(k, p, dx, dy, target_x, target_y):
        run, from_x, to_x, from_y, to_y = edge_pieces(dx, dy)[p]
        return pltpu.make_async_remote_copy(
            src_ref=wc.at[run, from_x, from_y, :],
            dst_ref=wc.at[run, to_x, to_y, :],
            send_sem=edge_send.at[2 * k + p],
            recv_sem=edge_recv.at[2 * k + p],
            device_id=(target_x, target_y),
            device_id_type=mesh_id,
        )

    for k, (dx, dy) in enumerate(faces):
        @pl.when(has_device(gi + dx, gj + dy))
        def _():
            for p in range(len(edge_pieces(dx, dy))):
                edge_copy(k, p, dx, dy, gi + dx, gj + dy).start()

    for k, (dx, dy) in enumerate(faces):
        @pl.when(has_device(gi + dx, gj + dy))
        def _():
            for p in range(len(edge_pieces(dx, dy))):
                edge_copy(k, p, dx, dy, gi + dx, gj + dy).wait_send()

        @pl.when(has_device(gi - dx, gj - dy))
        def _():
            for p in range(len(edge_pieces(dx, dy))):
                edge_copy(k, p, dx, dy, gi - dx, gj - dy).wait_recv()

    def image(x, carry):
        diag = aux[0, x]
        for s in range(8):
            c = basis_buf[s, x]
            inflow = inflow_of(basis_buf, x, s, c)
            img[s, x - HX] = jnp.where(m_rows, diag * c - inflow, 0.0)
            basis_ref[s, x - HX] = c[:NYL, :]
        return carry

    lax.fori_loop(HX, HX + NXL, image, 0)

    def pair_rows(s1):
        def pair_sums(x, acc):
            b = basis_buf[s1, x + HX]
            return tuple(acc[s2] + b * img[s2, x] for s2 in range(8))

        acc = lax.fori_loop(
            0, NXL, pair_sums, tuple(jnp.zeros((YE, L), jnp.float32) for _ in range(8))
        )
        for s2 in range(8):
            prod_ref[pl.ds(s1 * 8 + s2, 1), :] = jnp.sum(acc[s2], axis=0, keepdims=True)

    nbz = L // CB
    node = lax.broadcasted_iota(jnp.int32, (nbz, L), 0)
    block = lax.broadcasted_iota(jnp.int32, (nbz, L), 1) >> 4
    same_node = jnp.where(block == node, 1.0, 0.0)
    node_above = jnp.where(block + 1 == node, 1.0, 0.0)
    along_lanes = (((1,), (1,)), ((), ()))
    exact = lax.Precision.HIGHEST

    def class_terms(c):
        rows = pl.ds(16 * c, 16)
        pairs = prod_ref[rows, :]
        low = lax.dot_general(same_node, pairs, along_lanes, precision=exact,
                              preferred_element_type=jnp.float32)
        high = lax.dot_general(node_above, pairs, along_lanes, precision=exact,
                               preferred_element_type=jnp.float32)
        terms[c] = jnp.dot(low, placing[c, 0, rows, :], precision=exact,
                           preferred_element_type=jnp.float32) + jnp.dot(
            high, placing[c, 1, rows, :], precision=exact, preferred_element_type=jnp.float32)

    def coarse_copy(k, c, target_x, target_y):
        return pltpu.make_async_remote_copy(
            src_ref=terms.at[c],
            dst_ref=received.at[k],
            send_sem=coarse_send.at[k],
            recv_sem=coarse_recv.at[k],
            device_id=(target_x, target_y),
            device_id_type=mesh_id,
        )

    for s1 in range(2, 8):
        pair_rows(s1)
    for c in range(1, 4):
        class_terms(c)
    for k, (c, dx, dy) in enumerate(coarse_routes):
        @pl.when(has_device(gi + dx, gj + dy))
        def _():
            coarse_copy(k, c, gi + dx, gj + dy).start()

    for s1 in range(2):
        pair_rows(s1)
    class_terms(0)

    for k, (c, dx, dy) in enumerate(coarse_routes):
        @pl.when(has_device(gi + dx, gj + dy))
        def _():
            coarse_copy(k, c, gi + dx, gj + dy).wait_send()

        @pl.when(has_device(gi - dx, gj - dy))
        def _():
            coarse_copy(k, c, gi - dx, gj - dy).wait_recv()

    total = terms[0] + received[0] + received[1] + received[2]
    coarse_ref[...] = total[:, : coarse_ref.shape[1]]


def placing_matrix():
    table = np.zeros((4, 2, 64, 32), np.float32)
    for first_slot in range(8):
        for second_slot in range(8):
            one_x, one_y, one_z = corner_of(first_slot)
            two_x, two_y, two_z = corner_of(second_slot)
            offset_index = 9 * (two_x - one_x + 1) + 3 * (two_y - one_y + 1) + (two_z - one_z + 1)
            table[one_x * 2 + one_y, one_z, first_slot * 8 + second_slot, offset_index] = 1.0
    return table


def shards(initial_basis, labels, class_perm, support):
    size_x, size_y, size_z = labels.shape
    assert size_x == CB and size_y == CB and size_z % CB == 0
    blocks_z = size_z // CB
    nx = lax.axis_size("gx")
    ny = lax.axis_size("gy")
    XE = size_x + 2 * HX
    YE = -(-(size_y + 2 * HY) // 8) * 8
    f32 = jnp.float32
    vmem = pl.BlockSpec(memory_space=pltpu.VMEM)
    blocks_z = size_z // CB
    basis, coarse = pl.pallas_call(
        functools.partial(smooth_kernel, nx, ny),
        out_shape=(
            jax.ShapeDtypeStruct((8, size_x, size_y, size_z), f32),
            jax.ShapeDtypeStruct((blocks_z, 27), f32),
        ),
        in_specs=[vmem, vmem, pl.BlockSpec(memory_space=pltpu.SMEM), vmem, vmem],
        out_specs=(vmem, vmem),
        scratch_shapes=[
            pltpu.VMEM((8, XE, YE, size_z), f32),
            pltpu.VMEM((XE, YE, size_z), jnp.int32),
            pltpu.VMEM((XE, YE, size_z), jnp.int32),
            pltpu.VMEM((XE, YE, size_z), f32),
            pltpu.VMEM((12, XE, YE, size_z), f32),
            pltpu.VMEM((2, XE, YE, size_z), f32),
            pltpu.VMEM((8, XE, YE, size_z), f32),
            pltpu.VMEM((8, XE, YE, size_z), f32),
            pltpu.VMEM((8, XE, YE, size_z), f32),
            pltpu.VMEM((8, XE, YE, size_z), f32),
            pltpu.VMEM((8, size_x, YE, size_z), f32),
            pltpu.VMEM((64, size_z), f32),
            pltpu.VMEM((4, blocks_z, 32), f32),
            pltpu.VMEM((3, blocks_z, 32), f32),
            pltpu.SemaphoreType.DMA((32,)),
            pltpu.SemaphoreType.DMA((32,)),
            pltpu.SemaphoreType.DMA((3,)),
            pltpu.SemaphoreType.DMA((3,)),
            pltpu.SemaphoreType.DMA((3,)),
            pltpu.SemaphoreType.DMA((8,)),
            pltpu.SemaphoreType.DMA((8,)),
        ],
        compiler_params=pltpu.CompilerParams(collective_id=1, has_side_effects=True),
    )(initial_basis, labels, class_perm, support, jnp.asarray(placing_matrix()))
    return (basis, coarse.T.reshape(27, 1, 1, blocks_z))


def solution(mesh):
    return jax.shard_map(
        shards,
        mesh=mesh,
        in_specs=(P(None, "gx", "gy", None), P("gx", "gy", None), P(), P("gx", "gy", None)),
        out_specs=(P(None, "gx", "gy", None), P(None, "gx", "gy", None)),
        check_vma=False,
    )
```

```python
import functools
import numpy as np
import jax
import jax.numpy as jnp
from jax import lax
from jax.experimental import pallas as pl
from jax.experimental.pallas import tpu as pltpu
from jax.sharding import PartitionSpec as P

CB = 16
ITERS = 3
HX = ITERS
HY = ITERS

omega_jacobi = 2.0 / 3.0
renorm_floor = 0.5


def with_halo(block, sides, width):
    for axis, dim in sides:
        count = lax.axis_size(axis)
        forward = [(i, i + 1) for i in range(count - 1)]
        backward = [(target, source) for source, target in forward]
        low = lax.ppermute(
            lax.slice_in_dim(block, block.shape[dim] - width, None, axis=dim), axis, forward
        )
        high = lax.ppermute(lax.slice_in_dim(block, 0, width, axis=dim), axis, backward)
        block = jnp.concatenate([low, block, high], axis=dim)
    return block


def from_behind(shard, axis, by):
    peers = lax.axis_size(axis)
    pairs = [(i, i + by) for i in range(peers) if 0 <= i + by < peers]
    return lax.ppermute(shard, axis, pairs)


def corner_of(slot_index):
    return (slot_index >> 2 & 1, slot_index >> 1 & 1, slot_index & 1)


def conductance(centre, neighbour):
    total_perm = centre + neighbour
    divisor = jnp.where(total_perm > 0.0, total_perm, 1.0)
    return 2.0 * centre * neighbour / divisor


def class_lookup(labels, class_perm):
    classes = jnp.arange(class_perm.shape[0])
    hits = labels[None] == classes[:, None, None, None]
    return jnp.sum(jnp.where(hits, class_perm[:, None, None, None], 0.0), axis=0)


def existing_bits(count_x, count_y, count_z, first_x, first_y, limit_x, limit_y, limit_z):
    block_x = (jnp.arange(count_x) + first_x) // CB
    block_y = (jnp.arange(count_y) + first_y) // CB
    block_z = jnp.arange(count_z) // CB
    bits = jnp.zeros((count_x, count_y, count_z), jnp.int32)
    for slot_index in range(8):
        corner_x, corner_y, corner_z = corner_of(slot_index)
        inside = (
            (block_x + corner_x < limit_x)[:, None, None]
            & (block_y + corner_y < limit_y)[None, :, None]
            & (block_z + corner_z < limit_z)[None, None, :]
        )
        bits = bits | jnp.where(inside, 1 << slot_index, 0)
    return bits


def halo_window(ref, xs, ys, slots=None):
    if len(ref.shape) == 4:
        return ref.at[slots if slots is not None else slice(None), xs, ys, :]
    return ref.at[xs, ys, :]


def halo_range(d, count, halo):
    if d > 0:
        return pl.ds(count - halo, halo), pl.ds(0, halo)
    if d < 0:
        return pl.ds(0, halo), pl.ds(halo + count, halo)
    return pl.ds(0, count), pl.ds(halo, count)


def halo_rows(d, count, halo, total):
    if d > 0:
        return pl.ds(count - halo, halo), pl.ds(total - halo, halo)
    if d < 0:
        return pl.ds(0, halo), pl.ds(count, halo)
    return pl.ds(0, count), pl.ds(0, count)


def slot_runs(slots):
    runs = []
    for s in sorted(slots):
        if runs and runs[-1][1] == s:
            runs[-1][1] = s + 1
        else:
            runs.append([s, s + 1])
    return [pl.ds(lo, hi - lo) for lo, hi in runs]


def shared_slots(dx, dy):
    keep = []
    for s in range(8):
        bx, by, _ = corner_of(s)
        if (dx > 0 and not bx) or (dx < 0 and bx) or (dy > 0 and not by) or (dy < 0 and by):
            continue
        keep.append(s)
    return keep


def smooth_kernel(
    nx, ny,
    basis_in, labels_in, class_perm, support_in, placing, basis_ref, coarse_ref,
    eb, el, es, pm, tt, ts, aux, valid, wa, wb, wc, img, prod_ref, terms, received,
    send_sem, recv_sem, local_sem, coarse_send, coarse_recv, edge_send, edge_recv,
):
    gi = lax.axis_index("gx")
    gj = lax.axis_index("gy")
    _, XE, YE, L = eb.shape
    NXL = basis_ref.shape[1]
    NYL = basis_ref.shape[2]
    mesh_id = pl.DeviceIdType.MESH
    sources = (basis_in, labels_in, support_in)
    targets = (eb, el, es)
    local_copies = []
    for a in range(3):
        local_copy = pltpu.make_async_copy(
            sources[a], halo_window(targets[a], pl.ds(HX, NXL), pl.ds(0, NYL)), local_sem.at[a]
        )
        local_copy.start()
        local_copies.append(local_copy)

    directions = [(dx, dy) for dx in (-1, 0, 1) for dy in (-1, 0, 1) if (dx, dy) != (0, 0)]

    def has_device(x, y):
        return (x >= 0) & (x < nx) & (y >= 0) & (y < ny)

    barrier = pltpu.get_barrier_semaphore()
    for dx, dy in directions:
        @pl.when(has_device(gi + dx, gj + dy))
        def _():
            pl.semaphore_signal(barrier, 1, device_id=(gi + dx, gj + dy), device_id_type=mesh_id)

    def pieces(dx, dy):
        return [(0, run) for run in slot_runs(shared_slots(dx, dy))] + [(1, None), (2, None)]

    def edge_pieces(dx, dy):
        from_x = {1: pl.ds(HX + NXL - 1, 1), -1: pl.ds(HX, 1), 0: pl.ds(HX, NXL)}[dx]
        to_x = {1: pl.ds(HX - 1, 1), -1: pl.ds(HX + NXL, 1), 0: pl.ds(HX, NXL)}[dx]
        from_y = {1: pl.ds(NYL - 1, 1), -1: pl.ds(0, 1), 0: pl.ds(0, NYL)}[dy]
        to_y = {1: pl.ds(YE - 1, 1), -1: pl.ds(NYL, 1), 0: pl.ds(0, NYL)}[dy]
        return [(run, from_x, to_x, from_y, to_y) for run in slot_runs(shared_slots(dx, dy))]

    faces = ((1, 0), (-1, 0), (0, 1), (0, -1))
    peers = jnp.int32(0)
    for dx, dy in directions:
        _, to_x = halo_range(dx, NXL, HX)
        _, to_y = halo_rows(dy, NYL, HY, YE)
        from_here = has_device(gi - dx, gj - dy)
        peers = peers + from_here.astype(jnp.int32)
        unshared = [s for s in range(8) if s not in shared_slots(dx, dy)]
        for run in slot_runs(unshared):
            window = halo_window(eb, to_x, to_y, run)
            window[...] = jnp.zeros(window.shape, window.dtype)

        @pl.when(jnp.logical_not(from_here))
        def _():
            for a in range(3):
                window = halo_window(targets[a], to_x, to_y)
                window[...] = jnp.zeros(window.shape, window.dtype)

    if NYL + HY < YE - HY:
        junction = pl.ds(NYL + HY, YE - 2 * HY - NYL)
        for a in range(3):
            window = halo_window(targets[a], pl.ds(0, XE), junction)
            window[...] = jnp.zeros(window.shape, window.dtype)
    window = wc.at[:, pl.ds(HX, NXL), pl.ds(NYL, YE - NYL), :]
    window[...] = jnp.zeros(window.shape, window.dtype)
    for dx, dy in faces:
        @pl.when(jnp.logical_not(has_device(gi - dx, gj - dy)))
        def _():
            for run, _, to_x, _, to_y in edge_pieces(dx, dy):
                window = wc.at[run, to_x, to_y, :]
                window[...] = jnp.zeros(window.shape, window.dtype)

    coarse_routes = ((2, 1, 0), (1, 0, 1), (3, 1, 1))
    for k, (_, dx, dy) in enumerate(coarse_routes):
        @pl.when(jnp.logical_not(has_device(gi - dx, gj - dy)))
        def _():
            received[k] = jnp.zeros(received.shape[1:], received.dtype)

    pl.semaphore_wait(barrier, peers)

    def remote_copy(k, p, dx, dy, target_x, target_y):
        from_x, to_x = halo_range(dx, NXL, HX)
        from_y, to_y = halo_rows(dy, NYL, HY, YE)
        a, run = pieces(dx, dy)[p]
        return pltpu.make_async_remote_copy(
            src_ref=halo_window(sources[a], from_x, from_y, run),
            dst_ref=halo_window(targets[a], to_x, to_y, run),
            send_sem=send_sem.at[4 * k + p],
            recv_sem=recv_sem.at[4 * k + p],
            device_id=(target_x, target_y),
            device_id_type=mesh_id,
        )

    for k, (dx, dy) in enumerate(directions):
        @pl.when(has_device(gi + dx, gj + dy))
        def _():
            for p in range(len(pieces(dx, dy))):
                remote_copy(k, p, dx, dy, gi + dx, gj + dy).start()

    def wait_halo(chosen):
        for k, (dx, dy) in enumerate(directions):
            if not chosen(dx, dy):
                continue

            @pl.when(has_device(gi + dx, gj + dy))
            def _():
                for p in range(len(pieces(dx, dy))):
                    remote_copy(k, p, dx, dy, gi + dx, gj + dy).wait_send()

            @pl.when(has_device(gi - dx, gj - dy))
            def _():
                for p in range(len(pieces(dx, dy))):
                    remote_copy(k, p, dx, dy, gi - dx, gj - dy).wait_recv()

    row = lax.broadcasted_iota(jnp.int32, (YE, L), 0)
    lane = lax.broadcasted_iota(jnp.int32, (YE, L), 1)
    m_yhi = (row == NYL - 1) | (row == YE - 1)
    m_ylo = (row == 0) | (row == NYL)
    rz = lane & (CB - 1)
    m_zhi = rz == CB - 1
    m_zlo = rz == 0
    m_rows = row < NYL
    block_y = gj + jnp.where(row < NYL, 0, jnp.where(row < YE - HY, 1, -1))
    global_y = jnp.where(row < YE - HY, gj * NYL + row, gj * NYL + row - YE)
    inside_y = (global_y >= 0) & (global_y < ny * NYL)
    node_y = block_y + 1 < ny
    node_z = (lane >> 4) + 1 < L // CB

    def lookup(x, carry):
        labels = el[x]
        perm = jnp.zeros((YE, L), jnp.float32)
        for c in range(class_perm.shape[0]):
            perm = jnp.where(labels == c, class_perm[c], perm)
        global_x = gi * NXL + x - HX
        inside = inside_y & (global_x >= 0) & (global_x < nx * NXL)
        pm[x] = jnp.where(inside, perm, 0.0)
        return carry

    for local_copy in local_copies:
        local_copy.wait()
    wait_halo(lambda dx, dy: dx == 0)
    lax.fori_loop(HX, HX + NXL, lookup, 0)

    def xplace(x):
        return (x + (CB - HX)) & (CB - 1)

    def pre(x, carry):
        pc = pm[x]
        pxp = jnp.where(x + 1 < XE, pm[jnp.minimum(x + 1, XE - 1)], 0.0)
        pxm = jnp.where(x >= 1, pm[jnp.maximum(x - 1, 0)], 0.0)
        pyp = pltpu.roll(pc, YE - 1, 0)
        pym = pltpu.roll(pc, 1, 0)
        pzp = pltpu.roll(pc, L - 1, 1)
        pzm = pltpu.roll(pc, 1, 1)
        t_xp = conductance(pc, pxp)
        t_xm = conductance(pc, pxm)
        t_yp = conductance(pc, pyp)
        t_ym = conductance(pc, pym)
        t_zp = jnp.where(lane == L - 1, 0.0, conductance(pc, pzp))
        t_zm = jnp.where(lane == 0, 0.0, conductance(pc, pzm))
        diag = t_xp + t_xm + t_yp + t_ym + t_zp + t_zm
        inv = 1.0 / jnp.where(diag > 0.0, diag, 1.0)
        aux[0, x] = diag
        aux[1, x] = 1.0 - omega_jacobi * diag * inv
        scale = omega_jacobi * inv
        cx_hi = xplace(x) == CB - 1
        cx_lo = xplace(x) == 0
        faces_t = (
            t_xp, jnp.where(cx_hi, 0.0, t_xp), t_xm, jnp.where(cx_lo, 0.0, t_xm),
            t_yp, jnp.where(m_yhi, 0.0, t_yp), t_ym, jnp.where(m_ylo, 0.0, t_ym),
            t_zp, jnp.where(m_zhi, 0.0, t_zp), t_zm, jnp.where(m_zlo, 0.0, t_zm),
        )
        for f, t in enumerate(faces_t):
            tt[f, x] = t
            ts[f, x] = t * scale
        return carry

    def pre_w(x, carry):
        sup = es[x]
        node_x = gi + ((x + (CB - HX)) >> 4) < nx
        for s in range(8):
            bx, by, bz = corner_of(s)
            keep = ((sup >> s) & 1) > 0
            if bx:
                keep = keep & node_x
            if by:
                keep = keep & node_y
            if bz:
                keep = keep & node_z
            v = jnp.where(keep, 1.0, 0.0)
            valid[s, x] = v
            wa[s, x] = eb[s, x] * v
        return carry

    lax.fori_loop(HX, HX + NXL, pre_w, 0)
    lax.fori_loop(HX + 1, HX + NXL - 1, pre, 0)

    def inflow_of(src, x, s, c, tt=tt):
        bx, by, bz = corner_of(s)
        cx_hi = xplace(x) == CB - 1
        cx_lo = xplace(x) == 0
        if bx:
            xp = src[jnp.where(cx_hi, s ^ 4, s), x + 1]
            t1 = tt[0, x]
            xm = src[s, x - 1]
            t2 = tt[3, x]
        else:
            xp = src[s, x + 1]
            t1 = tt[1, x]
            xm = src[jnp.where(cx_lo, s ^ 4, s), x - 1]
            t2 = tt[2, x]
        if by:
            yp = pltpu.roll(jnp.where(m_ylo, src[s ^ 2, x], c), YE - 1, 0)
            t3 = tt[4, x]
            ym = pltpu.roll(c, 1, 0)
            t4 = tt[7, x]
        else:
            yp = pltpu.roll(c, YE - 1, 0)
            t3 = tt[5, x]
            ym = pltpu.roll(jnp.where(m_yhi, src[s ^ 2, x], c), 1, 0)
            t4 = tt[6, x]
        if bz:
            zp = pltpu.roll(jnp.where(m_zlo, src[s ^ 1, x], c), L - 1, 1)
            t5 = tt[8, x]
            zm = pltpu.roll(c, 1, 1)
            t6 = tt[11, x]
        else:
            zp = pltpu.roll(c, L - 1, 1)
            t5 = tt[9, x]
            zm = pltpu.roll(jnp.where(m_zhi, src[s ^ 1, x], c), 1, 1)
            t6 = tt[10, x]
        return t1 * xp + t2 * xm + t3 * yp + t4 * ym + t5 * zp + t6 * zm

    def sweep(src, dst, lo, hi):
        def body(x, carry):
            keep = aux[1, x]
            for s in range(8):
                c = src[s, x]
                inflow = inflow_of(src, x, s, c, ts)
                dst[s, x] = (c * keep + inflow) * valid[s, x]
            return carry

        lax.fori_loop(lo, hi, body, 0)

    bufs = (wa, wb)
    for step in range(ITERS):
        sweep(bufs[step % 2], bufs[(step + 1) % 2], HX + step + 1, HX + NXL - step - 1)
    wait_halo(lambda dx, dy: dx != 0)
    lax.fori_loop(0, HX, lookup, 0)
    lax.fori_loop(HX + NXL, XE, lookup, 0)
    lax.fori_loop(0, HX, pre_w, 0)
    lax.fori_loop(HX + NXL, XE, pre_w, 0)
    lax.fori_loop(0, HX + 1, pre, 0)
    lax.fori_loop(HX + NXL - 1, XE, pre, 0)
    for step in range(ITERS):
        sweep(bufs[step % 2], bufs[(step + 1) % 2], step + 1, HX + step + 1)
        sweep(bufs[step % 2], bufs[(step + 1) % 2], HX + NXL - step - 1, XE - step - 1)
    last = bufs[ITERS % 2]
    basis_buf = wc

    def normalize(x, carry):
        vals = [last[s, x] for s in range(8)]
        total = vals[0]
        for s in range(1, 8):
            total = total + vals[s]
        scale = jnp.maximum(total, renorm_floor)
        for s in range(8):
            basis_buf[s, x, pl.ds(0, NYL), :] = (vals[s] / scale)[:NYL, :]
        return carry

    lax.fori_loop(HX, HX + NXL, normalize, 0)

    def edge_copy(k, p, dx, dy, target_x, target_y):
        run, from_x, to_x, from_y, to_y = edge_pieces(dx, dy)[p]
        return pltpu.make_async_remote_copy(
            src_ref=wc.at[run, from_x, from_y, :],
            dst_ref=wc.at[run, to_x, to_y, :],
            send_sem=edge_send.at[2 * k + p],
            recv_sem=edge_recv.at[2 * k + p],
            device_id=(target_x, target_y),
            device_id_type=mesh_id,
        )

    for k, (dx, dy) in enumerate(faces):
        @pl.when(has_device(gi + dx, gj + dy))
        def _():
            for p in range(len(edge_pieces(dx, dy))):
                edge_copy(k, p, dx, dy, gi + dx, gj + dy).start()

    for k, (dx, dy) in enumerate(faces):
        @pl.when(has_device(gi + dx, gj + dy))
        def _():
            for p in range(len(edge_pieces(dx, dy))):
                edge_copy(k, p, dx, dy, gi + dx, gj + dy).wait_send()

        @pl.when(has_device(gi - dx, gj - dy))
        def _():
            for p in range(len(edge_pieces(dx, dy))):
                edge_copy(k, p, dx, dy, gi - dx, gj - dy).wait_recv()

    def image(x, carry):
        diag = aux[0, x]
        for s in range(8):
            c = basis_buf[s, x]
            inflow = inflow_of(basis_buf, x, s, c)
            img[s, x - HX] = jnp.where(m_rows, diag * c - inflow, 0.0)
            basis_ref[s, x - HX] = c[:NYL, :]
        return carry

    lax.fori_loop(HX, HX + NXL, image, 0)

    def pair_rows(s1):
        def pair_sums(x, acc):
            b = basis_buf[s1, x + HX]
            return tuple(acc[s2] + b * img[s2, x] for s2 in range(8))

        acc = lax.fori_loop(
            0, NXL, pair_sums, tuple(jnp.zeros((YE, L), jnp.float32) for _ in range(8))
        )
        for s2 in range(8):
            prod_ref[pl.ds(s1 * 8 + s2, 1), :] = jnp.sum(acc[s2], axis=0, keepdims=True)

    nbz = L // CB
    node = lax.broadcasted_iota(jnp.int32, (nbz, L), 0)
    block = lax.broadcasted_iota(jnp.int32, (nbz, L), 1) >> 4
    same_node = jnp.where(block == node, 1.0, 0.0)
    node_above = jnp.where(block + 1 == node, 1.0, 0.0)
    along_lanes = (((1,), (1,)), ((), ()))
    exact = lax.Precision.HIGHEST

    def class_terms(c):
        rows = pl.ds(16 * c, 16)
        pairs = prod_ref[rows, :]
        low = lax.dot_general(same_node, pairs, along_lanes, precision=exact,
                              preferred_element_type=jnp.float32)
        high = lax.dot_general(node_above, pairs, along_lanes, precision=exact,
                               preferred_element_type=jnp.float32)
        terms[c] = jnp.dot(low, placing[c, 0, rows, :], precision=exact,
                           preferred_element_type=jnp.float32) + jnp.dot(
            high, placing[c, 1, rows, :], precision=exact, preferred_element_type=jnp.float32)

    def coarse_copy(k, c, target_x, target_y):
        return pltpu.make_async_remote_copy(
            src_ref=terms.at[c],
            dst_ref=received.at[k],
            send_sem=coarse_send.at[k],
            recv_sem=coarse_recv.at[k],
            device_id=(target_x, target_y),
            device_id_type=mesh_id,
        )

    for s1 in range(2, 8):
        pair_rows(s1)
    for c in range(1, 4):
        class_terms(c)
    for k, (c, dx, dy) in enumerate(coarse_routes):
        @pl.when(has_device(gi + dx, gj + dy))
        def _():
            coarse_copy(k, c, gi + dx, gj + dy).start()

    for s1 in range(2):
        pair_rows(s1)
    class_terms(0)

    for k, (c, dx, dy) in enumerate(coarse_routes):
        @pl.when(has_device(gi + dx, gj + dy))
        def _():
            coarse_copy(k, c, gi + dx, gj + dy).wait_send()

        @pl.when(has_device(gi - dx, gj - dy))
        def _():
            coarse_copy(k, c, gi - dx, gj - dy).wait_recv()

    total = terms[0] + received[0] + received[1] + received[2]
    coarse_ref[...] = total[:, : coarse_ref.shape[1]]


def placing_matrix():
    table = np.zeros((4, 2, 64, 32), np.float32)
    for first_slot in range(8):
        for second_slot in range(8):
            one_x, one_y, one_z = corner_of(first_slot)
            two_x, two_y, two_z = corner_of(second_slot)
            offset_index = 9 * (two_x - one_x + 1) + 3 * (two_y - one_y + 1) + (two_z - one_z + 1)
            table[one_x * 2 + one_y, one_z, first_slot * 8 + second_slot, offset_index] = 1.0
    return table


def shards(initial_basis, labels, class_perm, support):
    size_x, size_y, size_z = labels.shape
    assert size_x == CB and size_y == CB and size_z % CB == 0
    blocks_z = size_z // CB
    nx = lax.axis_size("gx")
    ny = lax.axis_size("gy")
    XE = size_x + 2 * HX
    YE = -(-(size_y + 2 * HY) // 8) * 8
    f32 = jnp.float32
    vmem = pl.BlockSpec(memory_space=pltpu.VMEM)
    blocks_z = size_z // CB
    basis, coarse = pl.pallas_call(
        functools.partial(smooth_kernel, nx, ny),
        out_shape=(
            jax.ShapeDtypeStruct((8, size_x, size_y, size_z), f32),
            jax.ShapeDtypeStruct((blocks_z, 27), f32),
        ),
        in_specs=[vmem, vmem, pl.BlockSpec(memory_space=pltpu.SMEM), vmem, vmem],
        out_specs=(vmem, vmem),
        scratch_shapes=[
            pltpu.VMEM((8, XE, YE, size_z), f32),
            pltpu.VMEM((XE, YE, size_z), jnp.int32),
            pltpu.VMEM((XE, YE, size_z), jnp.int32),
            pltpu.VMEM((XE, YE, size_z), f32),
            pltpu.VMEM((12, XE, YE, size_z), f32),
            pltpu.VMEM((12, XE, YE, size_z), f32),
            pltpu.VMEM((2, XE, YE, size_z), f32),
            pltpu.VMEM((8, XE, YE, size_z), f32),
            pltpu.VMEM((8, XE, YE, size_z), f32),
            pltpu.VMEM((8, XE, YE, size_z), f32),
            pltpu.VMEM((8, XE, YE, size_z), f32),
            pltpu.VMEM((8, size_x, YE, size_z), f32),
            pltpu.VMEM((64, size_z), f32),
            pltpu.VMEM((4, blocks_z, 32), f32),
            pltpu.VMEM((3, blocks_z, 32), f32),
            pltpu.SemaphoreType.DMA((32,)),
            pltpu.SemaphoreType.DMA((32,)),
            pltpu.SemaphoreType.DMA((3,)),
            pltpu.SemaphoreType.DMA((3,)),
            pltpu.SemaphoreType.DMA((3,)),
            pltpu.SemaphoreType.DMA((8,)),
            pltpu.SemaphoreType.DMA((8,)),
        ],
        compiler_params=pltpu.CompilerParams(collective_id=1, has_side_effects=True),
    )(initial_basis, labels, class_perm, support, jnp.asarray(placing_matrix()))
    return (basis, coarse.T.reshape(27, 1, 1, blocks_z))


def solution(mesh):
    return jax.shard_map(
        shards,
        mesh=mesh,
        in_specs=(P(None, "gx", "gy", None), P("gx", "gy", None), P(), P("gx", "gy", None)),
        out_specs=(P(None, "gx", "gy", None), P(None, "gx", "gy", None)),
        check_vma=False,
    )
```

```python
import functools
import numpy as np
import jax
import jax.numpy as jnp
from jax import lax
from jax.experimental import pallas as pl
from jax.experimental.pallas import tpu as pltpu
from jax.sharding import PartitionSpec as P

CB = 16
ITERS = 3
HX = ITERS
HY = ITERS

omega_jacobi = 2.0 / 3.0
renorm_floor = 0.5


def with_halo(block, sides, width):
    for axis, dim in sides:
        count = lax.axis_size(axis)
        forward = [(i, i + 1) for i in range(count - 1)]
        backward = [(target, source) for source, target in forward]
        low = lax.ppermute(
            lax.slice_in_dim(block, block.shape[dim] - width, None, axis=dim), axis, forward
        )
        high = lax.ppermute(lax.slice_in_dim(block, 0, width, axis=dim), axis, backward)
        block = jnp.concatenate([low, block, high], axis=dim)
    return block


def from_behind(shard, axis, by):
    peers = lax.axis_size(axis)
    pairs = [(i, i + by) for i in range(peers) if 0 <= i + by < peers]
    return lax.ppermute(shard, axis, pairs)


def corner_of(slot_index):
    return (slot_index >> 2 & 1, slot_index >> 1 & 1, slot_index & 1)


def conductance(centre, neighbour):
    total_perm = centre + neighbour
    divisor = jnp.where(total_perm > 0.0, total_perm, 1.0)
    return 2.0 * centre * neighbour / divisor


def class_lookup(labels, class_perm):
    classes = jnp.arange(class_perm.shape[0])
    hits = labels[None] == classes[:, None, None, None]
    return jnp.sum(jnp.where(hits, class_perm[:, None, None, None], 0.0), axis=0)


def existing_bits(count_x, count_y, count_z, first_x, first_y, limit_x, limit_y, limit_z):
    block_x = (jnp.arange(count_x) + first_x) // CB
    block_y = (jnp.arange(count_y) + first_y) // CB
    block_z = jnp.arange(count_z) // CB
    bits = jnp.zeros((count_x, count_y, count_z), jnp.int32)
    for slot_index in range(8):
        corner_x, corner_y, corner_z = corner_of(slot_index)
        inside = (
            (block_x + corner_x < limit_x)[:, None, None]
            & (block_y + corner_y < limit_y)[None, :, None]
            & (block_z + corner_z < limit_z)[None, None, :]
        )
        bits = bits | jnp.where(inside, 1 << slot_index, 0)
    return bits


def halo_window(ref, xs, ys, slots=None):
    if len(ref.shape) == 4:
        return ref.at[slots if slots is not None else slice(None), xs, ys, :]
    return ref.at[xs, ys, :]


def halo_range(d, count, halo):
    if d > 0:
        return pl.ds(count - halo, halo), pl.ds(0, halo)
    if d < 0:
        return pl.ds(0, halo), pl.ds(halo + count, halo)
    return pl.ds(0, count), pl.ds(halo, count)


def halo_rows(d, count, halo, total):
    if d > 0:
        return pl.ds(count - halo, halo), pl.ds(total - halo, halo)
    if d < 0:
        return pl.ds(0, halo), pl.ds(count, halo)
    return pl.ds(0, count), pl.ds(0, count)


def slot_runs(slots):
    runs = []
    for s in sorted(slots):
        if runs and runs[-1][1] == s:
            runs[-1][1] = s + 1
        else:
            runs.append([s, s + 1])
    return [pl.ds(lo, hi - lo) for lo, hi in runs]


def shared_slots(dx, dy):
    keep = []
    for s in range(8):
        bx, by, _ = corner_of(s)
        if (dx > 0 and not bx) or (dx < 0 and bx) or (dy > 0 and not by) or (dy < 0 and by):
            continue
        keep.append(s)
    return keep


def smooth_kernel(
    nx, ny,
    basis_in, labels_in, class_perm, support_in, placing, basis_ref, coarse_ref,
    eb, el, es, pm, tt, ts, aux, valid, wa, wb, wc, img, prod_ref, terms, received,
    send_sem, recv_sem, local_sem, coarse_send, coarse_recv, edge_send, edge_recv,
):
    gi = lax.axis_index("gx")
    gj = lax.axis_index("gy")
    _, XE, YE, L = eb.shape
    NXL = basis_ref.shape[1]
    NYL = basis_ref.shape[2]
    mesh_id = pl.DeviceIdType.MESH
    sources = (basis_in, labels_in, support_in)
    targets = (eb, el, es)
    local_copies = []
    for a in range(3):
        local_copy = pltpu.make_async_copy(
            sources[a], halo_window(targets[a], pl.ds(HX, NXL), pl.ds(0, NYL)), local_sem.at[a]
        )
        local_copy.start()
        local_copies.append(local_copy)

    directions = [(dx, dy) for dx in (-1, 0, 1) for dy in (-1, 0, 1) if (dx, dy) != (0, 0)]

    def has_device(x, y):
        return (x >= 0) & (x < nx) & (y >= 0) & (y < ny)

    barrier = pltpu.get_barrier_semaphore()
    for dx, dy in directions:
        @pl.when(has_device(gi + dx, gj + dy))
        def _():
            pl.semaphore_signal(barrier, 1, device_id=(gi + dx, gj + dy), device_id_type=mesh_id)

    def pieces(dx, dy):
        return [(0, run) for run in slot_runs(shared_slots(dx, dy))] + [(1, None), (2, None)]

    def edge_pieces(dx, dy):
        from_x = {1: pl.ds(HX + NXL - 1, 1), -1: pl.ds(HX, 1), 0: pl.ds(HX, NXL)}[dx]
        to_x = {1: pl.ds(HX - 1, 1), -1: pl.ds(HX + NXL, 1), 0: pl.ds(HX, NXL)}[dx]
        from_y = {1: pl.ds(NYL - 1, 1), -1: pl.ds(0, 1), 0: pl.ds(0, NYL)}[dy]
        to_y = {1: pl.ds(YE - 1, 1), -1: pl.ds(NYL, 1), 0: pl.ds(0, NYL)}[dy]
        return [(run, from_x, to_x, from_y, to_y) for run in slot_runs(shared_slots(dx, dy))]

    faces = ((1, 0), (-1, 0), (0, 1), (0, -1))
    peers = jnp.int32(0)
    for dx, dy in directions:
        _, to_x = halo_range(dx, NXL, HX)
        _, to_y = halo_rows(dy, NYL, HY, YE)
        from_here = has_device(gi - dx, gj - dy)
        peers = peers + from_here.astype(jnp.int32)
        unshared = [s for s in range(8) if s not in shared_slots(dx, dy)]
        for run in slot_runs(unshared):
            window = halo_window(eb, to_x, to_y, run)
            window[...] = jnp.zeros(window.shape, window.dtype)

        @pl.when(jnp.logical_not(from_here))
        def _():
            for a in range(3):
                window = halo_window(targets[a], to_x, to_y)
                window[...] = jnp.zeros(window.shape, window.dtype)

    if NYL + HY < YE - HY:
        junction = pl.ds(NYL + HY, YE - 2 * HY - NYL)
        for a in range(3):
            window = halo_window(targets[a], pl.ds(0, XE), junction)
            window[...] = jnp.zeros(window.shape, window.dtype)
    window = wc.at[:, pl.ds(HX, NXL), pl.ds(NYL, YE - NYL), :]
    window[...] = jnp.zeros(window.shape, window.dtype)
    for dx, dy in faces:
        @pl.when(jnp.logical_not(has_device(gi - dx, gj - dy)))
        def _():
            for run, _, to_x, _, to_y in edge_pieces(dx, dy):
                window = wc.at[run, to_x, to_y, :]
                window[...] = jnp.zeros(window.shape, window.dtype)

    coarse_routes = ((2, 1, 0), (1, 0, 1), (3, 1, 1))
    for k, (_, dx, dy) in enumerate(coarse_routes):
        @pl.when(jnp.logical_not(has_device(gi - dx, gj - dy)))
        def _():
            received[k] = jnp.zeros(received.shape[1:], received.dtype)

    pl.semaphore_wait(barrier, peers)

    def remote_copy(k, p, dx, dy, target_x, target_y):
        from_x, to_x = halo_range(dx, NXL, HX)
        from_y, to_y = halo_rows(dy, NYL, HY, YE)
        a, run = pieces(dx, dy)[p]
        return pltpu.make_async_remote_copy(
            src_ref=halo_window(sources[a], from_x, from_y, run),
            dst_ref=halo_window(targets[a], to_x, to_y, run),
            send_sem=send_sem.at[4 * k + p],
            recv_sem=recv_sem.at[4 * k + p],
            device_id=(target_x, target_y),
            device_id_type=mesh_id,
        )

    for k, (dx, dy) in enumerate(directions):
        @pl.when(has_device(gi + dx, gj + dy))
        def _():
            for p in range(len(pieces(dx, dy))):
                remote_copy(k, p, dx, dy, gi + dx, gj + dy).start()

    def wait_halo(chosen):
        for k, (dx, dy) in enumerate(directions):
            if not chosen(dx, dy):
                continue

            @pl.when(has_device(gi + dx, gj + dy))
            def _():
                for p in range(len(pieces(dx, dy))):
                    remote_copy(k, p, dx, dy, gi + dx, gj + dy).wait_send()

            @pl.when(has_device(gi - dx, gj - dy))
            def _():
                for p in range(len(pieces(dx, dy))):
                    remote_copy(k, p, dx, dy, gi - dx, gj - dy).wait_recv()

    row = lax.broadcasted_iota(jnp.int32, (YE, L), 0)
    lane = lax.broadcasted_iota(jnp.int32, (YE, L), 1)
    m_yhi = (row == NYL - 1) | (row == YE - 1)
    m_ylo = (row == 0) | (row == NYL)
    rz = lane & (CB - 1)
    m_zhi = rz == CB - 1
    m_zlo = rz == 0
    m_rows = row < NYL
    block_y = gj + jnp.where(row < NYL, 0, jnp.where(row < YE - HY, 1, -1))
    global_y = jnp.where(row < YE - HY, gj * NYL + row, gj * NYL + row - YE)
    inside_y = (global_y >= 0) & (global_y < ny * NYL)
    node_y = block_y + 1 < ny
    node_z = (lane >> 4) + 1 < L // CB

    def lookup(x, carry):
        labels = el[x]
        perm = jnp.zeros((YE, L), jnp.float32)
        for c in range(class_perm.shape[0]):
            perm = jnp.where(labels == c, class_perm[c], perm)
        global_x = gi * NXL + x - HX
        inside = inside_y & (global_x >= 0) & (global_x < nx * NXL)
        pm[x] = jnp.where(inside, perm, 0.0)
        return carry

    for local_copy in local_copies:
        local_copy.wait()
    wait_halo(lambda dx, dy: dx == 0)
    lax.fori_loop(HX, HX + NXL, lookup, 0)

    def xplace(x):
        return (x + (CB - HX)) & (CB - 1)

    def pre(x, carry):
        pc = pm[x]
        pxp = jnp.where(x + 1 < XE, pm[jnp.minimum(x + 1, XE - 1)], 0.0)
        pxm = jnp.where(x >= 1, pm[jnp.maximum(x - 1, 0)], 0.0)
        pyp = pltpu.roll(pc, YE - 1, 0)
        pym = pltpu.roll(pc, 1, 0)
        pzp = pltpu.roll(pc, L - 1, 1)
        pzm = pltpu.roll(pc, 1, 1)
        t_xp = conductance(pc, pxp)
        t_xm = conductance(pc, pxm)
        t_yp = conductance(pc, pyp)
        t_ym = conductance(pc, pym)
        t_zp = jnp.where(lane == L - 1, 0.0, conductance(pc, pzp))
        t_zm = jnp.where(lane == 0, 0.0, conductance(pc, pzm))
        diag = t_xp + t_xm + t_yp + t_ym + t_zp + t_zm
        inv = 1.0 / jnp.where(diag > 0.0, diag, 1.0)
        aux[0, x] = diag
        aux[1, x] = 1.0 - omega_jacobi * diag * inv
        scale = omega_jacobi * inv
        cx_hi = xplace(x) == CB - 1
        cx_lo = xplace(x) == 0
        faces_t = (
            t_xp, jnp.where(cx_hi, 0.0, t_xp), t_xm, jnp.where(cx_lo, 0.0, t_xm),
            t_yp, jnp.where(m_yhi, 0.0, t_yp), t_ym, jnp.where(m_ylo, 0.0, t_ym),
            t_zp, jnp.where(m_zhi, 0.0, t_zp), t_zm, jnp.where(m_zlo, 0.0, t_zm),
        )
        for f, t in enumerate(faces_t):
            tt[f, x] = t
            ts[f, x] = t * scale
        return carry

    def pre_w(x, carry):
        sup = es[x]
        node_x = gi + ((x + (CB - HX)) >> 4) < nx
        for s in range(8):
            bx, by, bz = corner_of(s)
            keep = ((sup >> s) & 1) > 0
            if bx:
                keep = keep & node_x
            if by:
                keep = keep & node_y
            if bz:
                keep = keep & node_z
            v = jnp.where(keep, 1.0, 0.0)
            valid[s, x] = v
            wa[s, x] = eb[s, x] * v
        return carry

    lax.fori_loop(HX, HX + NXL, pre_w, 0)
    lax.fori_loop(HX + 1, HX + NXL - 1, pre, 0)

    def inflow_of(src, x, s, c, tt=tt):
        bx, by, bz = corner_of(s)
        cx_hi = xplace(x) == CB - 1
        cx_lo = xplace(x) == 0
        if bx:
            xp = src[jnp.where(cx_hi, s ^ 4, s), x + 1]
            t1 = tt[0, x]
            xm = src[s, x - 1]
            t2 = tt[3, x]
        else:
            xp = src[s, x + 1]
            t1 = tt[1, x]
            xm = src[jnp.where(cx_lo, s ^ 4, s), x - 1]
            t2 = tt[2, x]
        if by:
            yp = pltpu.roll(jnp.where(m_ylo, src[s ^ 2, x], c), YE - 1, 0)
            t3 = tt[4, x]
            ym = pltpu.roll(c, 1, 0)
            t4 = tt[7, x]
        else:
            yp = pltpu.roll(c, YE - 1, 0)
            t3 = tt[5, x]
            ym = pltpu.roll(jnp.where(m_yhi, src[s ^ 2, x], c), 1, 0)
            t4 = tt[6, x]
        if bz:
            zp = pltpu.roll(jnp.where(m_zlo, src[s ^ 1, x], c), L - 1, 1)
            t5 = tt[8, x]
            zm = pltpu.roll(c, 1, 1)
            t6 = tt[11, x]
        else:
            zp = pltpu.roll(c, L - 1, 1)
            t5 = tt[9, x]
            zm = pltpu.roll(jnp.where(m_zhi, src[s ^ 1, x], c), 1, 1)
            t6 = tt[10, x]
        return t1 * xp + t2 * xm + t3 * yp + t4 * ym + t5 * zp + t6 * zm

    def sweep(src, dst, lo, hi):
        def body(x, carry):
            keep = aux[1, x]
            for s in range(8):
                c = src[s, x]
                inflow = inflow_of(src, x, s, c, ts)
                dst[s, x] = (c * keep + inflow) * valid[s, x]
            return carry

        lax.fori_loop(lo, hi, body, 0)

    bufs = (wa, wb)
    for step in range(ITERS):
        sweep(bufs[step % 2], bufs[(step + 1) % 2], HX + step + 1, HX + NXL - step - 1)
    wait_halo(lambda dx, dy: dx != 0)
    lax.fori_loop(0, HX, lookup, 0)
    lax.fori_loop(HX + NXL, XE, lookup, 0)
    lax.fori_loop(0, HX, pre_w, 0)
    lax.fori_loop(HX + NXL, XE, pre_w, 0)
    lax.fori_loop(0, HX + 1, pre, 0)
    lax.fori_loop(HX + NXL - 1, XE, pre, 0)
    for step in range(ITERS):
        sweep(bufs[step % 2], bufs[(step + 1) % 2], step + 1, HX + step + 1)
        sweep(bufs[step % 2], bufs[(step + 1) % 2], HX + NXL - step - 1, XE - step - 1)
    last = bufs[ITERS % 2]
    basis_buf = wc

    def normalize(x, carry):
        vals = [last[s, x] for s in range(8)]
        total = vals[0]
        for s in range(1, 8):
            total = total + vals[s]
        scale = jnp.maximum(total, renorm_floor)
        for s in range(8):
            basis_buf[s, x, pl.ds(0, NYL), :] = (vals[s] / scale)[:NYL, :]
        return carry

    lax.fori_loop(HX, HX + NXL, normalize, 0)
    out_copy = pltpu.make_async_copy(
        wc.at[:, pl.ds(HX, NXL), pl.ds(0, NYL), :], basis_ref, local_sem.at[3]
    )
    out_copy.start()

    def edge_copy(k, p, dx, dy, target_x, target_y):
        run, from_x, to_x, from_y, to_y = edge_pieces(dx, dy)[p]
        return pltpu.make_async_remote_copy(
            src_ref=wc.at[run, from_x, from_y, :],
            dst_ref=wc.at[run, to_x, to_y, :],
            send_sem=edge_send.at[2 * k + p],
            recv_sem=edge_recv.at[2 * k + p],
            device_id=(target_x, target_y),
            device_id_type=mesh_id,
        )

    for k, (dx, dy) in enumerate(faces):
        @pl.when(has_device(gi + dx, gj + dy))
        def _():
            for p in range(len(edge_pieces(dx, dy))):
                edge_copy(k, p, dx, dy, gi + dx, gj + dy).start()

    for k, (dx, dy) in enumerate(faces):
        @pl.when(has_device(gi + dx, gj + dy))
        def _():
            for p in range(len(edge_pieces(dx, dy))):
                edge_copy(k, p, dx, dy, gi + dx, gj + dy).wait_send()

        @pl.when(has_device(gi - dx, gj - dy))
        def _():
            for p in range(len(edge_pieces(dx, dy))):
                edge_copy(k, p, dx, dy, gi - dx, gj - dy).wait_recv()

    def image(x, carry):
        diag = aux[0, x]
        for s in range(8):
            c = basis_buf[s, x]
            inflow = inflow_of(basis_buf, x, s, c)
            img[s, x - HX] = jnp.where(m_rows, diag * c - inflow, 0.0)
        return carry

    lax.fori_loop(HX, HX + NXL, image, 0)

    def pair_rows(s1):
        def pair_sums(x, acc):
            b = basis_buf[s1, x + HX]
            return tuple(acc[s2] + b * img[s2, x] for s2 in range(8))

        acc = lax.fori_loop(
            0, NXL, pair_sums, tuple(jnp.zeros((YE, L), jnp.float32) for _ in range(8))
        )
        for s2 in range(8):
            prod_ref[pl.ds(s1 * 8 + s2, 1), :] = jnp.sum(acc[s2], axis=0, keepdims=True)

    nbz = L // CB
    node = lax.broadcasted_iota(jnp.int32, (nbz, L), 0)
    block = lax.broadcasted_iota(jnp.int32, (nbz, L), 1) >> 4
    same_node = jnp.where(block == node, 1.0, 0.0)
    node_above = jnp.where(block + 1 == node, 1.0, 0.0)
    along_lanes = (((1,), (1,)), ((), ()))
    exact = lax.Precision.HIGHEST

    def class_terms(c):
        rows = pl.ds(16 * c, 16)
        pairs = prod_ref[rows, :]
        low = lax.dot_general(same_node, pairs, along_lanes, precision=exact,
                              preferred_element_type=jnp.float32)
        high = lax.dot_general(node_above, pairs, along_lanes, precision=exact,
                               preferred_element_type=jnp.float32)
        terms[c] = jnp.dot(low, placing[c, 0, rows, :], precision=exact,
                           preferred_element_type=jnp.float32) + jnp.dot(
            high, placing[c, 1, rows, :], precision=exact, preferred_element_type=jnp.float32)

    def coarse_copy(k, c, target_x, target_y):
        return pltpu.make_async_remote_copy(
            src_ref=terms.at[c],
            dst_ref=received.at[k],
            send_sem=coarse_send.at[k],
            recv_sem=coarse_recv.at[k],
            device_id=(target_x, target_y),
            device_id_type=mesh_id,
        )

    for s1 in range(2, 8):
        pair_rows(s1)
    for c in range(1, 4):
        class_terms(c)
    for k, (c, dx, dy) in enumerate(coarse_routes):
        @pl.when(has_device(gi + dx, gj + dy))
        def _():
            coarse_copy(k, c, gi + dx, gj + dy).start()

    for s1 in range(2):
        pair_rows(s1)
    class_terms(0)

    for k, (c, dx, dy) in enumerate(coarse_routes):
        @pl.when(has_device(gi + dx, gj + dy))
        def _():
            coarse_copy(k, c, gi + dx, gj + dy).wait_send()

        @pl.when(has_device(gi - dx, gj - dy))
        def _():
            coarse_copy(k, c, gi - dx, gj - dy).wait_recv()

    out_copy.wait()
    total = terms[0] + received[0] + received[1] + received[2]
    coarse_ref[...] = total[:, : coarse_ref.shape[1]]


def placing_matrix():
    table = np.zeros((4, 2, 64, 32), np.float32)
    for first_slot in range(8):
        for second_slot in range(8):
            one_x, one_y, one_z = corner_of(first_slot)
            two_x, two_y, two_z = corner_of(second_slot)
            offset_index = 9 * (two_x - one_x + 1) + 3 * (two_y - one_y + 1) + (two_z - one_z + 1)
            table[one_x * 2 + one_y, one_z, first_slot * 8 + second_slot, offset_index] = 1.0
    return table


def shards(initial_basis, labels, class_perm, support):
    size_x, size_y, size_z = labels.shape
    assert size_x == CB and size_y == CB and size_z % CB == 0
    blocks_z = size_z // CB
    nx = lax.axis_size("gx")
    ny = lax.axis_size("gy")
    XE = size_x + 2 * HX
    YE = -(-(size_y + 2 * HY) // 8) * 8
    f32 = jnp.float32
    vmem = pl.BlockSpec(memory_space=pltpu.VMEM)
    blocks_z = size_z // CB
    basis, coarse = pl.pallas_call(
        functools.partial(smooth_kernel, nx, ny),
        out_shape=(
            jax.ShapeDtypeStruct((8, size_x, size_y, size_z), f32),
            jax.ShapeDtypeStruct((blocks_z, 27), f32),
        ),
        in_specs=[vmem, vmem, pl.BlockSpec(memory_space=pltpu.SMEM), vmem, vmem],
        out_specs=(pl.BlockSpec(memory_space=pl.ANY), vmem),
        scratch_shapes=[
            pltpu.VMEM((8, XE, YE, size_z), f32),
            pltpu.VMEM((XE, YE, size_z), jnp.int32),
            pltpu.VMEM((XE, YE, size_z), jnp.int32),
            pltpu.VMEM((XE, YE, size_z), f32),
            pltpu.VMEM((12, XE, YE, size_z), f32),
            pltpu.VMEM((12, XE, YE, size_z), f32),
            pltpu.VMEM((2, XE, YE, size_z), f32),
            pltpu.VMEM((8, XE, YE, size_z), f32),
            pltpu.VMEM((8, XE, YE, size_z), f32),
            pltpu.VMEM((8, XE, YE, size_z), f32),
            pltpu.VMEM((8, XE, YE, size_z), f32),
            pltpu.VMEM((8, size_x, YE, size_z), f32),
            pltpu.VMEM((64, size_z), f32),
            pltpu.VMEM((4, blocks_z, 32), f32),
            pltpu.VMEM((3, blocks_z, 32), f32),
            pltpu.SemaphoreType.DMA((32,)),
            pltpu.SemaphoreType.DMA((32,)),
            pltpu.SemaphoreType.DMA((4,)),
            pltpu.SemaphoreType.DMA((3,)),
            pltpu.SemaphoreType.DMA((3,)),
            pltpu.SemaphoreType.DMA((8,)),
            pltpu.SemaphoreType.DMA((8,)),
        ],
        compiler_params=pltpu.CompilerParams(collective_id=1, has_side_effects=True),
    )(initial_basis, labels, class_perm, support, jnp.asarray(placing_matrix()))
    return (basis, coarse.T.reshape(27, 1, 1, blocks_z))


def solution(mesh):
    return jax.shard_map(
        shards,
        mesh=mesh,
        in_specs=(P(None, "gx", "gy", None), P("gx", "gy", None), P(), P("gx", "gy", None)),
        out_specs=(P(None, "gx", "gy", None), P(None, "gx", "gy", None)),
        check_vma=False,
    )
```

```python
import functools
import numpy as np
import jax
import jax.numpy as jnp
from jax import lax
from jax.experimental import pallas as pl
from jax.experimental.pallas import tpu as pltpu
from jax.sharding import PartitionSpec as P

CB = 16
ITERS = 3
HX = ITERS
HY = ITERS

omega_jacobi = 2.0 / 3.0
renorm_floor = 0.5


def with_halo(block, sides, width):
    for axis, dim in sides:
        count = lax.axis_size(axis)
        forward = [(i, i + 1) for i in range(count - 1)]
        backward = [(target, source) for source, target in forward]
        low = lax.ppermute(
            lax.slice_in_dim(block, block.shape[dim] - width, None, axis=dim), axis, forward
        )
        high = lax.ppermute(lax.slice_in_dim(block, 0, width, axis=dim), axis, backward)
        block = jnp.concatenate([low, block, high], axis=dim)
    return block


def from_behind(shard, axis, by):
    peers = lax.axis_size(axis)
    pairs = [(i, i + by) for i in range(peers) if 0 <= i + by < peers]
    return lax.ppermute(shard, axis, pairs)


def corner_of(slot_index):
    return (slot_index >> 2 & 1, slot_index >> 1 & 1, slot_index & 1)


def conductance(centre, neighbour):
    total_perm = centre + neighbour
    divisor = jnp.where(total_perm > 0.0, total_perm, 1.0)
    return 2.0 * centre * neighbour / divisor


def class_lookup(labels, class_perm):
    classes = jnp.arange(class_perm.shape[0])
    hits = labels[None] == classes[:, None, None, None]
    return jnp.sum(jnp.where(hits, class_perm[:, None, None, None], 0.0), axis=0)


def existing_bits(count_x, count_y, count_z, first_x, first_y, limit_x, limit_y, limit_z):
    block_x = (jnp.arange(count_x) + first_x) // CB
    block_y = (jnp.arange(count_y) + first_y) // CB
    block_z = jnp.arange(count_z) // CB
    bits = jnp.zeros((count_x, count_y, count_z), jnp.int32)
    for slot_index in range(8):
        corner_x, corner_y, corner_z = corner_of(slot_index)
        inside = (
            (block_x + corner_x < limit_x)[:, None, None]
            & (block_y + corner_y < limit_y)[None, :, None]
            & (block_z + corner_z < limit_z)[None, None, :]
        )
        bits = bits | jnp.where(inside, 1 << slot_index, 0)
    return bits


def halo_window(ref, xs, ys, slots=None):
    if len(ref.shape) == 4:
        return ref.at[slots if slots is not None else slice(None), xs, ys, :]
    return ref.at[xs, ys, :]


def halo_range(d, count, halo):
    if d > 0:
        return pl.ds(count - halo, halo), pl.ds(0, halo)
    if d < 0:
        return pl.ds(0, halo), pl.ds(halo + count, halo)
    return pl.ds(0, count), pl.ds(halo, count)


def halo_rows(d, count, halo, total):
    if d > 0:
        return pl.ds(count - halo, halo), pl.ds(total - halo, halo)
    if d < 0:
        return pl.ds(0, halo), pl.ds(count, halo)
    return pl.ds(0, count), pl.ds(0, count)


def slot_runs(slots):
    runs = []
    for s in sorted(slots):
        if runs and runs[-1][1] == s:
            runs[-1][1] = s + 1
        else:
            runs.append([s, s + 1])
    return [pl.ds(lo, hi - lo) for lo, hi in runs]


def shared_slots(dx, dy):
    keep = []
    for s in range(8):
        bx, by, _ = corner_of(s)
        if (dx > 0 and not bx) or (dx < 0 and bx) or (dy > 0 and not by) or (dy < 0 and by):
            continue
        keep.append(s)
    return keep


def smooth_kernel(
    nx, ny,
    basis_in, labels_in, class_perm, support_in, placing, basis_ref, coarse_ref,
    eb, el, es, pm, tt, ts, aux, valid, wa, wb, wc, img, prod_ref, terms, received,
    send_sem, recv_sem, local_sem, coarse_send, coarse_recv, edge_send, edge_recv,
):
    gi = lax.axis_index("gx")
    gj = lax.axis_index("gy")
    _, XE, YE, L = eb.shape
    NXL = basis_ref.shape[1]
    NYL = basis_ref.shape[2]
    mesh_id = pl.DeviceIdType.MESH
    sources = (basis_in, labels_in, support_in)
    targets = (eb, el, es)
    local_copies = []
    for a in range(3):
        local_copy = pltpu.make_async_copy(
            sources[a], halo_window(targets[a], pl.ds(HX, NXL), pl.ds(0, NYL)), local_sem.at[a]
        )
        local_copy.start()
        local_copies.append(local_copy)

    directions = [(dx, dy) for dx in (-1, 0, 1) for dy in (-1, 0, 1) if (dx, dy) != (0, 0)]

    def has_device(x, y):
        return (x >= 0) & (x < nx) & (y >= 0) & (y < ny)

    barrier = pltpu.get_barrier_semaphore()
    for dx, dy in directions:
        @pl.when(has_device(gi + dx, gj + dy))
        def _():
            pl.semaphore_signal(barrier, 1, device_id=(gi + dx, gj + dy), device_id_type=mesh_id)

    def pieces(dx, dy):
        return [(0, run) for run in slot_runs(shared_slots(dx, dy))] + [(1, None), (2, None)]

    def edge_pieces(dx, dy):
        from_x = {1: pl.ds(HX + NXL - 1, 1), -1: pl.ds(HX, 1), 0: pl.ds(HX, NXL)}[dx]
        to_x = {1: pl.ds(HX - 1, 1), -1: pl.ds(HX + NXL, 1), 0: pl.ds(HX, NXL)}[dx]
        from_y = {1: pl.ds(NYL - 1, 1), -1: pl.ds(0, 1), 0: pl.ds(0, NYL)}[dy]
        to_y = {1: pl.ds(YE - 1, 1), -1: pl.ds(NYL, 1), 0: pl.ds(0, NYL)}[dy]
        return [(run, from_x, to_x, from_y, to_y) for run in slot_runs(shared_slots(dx, dy))]

    faces = ((1, 0), (-1, 0), (0, 1), (0, -1))
    peers = jnp.int32(0)
    for dx, dy in directions:
        _, to_x = halo_range(dx, NXL, HX)
        _, to_y = halo_rows(dy, NYL, HY, YE)
        from_here = has_device(gi - dx, gj - dy)
        peers = peers + from_here.astype(jnp.int32)
        unshared = [s for s in range(8) if s not in shared_slots(dx, dy)]
        for run in slot_runs(unshared):
            window = halo_window(eb, to_x, to_y, run)
            window[...] = jnp.zeros(window.shape, window.dtype)

        @pl.when(jnp.logical_not(from_here))
        def _():
            for a in range(3):
                window = halo_window(targets[a], to_x, to_y)
                window[...] = jnp.zeros(window.shape, window.dtype)

    if NYL + HY < YE - HY:
        junction = pl.ds(NYL + HY, YE - 2 * HY - NYL)
        for a in range(3):
            window = halo_window(targets[a], pl.ds(0, XE), junction)
            window[...] = jnp.zeros(window.shape, window.dtype)
    window = wc.at[:, pl.ds(HX, NXL), pl.ds(NYL, YE - NYL), :]
    window[...] = jnp.zeros(window.shape, window.dtype)
    for dx, dy in faces:
        @pl.when(jnp.logical_not(has_device(gi - dx, gj - dy)))
        def _():
            for run, _, to_x, _, to_y in edge_pieces(dx, dy):
                window = wc.at[run, to_x, to_y, :]
                window[...] = jnp.zeros(window.shape, window.dtype)

    coarse_routes = ((2, 1, 0), (1, 0, 1), (3, 1, 1))
    for k, (_, dx, dy) in enumerate(coarse_routes):
        @pl.when(jnp.logical_not(has_device(gi - dx, gj - dy)))
        def _():
            received[k] = jnp.zeros(received.shape[1:], received.dtype)

    pl.semaphore_wait(barrier, peers)

    def remote_copy(k, p, dx, dy, target_x, target_y):
        from_x, to_x = halo_range(dx, NXL, HX)
        from_y, to_y = halo_rows(dy, NYL, HY, YE)
        a, run = pieces(dx, dy)[p]
        return pltpu.make_async_remote_copy(
            src_ref=halo_window(sources[a], from_x, from_y, run),
            dst_ref=halo_window(targets[a], to_x, to_y, run),
            send_sem=send_sem.at[4 * k + p],
            recv_sem=recv_sem.at[4 * k + p],
            device_id=(target_x, target_y),
            device_id_type=mesh_id,
        )

    for k, (dx, dy) in enumerate(directions):
        @pl.when(has_device(gi + dx, gj + dy))
        def _():
            for p in range(len(pieces(dx, dy))):
                remote_copy(k, p, dx, dy, gi + dx, gj + dy).start()

    def wait_halo(chosen):
        for k, (dx, dy) in enumerate(directions):
            if not chosen(dx, dy):
                continue

            @pl.when(has_device(gi + dx, gj + dy))
            def _():
                for p in range(len(pieces(dx, dy))):
                    remote_copy(k, p, dx, dy, gi + dx, gj + dy).wait_send()

            @pl.when(has_device(gi - dx, gj - dy))
            def _():
                for p in range(len(pieces(dx, dy))):
                    remote_copy(k, p, dx, dy, gi - dx, gj - dy).wait_recv()

    row = lax.broadcasted_iota(jnp.int32, (YE, L), 0)
    lane = lax.broadcasted_iota(jnp.int32, (YE, L), 1)
    m_yhi = (row == NYL - 1) | (row == YE - 1)
    m_ylo = (row == 0) | (row == NYL)
    rz = lane & (CB - 1)
    m_zhi = rz == CB - 1
    m_zlo = rz == 0
    m_rows = row < NYL
    block_y = gj + jnp.where(row < NYL, 0, jnp.where(row < YE - HY, 1, -1))
    global_y = jnp.where(row < YE - HY, gj * NYL + row, gj * NYL + row - YE)
    inside_y = (global_y >= 0) & (global_y < ny * NYL)
    node_y = block_y + 1 < ny
    node_z = (lane >> 4) + 1 < L // CB

    def lookup(x, carry):
        labels = el[x]
        perm = jnp.zeros((YE, L), jnp.float32)
        for c in range(class_perm.shape[0]):
            perm = jnp.where(labels == c, class_perm[c], perm)
        global_x = gi * NXL + x - HX
        inside = inside_y & (global_x >= 0) & (global_x < nx * NXL)
        pm[x] = jnp.where(inside, perm, 0.0)
        return carry

    for local_copy in local_copies:
        local_copy.wait()
    wait_halo(lambda dx, dy: dx == 0)
    lax.fori_loop(HX, HX + NXL, lookup, 0)

    def xplace(x):
        return (x + (CB - HX)) & (CB - 1)

    def pre(x, carry):
        pc = pm[x]
        pxp = jnp.where(x + 1 < XE, pm[jnp.minimum(x + 1, XE - 1)], 0.0)
        pxm = jnp.where(x >= 1, pm[jnp.maximum(x - 1, 0)], 0.0)
        pyp = pltpu.roll(pc, YE - 1, 0)
        pym = pltpu.roll(pc, 1, 0)
        pzp = pltpu.roll(pc, L - 1, 1)
        pzm = pltpu.roll(pc, 1, 1)
        t_xp = conductance(pc, pxp)
        t_xm = conductance(pc, pxm)
        t_yp = conductance(pc, pyp)
        t_ym = conductance(pc, pym)
        t_zp = jnp.where(lane == L - 1, 0.0, conductance(pc, pzp))
        t_zm = jnp.where(lane == 0, 0.0, conductance(pc, pzm))
        diag = t_xp + t_xm + t_yp + t_ym + t_zp + t_zm
        inv = 1.0 / jnp.where(diag > 0.0, diag, 1.0)
        aux[0, x] = diag
        aux[1, x] = 1.0 - omega_jacobi * diag * inv
        scale = omega_jacobi * inv
        cx_hi = xplace(x) == CB - 1
        cx_lo = xplace(x) == 0
        faces_t = (
            t_xp, jnp.where(cx_hi, 0.0, t_xp), t_xm, jnp.where(cx_lo, 0.0, t_xm),
            t_yp, jnp.where(m_yhi, 0.0, t_yp), t_ym, jnp.where(m_ylo, 0.0, t_ym),
            t_zp, jnp.where(m_zhi, 0.0, t_zp), t_zm, jnp.where(m_zlo, 0.0, t_zm),
        )
        for f, t in enumerate(faces_t):
            tt[f, x] = t
            ts[f, x] = t * scale
        return carry

    def pre_w(x, carry):
        sup = es[x]
        node_x = gi + ((x + (CB - HX)) >> 4) < nx
        for s in range(8):
            bx, by, bz = corner_of(s)
            keep = ((sup >> s) & 1) > 0
            if bx:
                keep = keep & node_x
            if by:
                keep = keep & node_y
            if bz:
                keep = keep & node_z
            v = jnp.where(keep, 1.0, 0.0)
            valid[s, x] = v
            wa[s, x] = eb[s, x] * v
        return carry

    lax.fori_loop(HX, HX + NXL, pre_w, 0)
    lax.fori_loop(HX + 1, HX + NXL - 1, pre, 0)

    def inflow_of(src, x, s, c, tt=tt):
        bx, by, bz = corner_of(s)
        cx_hi = xplace(x) == CB - 1
        cx_lo = xplace(x) == 0
        if bx:
            xp = src[jnp.where(cx_hi, s ^ 4, s), x + 1]
            t1 = tt[0, x]
            xm = src[s, x - 1]
            t2 = tt[3, x]
        else:
            xp = src[s, x + 1]
            t1 = tt[1, x]
            xm = src[jnp.where(cx_lo, s ^ 4, s), x - 1]
            t2 = tt[2, x]
        if by:
            yp = pltpu.roll(jnp.where(m_ylo, src[s ^ 2, x], c), YE - 1, 0)
            t3 = tt[4, x]
            ym = pltpu.roll(c, 1, 0)
            t4 = tt[7, x]
        else:
            yp = pltpu.roll(c, YE - 1, 0)
            t3 = tt[5, x]
            ym = pltpu.roll(jnp.where(m_yhi, src[s ^ 2, x], c), 1, 0)
            t4 = tt[6, x]
        if bz:
            zp = pltpu.roll(jnp.where(m_zlo, src[s ^ 1, x], c), L - 1, 1)
            t5 = tt[8, x]
            zm = pltpu.roll(c, 1, 1)
            t6 = tt[11, x]
        else:
            zp = pltpu.roll(c, L - 1, 1)
            t5 = tt[9, x]
            zm = pltpu.roll(jnp.where(m_zhi, src[s ^ 1, x], c), 1, 1)
            t6 = tt[10, x]
        return t1 * xp + t2 * xm + t3 * yp + t4 * ym + t5 * zp + t6 * zm

    def sweep(src, dst, lo, hi):
        def body(x, carry):
            keep = aux[1, x]
            for s in range(8):
                c = src[s, x]
                inflow = inflow_of(src, x, s, c, ts)
                dst[s, x] = (c * keep + inflow) * valid[s, x]
            return carry

        lax.fori_loop(lo, hi, body, 0)

    bufs = (wa, wb)
    for step in range(ITERS):
        sweep(bufs[step % 2], bufs[(step + 1) % 2], HX + step + 1, HX + NXL - step - 1)
    wait_halo(lambda dx, dy: dx != 0)
    lax.fori_loop(0, HX, lookup, 0)
    lax.fori_loop(HX + NXL, XE, lookup, 0)
    lax.fori_loop(0, HX, pre_w, 0)
    lax.fori_loop(HX + NXL, XE, pre_w, 0)
    lax.fori_loop(0, HX + 1, pre, 0)
    lax.fori_loop(HX + NXL - 1, XE, pre, 0)
    for step in range(ITERS):
        sweep(bufs[step % 2], bufs[(step + 1) % 2], step + 1, HX + step + 1)
        sweep(bufs[step % 2], bufs[(step + 1) % 2], HX + NXL - step - 1, XE - step - 1)
    last = bufs[ITERS % 2]
    basis_buf = wc

    def normalize(x, carry):
        vals = [last[s, x] for s in range(8)]
        total = vals[0]
        for s in range(1, 8):
            total = total + vals[s]
        scale = jnp.maximum(total, renorm_floor)
        for s in range(8):
            basis_buf[s, x, pl.ds(0, NYL), :] = (vals[s] / scale)[:NYL, :]
        return carry

    lax.fori_loop(HX, HX + NXL, normalize, 0)
    out_copy = pltpu.make_async_copy(
        wc.at[:, pl.ds(HX, NXL), pl.ds(0, NYL), :], basis_ref, local_sem.at[3]
    )
    out_copy.start()

    def edge_copy(k, p, dx, dy, target_x, target_y):
        run, from_x, to_x, from_y, to_y = edge_pieces(dx, dy)[p]
        return pltpu.make_async_remote_copy(
            src_ref=wc.at[run, from_x, from_y, :],
            dst_ref=wc.at[run, to_x, to_y, :],
            send_sem=edge_send.at[2 * k + p],
            recv_sem=edge_recv.at[2 * k + p],
            device_id=(target_x, target_y),
            device_id_type=mesh_id,
        )

    for k, (dx, dy) in enumerate(faces):
        @pl.when(has_device(gi + dx, gj + dy))
        def _():
            for p in range(len(edge_pieces(dx, dy))):
                edge_copy(k, p, dx, dy, gi + dx, gj + dy).start()

    for k, (dx, dy) in enumerate(faces):
        @pl.when(has_device(gi + dx, gj + dy))
        def _():
            for p in range(len(edge_pieces(dx, dy))):
                edge_copy(k, p, dx, dy, gi + dx, gj + dy).wait_send()

        @pl.when(has_device(gi - dx, gj - dy))
        def _():
            for p in range(len(edge_pieces(dx, dy))):
                edge_copy(k, p, dx, dy, gi - dx, gj - dy).wait_recv()

    def image(x, carry):
        diag = aux[0, x]
        for s in range(8):
            c = basis_buf[s, x]
            inflow = inflow_of(basis_buf, x, s, c)
            img[s, x - HX] = jnp.where(m_rows, diag * c - inflow, 0.0)
        return carry

    lax.fori_loop(HX, HX + NXL, image, 0)

    def pair_rows(s1):
        def pair_sums(x, acc):
            b = basis_buf[s1, x + HX]
            return tuple(acc[s2] + b * img[s2, x] for s2 in range(8))

        acc = lax.fori_loop(
            0, NXL, pair_sums, tuple(jnp.zeros((YE, L), jnp.float32) for _ in range(8))
        )
        for s2 in range(8):
            prod_ref[pl.ds(s1 * 8 + s2, 1), :] = jnp.sum(acc[s2], axis=0, keepdims=True)

    nbz = L // CB
    node = lax.broadcasted_iota(jnp.int32, (nbz, L), 0)
    block = lax.broadcasted_iota(jnp.int32, (nbz, L), 1) >> 4
    same_node = jnp.where(block == node, 1.0, 0.0)
    node_above = jnp.where(block + 1 == node, 1.0, 0.0)
    along_lanes = (((1,), (1,)), ((), ()))
    exact = lax.Precision.HIGHEST

    def class_terms(c):
        rows = pl.ds(16 * c, 16)
        pairs = prod_ref[rows, :]
        low = lax.dot_general(same_node, pairs, along_lanes, precision=exact,
                              preferred_element_type=jnp.float32)
        high = lax.dot_general(node_above, pairs, along_lanes, precision=exact,
                               preferred_element_type=jnp.float32)
        terms[c] = jnp.dot(low, placing[c, 0, rows, :], precision=exact,
                           preferred_element_type=jnp.float32) + jnp.dot(
            high, placing[c, 1, rows, :], precision=exact, preferred_element_type=jnp.float32)

    def coarse_copy(k, c, target_x, target_y):
        return pltpu.make_async_remote_copy(
            src_ref=terms.at[c],
            dst_ref=received.at[k],
            send_sem=coarse_send.at[k],
            recv_sem=coarse_recv.at[k],
            device_id=(target_x, target_y),
            device_id_type=mesh_id,
        )

    for s1 in range(2, 8):
        pair_rows(s1)
    for c in range(1, 4):
        class_terms(c)
    for k, (c, dx, dy) in enumerate(coarse_routes):
        @pl.when(has_device(gi + dx, gj + dy))
        def _():
            coarse_copy(k, c, gi + dx, gj + dy).start()

    for s1 in range(2):
        pair_rows(s1)
    class_terms(0)

    for k, (c, dx, dy) in enumerate(coarse_routes):
        @pl.when(has_device(gi + dx, gj + dy))
        def _():
            coarse_copy(k, c, gi + dx, gj + dy).wait_send()

        @pl.when(has_device(gi - dx, gj - dy))
        def _():
            coarse_copy(k, c, gi - dx, gj - dy).wait_recv()

    out_copy.wait()
    total = terms[0] + received[0] + received[1] + received[2]
    coarse_ref[...] = total[:, : coarse_ref.shape[1]]


def placing_matrix():
    table = np.zeros((4, 2, 64, 32), np.float32)
    for first_slot in range(8):
        for second_slot in range(8):
            one_x, one_y, one_z = corner_of(first_slot)
            two_x, two_y, two_z = corner_of(second_slot)
            offset_index = 9 * (two_x - one_x + 1) + 3 * (two_y - one_y + 1) + (two_z - one_z + 1)
            table[one_x * 2 + one_y, one_z, first_slot * 8 + second_slot, offset_index] = 1.0
    return table


def shards(initial_basis, labels, class_perm, support):
    size_x, size_y, size_z = labels.shape
    assert size_x == CB and size_y == CB and size_z % CB == 0
    blocks_z = size_z // CB
    nx = lax.axis_size("gx")
    ny = lax.axis_size("gy")
    XE = size_x + 2 * HX
    YE = -(-(size_y + 2 * HY) // 8) * 8
    f32 = jnp.float32
    vmem = pl.BlockSpec(memory_space=pltpu.VMEM)
    hbm = pl.BlockSpec(memory_space=pl.ANY)
    blocks_z = size_z // CB
    basis, coarse = pl.pallas_call(
        functools.partial(smooth_kernel, nx, ny),
        out_shape=(
            jax.ShapeDtypeStruct((8, size_x, size_y, size_z), f32),
            jax.ShapeDtypeStruct((blocks_z, 27), f32),
        ),
        in_specs=[hbm, hbm, pl.BlockSpec(memory_space=pltpu.SMEM), hbm, vmem],
        out_specs=(pl.BlockSpec(memory_space=pl.ANY), vmem),
        scratch_shapes=[
            pltpu.VMEM((8, XE, YE, size_z), f32),
            pltpu.VMEM((XE, YE, size_z), jnp.int32),
            pltpu.VMEM((XE, YE, size_z), jnp.int32),
            pltpu.VMEM((XE, YE, size_z), f32),
            pltpu.VMEM((12, XE, YE, size_z), f32),
            pltpu.VMEM((12, XE, YE, size_z), f32),
            pltpu.VMEM((2, XE, YE, size_z), f32),
            pltpu.VMEM((8, XE, YE, size_z), f32),
            pltpu.VMEM((8, XE, YE, size_z), f32),
            pltpu.VMEM((8, XE, YE, size_z), f32),
            pltpu.VMEM((8, XE, YE, size_z), f32),
            pltpu.VMEM((8, size_x, YE, size_z), f32),
            pltpu.VMEM((64, size_z), f32),
            pltpu.VMEM((4, blocks_z, 32), f32),
            pltpu.VMEM((3, blocks_z, 32), f32),
            pltpu.SemaphoreType.DMA((32,)),
            pltpu.SemaphoreType.DMA((32,)),
            pltpu.SemaphoreType.DMA((4,)),
            pltpu.SemaphoreType.DMA((3,)),
            pltpu.SemaphoreType.DMA((3,)),
            pltpu.SemaphoreType.DMA((8,)),
            pltpu.SemaphoreType.DMA((8,)),
        ],
        compiler_params=pltpu.CompilerParams(collective_id=1, has_side_effects=True),
    )(initial_basis, labels, class_perm, support, jnp.asarray(placing_matrix()))
    return (basis, coarse.T.reshape(27, 1, 1, blocks_z))


def solution(mesh):
    return jax.shard_map(
        shards,
        mesh=mesh,
        in_specs=(P(None, "gx", "gy", None), P("gx", "gy", None), P(), P("gx", "gy", None)),
        out_specs=(P(None, "gx", "gy", None), P(None, "gx", "gy", None)),
        check_vma=False,
    )
```

```python
import functools
import numpy as np
import jax
import jax.numpy as jnp
from jax import lax
from jax.experimental import pallas as pl
from jax.experimental.pallas import tpu as pltpu
from jax.sharding import PartitionSpec as P

CB = 16
ITERS = 3
HX = ITERS
HY = ITERS

omega_jacobi = 2.0 / 3.0
renorm_floor = 0.5


def with_halo(block, sides, width):
    for axis, dim in sides:
        count = lax.axis_size(axis)
        forward = [(i, i + 1) for i in range(count - 1)]
        backward = [(target, source) for source, target in forward]
        low = lax.ppermute(
            lax.slice_in_dim(block, block.shape[dim] - width, None, axis=dim), axis, forward
        )
        high = lax.ppermute(lax.slice_in_dim(block, 0, width, axis=dim), axis, backward)
        block = jnp.concatenate([low, block, high], axis=dim)
    return block


def from_behind(shard, axis, by):
    peers = lax.axis_size(axis)
    pairs = [(i, i + by) for i in range(peers) if 0 <= i + by < peers]
    return lax.ppermute(shard, axis, pairs)


def corner_of(slot_index):
    return (slot_index >> 2 & 1, slot_index >> 1 & 1, slot_index & 1)


def conductance(centre, neighbour):
    total_perm = centre + neighbour
    divisor = jnp.where(total_perm > 0.0, total_perm, 1.0)
    return 2.0 * centre * neighbour / divisor


def class_lookup(labels, class_perm):
    classes = jnp.arange(class_perm.shape[0])
    hits = labels[None] == classes[:, None, None, None]
    return jnp.sum(jnp.where(hits, class_perm[:, None, None, None], 0.0), axis=0)


def existing_bits(count_x, count_y, count_z, first_x, first_y, limit_x, limit_y, limit_z):
    block_x = (jnp.arange(count_x) + first_x) // CB
    block_y = (jnp.arange(count_y) + first_y) // CB
    block_z = jnp.arange(count_z) // CB
    bits = jnp.zeros((count_x, count_y, count_z), jnp.int32)
    for slot_index in range(8):
        corner_x, corner_y, corner_z = corner_of(slot_index)
        inside = (
            (block_x + corner_x < limit_x)[:, None, None]
            & (block_y + corner_y < limit_y)[None, :, None]
            & (block_z + corner_z < limit_z)[None, None, :]
        )
        bits = bits | jnp.where(inside, 1 << slot_index, 0)
    return bits


def halo_window(ref, xs, ys, slots=None):
    if len(ref.shape) == 4:
        return ref.at[slots if slots is not None else slice(None), xs, ys, :]
    return ref.at[xs, ys, :]


def halo_range(d, count, halo):
    if d > 0:
        return pl.ds(count - halo, halo), pl.ds(0, halo)
    if d < 0:
        return pl.ds(0, halo), pl.ds(halo + count, halo)
    return pl.ds(0, count), pl.ds(halo, count)


def halo_rows(d, count, halo, total):
    if d > 0:
        return pl.ds(count - halo, halo), pl.ds(total - halo, halo)
    if d < 0:
        return pl.ds(0, halo), pl.ds(count, halo)
    return pl.ds(0, count), pl.ds(0, count)


def slot_runs(slots):
    runs = []
    for s in sorted(slots):
        if runs and runs[-1][1] == s:
            runs[-1][1] = s + 1
        else:
            runs.append([s, s + 1])
    return [pl.ds(lo, hi - lo) for lo, hi in runs]


def shared_slots(dx, dy):
    keep = []
    for s in range(8):
        bx, by, _ = corner_of(s)
        if (dx > 0 and not bx) or (dx < 0 and bx) or (dy > 0 and not by) or (dy < 0 and by):
            continue
        keep.append(s)
    return keep


def smooth_kernel(
    nx, ny,
    basis_in, labels_in, class_perm, support_in, placing, basis_ref, coarse_ref,
    eb, el, es, pm, tt, ts, aux, valid, wa, wb, wc, img, prod_ref, terms, received,
    send_sem, recv_sem, local_sem, coarse_send, coarse_recv, edge_send, edge_recv,
):
    gi = lax.axis_index("gx")
    gj = lax.axis_index("gy")
    _, XE, YE, L = eb.shape
    NXL = basis_ref.shape[1]
    NYL = basis_ref.shape[2]
    mesh_id = pl.DeviceIdType.MESH
    sources = (basis_in, labels_in, support_in)
    targets = (eb, el, es)
    local_copies = []
    for a in range(3):
        local_copy = pltpu.make_async_copy(
            sources[a], halo_window(targets[a], pl.ds(HX, NXL), pl.ds(0, NYL)), local_sem.at[a]
        )
        local_copy.start()
        local_copies.append(local_copy)

    directions = [(dx, dy) for dx in (-1, 0, 1) for dy in (-1, 0, 1) if (dx, dy) != (0, 0)]

    def has_device(x, y):
        return (x >= 0) & (x < nx) & (y >= 0) & (y < ny)

    barrier = pltpu.get_barrier_semaphore()
    for dx, dy in directions:
        @pl.when(has_device(gi + dx, gj + dy))
        def _():
            pl.semaphore_signal(barrier, 1, device_id=(gi + dx, gj + dy), device_id_type=mesh_id)

    def pieces(dx, dy):
        return [(0, run) for run in slot_runs(shared_slots(dx, dy))] + [(1, None), (2, None)]

    def edge_pieces(dx, dy):
        from_x = {1: pl.ds(HX + NXL - 1, 1), -1: pl.ds(HX, 1), 0: pl.ds(HX, NXL)}[dx]
        to_x = {1: pl.ds(HX - 1, 1), -1: pl.ds(HX + NXL, 1), 0: pl.ds(HX, NXL)}[dx]
        from_y = {1: pl.ds(NYL - 1, 1), -1: pl.ds(0, 1), 0: pl.ds(0, NYL)}[dy]
        to_y = {1: pl.ds(YE - 1, 1), -1: pl.ds(NYL, 1), 0: pl.ds(0, NYL)}[dy]
        return [(run, from_x, to_x, from_y, to_y) for run in slot_runs(shared_slots(dx, dy))]

    faces = ((1, 0), (-1, 0), (0, 1), (0, -1))
    peers = jnp.int32(0)
    for dx, dy in directions:
        _, to_x = halo_range(dx, NXL, HX)
        _, to_y = halo_rows(dy, NYL, HY, YE)
        from_here = has_device(gi - dx, gj - dy)
        peers = peers + from_here.astype(jnp.int32)
        unshared = [s for s in range(8) if s not in shared_slots(dx, dy)]
        for run in slot_runs(unshared):
            window = halo_window(eb, to_x, to_y, run)
            window[...] = jnp.zeros(window.shape, window.dtype)

        @pl.when(jnp.logical_not(from_here))
        def _():
            for a in range(3):
                window = halo_window(targets[a], to_x, to_y)
                window[...] = jnp.zeros(window.shape, window.dtype)

    if NYL + HY < YE - HY:
        junction = pl.ds(NYL + HY, YE - 2 * HY - NYL)
        for a in range(3):
            window = halo_window(targets[a], pl.ds(0, XE), junction)
            window[...] = jnp.zeros(window.shape, window.dtype)
    window = wc.at[:, pl.ds(HX, NXL), pl.ds(NYL, YE - NYL), :]
    window[...] = jnp.zeros(window.shape, window.dtype)
    for dx, dy in faces:
        @pl.when(jnp.logical_not(has_device(gi - dx, gj - dy)))
        def _():
            for run, _, to_x, _, to_y in edge_pieces(dx, dy):
                window = wc.at[run, to_x, to_y, :]
                window[...] = jnp.zeros(window.shape, window.dtype)

    coarse_routes = ((2, 1, 0), (1, 0, 1), (3, 1, 1))
    for k, (_, dx, dy) in enumerate(coarse_routes):
        @pl.when(jnp.logical_not(has_device(gi - dx, gj - dy)))
        def _():
            received[k] = jnp.zeros(received.shape[1:], received.dtype)

    pl.semaphore_wait(barrier, peers)

    def remote_copy(k, p, dx, dy, target_x, target_y):
        from_x, to_x = halo_range(dx, NXL, HX)
        from_y, to_y = halo_rows(dy, NYL, HY, YE)
        a, run = pieces(dx, dy)[p]
        return pltpu.make_async_remote_copy(
            src_ref=halo_window(sources[a], from_x, from_y, run),
            dst_ref=halo_window(targets[a], to_x, to_y, run),
            send_sem=send_sem.at[4 * k + p],
            recv_sem=recv_sem.at[4 * k + p],
            device_id=(target_x, target_y),
            device_id_type=mesh_id,
        )

    for k, (dx, dy) in enumerate(directions):
        @pl.when(has_device(gi + dx, gj + dy))
        def _():
            for p in range(len(pieces(dx, dy))):
                remote_copy(k, p, dx, dy, gi + dx, gj + dy).start()

    def wait_halo(chosen):
        for k, (dx, dy) in enumerate(directions):
            if not chosen(dx, dy):
                continue

            @pl.when(has_device(gi + dx, gj + dy))
            def _():
                for p in range(len(pieces(dx, dy))):
                    remote_copy(k, p, dx, dy, gi + dx, gj + dy).wait_send()

            @pl.when(has_device(gi - dx, gj - dy))
            def _():
                for p in range(len(pieces(dx, dy))):
                    remote_copy(k, p, dx, dy, gi - dx, gj - dy).wait_recv()

    row = lax.broadcasted_iota(jnp.int32, (YE, L), 0)
    lane = lax.broadcasted_iota(jnp.int32, (YE, L), 1)
    m_yhi = (row == NYL - 1) | (row == YE - 1)
    m_ylo = (row == 0) | (row == NYL)
    rz = lane & (CB - 1)
    m_zhi = rz == CB - 1
    m_zlo = rz == 0
    m_rows = row < NYL
    block_y = gj + jnp.where(row < NYL, 0, jnp.where(row < YE - HY, 1, -1))
    global_y = jnp.where(row < YE - HY, gj * NYL + row, gj * NYL + row - YE)
    inside_y = (global_y >= 0) & (global_y < ny * NYL)
    node_y = block_y + 1 < ny
    node_z = (lane >> 4) + 1 < L // CB

    def lookup(x, carry):
        labels = el[x]
        perm = jnp.zeros((YE, L), jnp.float32)
        for c in range(class_perm.shape[0]):
            perm = jnp.where(labels == c, class_perm[c], perm)
        global_x = gi * NXL + x - HX
        inside = inside_y & (global_x >= 0) & (global_x < nx * NXL)
        pm[x] = jnp.where(inside, perm, 0.0)
        return carry

    for local_copy in local_copies:
        local_copy.wait()
    wait_halo(lambda dx, dy: dx == 0)
    lax.fori_loop(HX, HX + NXL, lookup, 0)

    def xplace(x):
        return (x + (CB - HX)) & (CB - 1)

    def pre(x, carry):
        pc = pm[x]
        pxp = jnp.where(x + 1 < XE, pm[jnp.minimum(x + 1, XE - 1)], 0.0)
        pxm = jnp.where(x >= 1, pm[jnp.maximum(x - 1, 0)], 0.0)
        pyp = pltpu.roll(pc, YE - 1, 0)
        pym = pltpu.roll(pc, 1, 0)
        pzp = pltpu.roll(pc, L - 1, 1)
        pzm = pltpu.roll(pc, 1, 1)
        t_xp = conductance(pc, pxp)
        t_xm = conductance(pc, pxm)
        t_yp = conductance(pc, pyp)
        t_ym = conductance(pc, pym)
        t_zp = jnp.where(lane == L - 1, 0.0, conductance(pc, pzp))
        t_zm = jnp.where(lane == 0, 0.0, conductance(pc, pzm))
        diag = t_xp + t_xm + t_yp + t_ym + t_zp + t_zm
        inv = 1.0 / jnp.where(diag > 0.0, diag, 1.0)
        aux[0, x] = diag
        aux[1, x] = 1.0 - omega_jacobi * diag * inv
        scale = omega_jacobi * inv
        cx_hi = xplace(x) == CB - 1
        cx_lo = xplace(x) == 0
        faces_t = (
            t_xp, jnp.where(cx_hi, 0.0, t_xp), t_xm, jnp.where(cx_lo, 0.0, t_xm),
            t_yp, jnp.where(m_yhi, 0.0, t_yp), t_ym, jnp.where(m_ylo, 0.0, t_ym),
            t_zp, jnp.where(m_zhi, 0.0, t_zp), t_zm, jnp.where(m_zlo, 0.0, t_zm),
        )
        for f, t in enumerate(faces_t):
            tt[f, x] = t
            ts[f, x] = t * scale
        return carry

    def pre_w(x, carry):
        sup = es[x]
        node_x = gi + ((x + (CB - HX)) >> 4) < nx
        for s in range(8):
            bx, by, bz = corner_of(s)
            keep = ((sup >> s) & 1) > 0
            if bx:
                keep = keep & node_x
            if by:
                keep = keep & node_y
            if bz:
                keep = keep & node_z
            v = jnp.where(keep, 1.0, 0.0)
            valid[s, x] = v
            wa[s, x] = eb[s, x] * v
        return carry

    lax.fori_loop(HX, HX + NXL, pre_w, 0)
    lax.fori_loop(HX + 1, HX + NXL - 1, pre, 0)

    def inflow_of(src, x, s, c, tt=tt):
        bx, by, bz = corner_of(s)
        cx_hi = xplace(x) == CB - 1
        cx_lo = xplace(x) == 0
        if bx:
            xp = src[jnp.where(cx_hi, s ^ 4, s), x + 1]
            t1 = tt[0, x]
            xm = src[s, x - 1]
            t2 = tt[3, x]
        else:
            xp = src[s, x + 1]
            t1 = tt[1, x]
            xm = src[jnp.where(cx_lo, s ^ 4, s), x - 1]
            t2 = tt[2, x]
        if by:
            yp = pltpu.roll(jnp.where(m_ylo, src[s ^ 2, x], c), YE - 1, 0)
            t3 = tt[4, x]
            ym = pltpu.roll(c, 1, 0)
            t4 = tt[7, x]
        else:
            yp = pltpu.roll(c, YE - 1, 0)
            t3 = tt[5, x]
            ym = pltpu.roll(jnp.where(m_yhi, src[s ^ 2, x], c), 1, 0)
            t4 = tt[6, x]
        if bz:
            zp = pltpu.roll(jnp.where(m_zlo, src[s ^ 1, x], c), L - 1, 1)
            t5 = tt[8, x]
            zm = pltpu.roll(c, 1, 1)
            t6 = tt[11, x]
        else:
            zp = pltpu.roll(c, L - 1, 1)
            t5 = tt[9, x]
            zm = pltpu.roll(jnp.where(m_zhi, src[s ^ 1, x], c), 1, 1)
            t6 = tt[10, x]
        return t1 * xp + t2 * xm + t3 * yp + t4 * ym + t5 * zp + t6 * zm

    def sweep(src, dst, lo, hi):
        def body(x, carry):
            keep = aux[1, x]
            for s in range(8):
                c = src[s, x]
                inflow = inflow_of(src, x, s, c, ts)
                dst[s, x] = (c * keep + inflow) * valid[s, x]
            return carry

        lax.fori_loop(lo, hi, body, 0)

    bufs = (wa, wb)
    for step in range(ITERS):
        sweep(bufs[step % 2], bufs[(step + 1) % 2], HX + step + 1, HX + NXL - step - 1)
    wait_halo(lambda dx, dy: dx != 0)
    lax.fori_loop(0, HX, lookup, 0)
    lax.fori_loop(HX + NXL, XE, lookup, 0)
    lax.fori_loop(0, HX, pre_w, 0)
    lax.fori_loop(HX + NXL, XE, pre_w, 0)
    lax.fori_loop(0, HX + 1, pre, 0)
    lax.fori_loop(HX + NXL - 1, XE, pre, 0)
    for step in range(ITERS):
        sweep(bufs[step % 2], bufs[(step + 1) % 2], step + 1, HX + step + 1)
        sweep(bufs[step % 2], bufs[(step + 1) % 2], HX + NXL - step - 1, XE - step - 1)
    last = bufs[ITERS % 2]
    basis_buf = wc

    def normalize(x, carry):
        vals = [last[s, x] for s in range(8)]
        total = vals[0]
        for s in range(1, 8):
            total = total + vals[s]
        scale = jnp.maximum(total, renorm_floor)
        for s in range(8):
            basis_buf[s, x, pl.ds(0, NYL), :] = (vals[s] / scale)[:NYL, :]
        return carry

    lax.fori_loop(HX, HX + 1, normalize, 0)
    lax.fori_loop(HX + NXL - 1, HX + NXL, normalize, 0)

    def edge_copy(k, p, dx, dy, target_x, target_y):
        run, from_x, to_x, from_y, to_y = edge_pieces(dx, dy)[p]
        return pltpu.make_async_remote_copy(
            src_ref=wc.at[run, from_x, from_y, :],
            dst_ref=wc.at[run, to_x, to_y, :],
            send_sem=edge_send.at[2 * k + p],
            recv_sem=edge_recv.at[2 * k + p],
            device_id=(target_x, target_y),
            device_id_type=mesh_id,
        )

    for k, (dx, dy) in enumerate(faces):
        if dy != 0:
            continue

        @pl.when(has_device(gi + dx, gj + dy))
        def _():
            for p in range(len(edge_pieces(dx, dy))):
                edge_copy(k, p, dx, dy, gi + dx, gj + dy).start()
    lax.fori_loop(HX + 1, HX + NXL - 1, normalize, 0)
    out_copy = pltpu.make_async_copy(
        wc.at[:, pl.ds(HX, NXL), pl.ds(0, NYL), :], basis_ref, local_sem.at[3]
    )
    out_copy.start()
    for k, (dx, dy) in enumerate(faces):
        if dx != 0:
            continue

        @pl.when(has_device(gi + dx, gj + dy))
        def _():
            for p in range(len(edge_pieces(dx, dy))):
                edge_copy(k, p, dx, dy, gi + dx, gj + dy).start()

    for k, (dx, dy) in enumerate(faces):
        @pl.when(has_device(gi + dx, gj + dy))
        def _():
            for p in range(len(edge_pieces(dx, dy))):
                edge_copy(k, p, dx, dy, gi + dx, gj + dy).wait_send()

        @pl.when(has_device(gi - dx, gj - dy))
        def _():
            for p in range(len(edge_pieces(dx, dy))):
                edge_copy(k, p, dx, dy, gi - dx, gj - dy).wait_recv()

    def image(x, carry):
        diag = aux[0, x]
        for s in range(8):
            c = basis_buf[s, x]
            inflow = inflow_of(basis_buf, x, s, c)
            img[s, x - HX] = jnp.where(m_rows, diag * c - inflow, 0.0)
        return carry

    lax.fori_loop(HX, HX + NXL, image, 0)

    def pair_rows(s1):
        def pair_sums(x, acc):
            b = basis_buf[s1, x + HX]
            return tuple(acc[s2] + b * img[s2, x] for s2 in range(8))

        acc = lax.fori_loop(
            0, NXL, pair_sums, tuple(jnp.zeros((YE, L), jnp.float32) for _ in range(8))
        )
        for s2 in range(8):
            prod_ref[pl.ds(s1 * 8 + s2, 1), :] = jnp.sum(acc[s2], axis=0, keepdims=True)

    nbz = L // CB
    node = lax.broadcasted_iota(jnp.int32, (nbz, L), 0)
    block = lax.broadcasted_iota(jnp.int32, (nbz, L), 1) >> 4
    same_node = jnp.where(block == node, 1.0, 0.0)
    node_above = jnp.where(block + 1 == node, 1.0, 0.0)
    along_lanes = (((1,), (1,)), ((), ()))
    exact = lax.Precision.HIGHEST

    def class_terms(c):
        rows = pl.ds(16 * c, 16)
        pairs = prod_ref[rows, :]
        low = lax.dot_general(same_node, pairs, along_lanes, precision=exact,
                              preferred_element_type=jnp.float32)
        high = lax.dot_general(node_above, pairs, along_lanes, precision=exact,
                               preferred_element_type=jnp.float32)
        terms[c] = jnp.dot(low, placing[c, 0, rows, :], precision=exact,
                           preferred_element_type=jnp.float32) + jnp.dot(
            high, placing[c, 1, rows, :], precision=exact, preferred_element_type=jnp.float32)

    def coarse_copy(k, c, target_x, target_y):
        return pltpu.make_async_remote_copy(
            src_ref=terms.at[c],
            dst_ref=received.at[k],
            send_sem=coarse_send.at[k],
            recv_sem=coarse_recv.at[k],
            device_id=(target_x, target_y),
            device_id_type=mesh_id,
        )

    for s1 in range(2, 8):
        pair_rows(s1)
    for c in range(1, 4):
        class_terms(c)
    for k, (c, dx, dy) in enumerate(coarse_routes):
        @pl.when(has_device(gi + dx, gj + dy))
        def _():
            coarse_copy(k, c, gi + dx, gj + dy).start()

    for s1 in range(2):
        pair_rows(s1)
    class_terms(0)

    for k, (c, dx, dy) in enumerate(coarse_routes):
        @pl.when(has_device(gi + dx, gj + dy))
        def _():
            coarse_copy(k, c, gi + dx, gj + dy).wait_send()

        @pl.when(has_device(gi - dx, gj - dy))
        def _():
            coarse_copy(k, c, gi - dx, gj - dy).wait_recv()

    out_copy.wait()
    total = terms[0] + received[0] + received[1] + received[2]
    coarse_ref[...] = total[:, : coarse_ref.shape[1]]


def placing_matrix():
    table = np.zeros((4, 2, 64, 32), np.float32)
    for first_slot in range(8):
        for second_slot in range(8):
            one_x, one_y, one_z = corner_of(first_slot)
            two_x, two_y, two_z = corner_of(second_slot)
            offset_index = 9 * (two_x - one_x + 1) + 3 * (two_y - one_y + 1) + (two_z - one_z + 1)
            table[one_x * 2 + one_y, one_z, first_slot * 8 + second_slot, offset_index] = 1.0
    return table


def shards(initial_basis, labels, class_perm, support):
    size_x, size_y, size_z = labels.shape
    assert size_x == CB and size_y == CB and size_z % CB == 0
    blocks_z = size_z // CB
    nx = lax.axis_size("gx")
    ny = lax.axis_size("gy")
    XE = size_x + 2 * HX
    YE = -(-(size_y + 2 * HY) // 8) * 8
    f32 = jnp.float32
    vmem = pl.BlockSpec(memory_space=pltpu.VMEM)
    hbm = pl.BlockSpec(memory_space=pl.ANY)
    blocks_z = size_z // CB
    basis, coarse = pl.pallas_call(
        functools.partial(smooth_kernel, nx, ny),
        out_shape=(
            jax.ShapeDtypeStruct((8, size_x, size_y, size_z), f32),
            jax.ShapeDtypeStruct((blocks_z, 27), f32),
        ),
        in_specs=[hbm, hbm, pl.BlockSpec(memory_space=pltpu.SMEM), hbm, vmem],
        out_specs=(pl.BlockSpec(memory_space=pl.ANY), vmem),
        scratch_shapes=[
            pltpu.VMEM((8, XE, YE, size_z), f32),
            pltpu.VMEM((XE, YE, size_z), jnp.int32),
            pltpu.VMEM((XE, YE, size_z), jnp.int32),
            pltpu.VMEM((XE, YE, size_z), f32),
            pltpu.VMEM((12, XE, YE, size_z), f32),
            pltpu.VMEM((12, XE, YE, size_z), f32),
            pltpu.VMEM((2, XE, YE, size_z), f32),
            pltpu.VMEM((8, XE, YE, size_z), f32),
            pltpu.VMEM((8, XE, YE, size_z), f32),
            pltpu.VMEM((8, XE, YE, size_z), f32),
            pltpu.VMEM((8, XE, YE, size_z), f32),
            pltpu.VMEM((8, size_x, YE, size_z), f32),
            pltpu.VMEM((64, size_z), f32),
            pltpu.VMEM((4, blocks_z, 32), f32),
            pltpu.VMEM((3, blocks_z, 32), f32),
            pltpu.SemaphoreType.DMA((32,)),
            pltpu.SemaphoreType.DMA((32,)),
            pltpu.SemaphoreType.DMA((4,)),
            pltpu.SemaphoreType.DMA((3,)),
            pltpu.SemaphoreType.DMA((3,)),
            pltpu.SemaphoreType.DMA((8,)),
            pltpu.SemaphoreType.DMA((8,)),
        ],
        compiler_params=pltpu.CompilerParams(collective_id=1, has_side_effects=True),
    )(initial_basis, labels, class_perm, support, jnp.asarray(placing_matrix()))
    return (basis, coarse.T.reshape(27, 1, 1, blocks_z))


def solution(mesh):
    return jax.shard_map(
        shards,
        mesh=mesh,
        in_specs=(P(None, "gx", "gy", None), P("gx", "gy", None), P(), P("gx", "gy", None)),
        out_specs=(P(None, "gx", "gy", None), P(None, "gx", "gy", None)),
        check_vma=False,
    )
```
